32 devices in a mesh: dp: 4 (over z), seq: 4 (over y, x), mp: 2 (over core).
Axes of the slice: x: 2, y: 2, z: 4, core: 2. Of those that a mesh axis runs over, the one named last changes fastest.
Arguments:
- tokens: bfloat16 [4, 1024, 896], P('dp', 'seq')
- neighbours: bfloat16 [4, 16, 2, 128, 896], P('dp', 'seq'), may hold values from -6 to 6
- neighbour_lengths: int32 [4, 16, 2], P('dp', 'seq'), may hold values from 1 to 128, as said below
- segment_ids: int32 [4, 1024], P('dp', 'seq'), may hold values from 0 to 7, never falling along the last dimension, each value on 1 to 512 neighbouring positions
- out_grad: bfloat16 [4, 1024, 896], P('dp', 'seq'), may hold values from -6 to 6
- self_weights: float32 [4, 896, 1024], P(None, ('dp', 'seq'), 'mp')
- cross_weights: float32 [4, 896, 1024], P(None, ('dp', 'seq'), 'mp')
- feed_weights: float32 [2, 896, 3584], P(None, ('dp', 'seq'), 'mp')
- norm_gains: float32 [3, 896], P(None, ('dp', 'seq'))
- self_first: float32 [4, 896, 1024], P(None, ('dp', 'seq'), 'mp'), may hold values from -0.0004272461 to 0.0004272461
- cross_first: float32 [4, 896, 1024], P(None, ('dp', 'seq'), 'mp'), may hold values from -0.0004272461 to 0.0004272461
- feed_first: float32 [2, 896, 3584], P(None, ('dp', 'seq'), 'mp'), may hold values from -0.0004272461 to 0.0004272461
- gains_first: float32 [3, 896], P(None, ('dp', 'seq')), may hold values from -0.0012207031 to 0.0012207031
- self_second: float32 [4, 896, 1024], P(None, ('dp', 'seq'), 'mp'), may hold values from 2.1794013e-09 to 2.9058684e-08
- cross_second: float32 [4, 896, 1024], P(None, ('dp', 'seq'), 'mp'), may hold values from 2.1794013e-09 to 2.9058684e-08
- feed_second: float32 [2, 896, 3584], P(None, ('dp', 'seq'), 'mp'), may hold values from 2.1794013e-09 to 2.9058684e-08
- gains_second: float32 [3, 896], P(None, ('dp', 'seq')), may hold values from 1.9614612e-08 to 2.6152816e-07
Outputs:
- out: bfloat16 [4, 1024, 896], P('dp', 'seq')
- in_grad: float32 [4, 1024, 896], P('dp', 'seq')
- grad_norm: float32 [], replicated
- self_new: float32 [4, 896, 1024], P(None, ('dp', 'seq'), 'mp')
- cross_new: float32 [4, 896, 1024], P(None, ('dp', 'seq'), 'mp')
- feed_new: float32 [2, 896, 3584], P(None, ('dp', 'seq'), 'mp')
- gains_new: float32 [3, 896], P(None, ('dp', 'seq'))
- self_first_new: float32 [4, 896, 1024], P(None, ('dp', 'seq'), 'mp')
- cross_first_new: float32 [4, 896, 1024], P(None, ('dp', 'seq'), 'mp')
- feed_first_new: float32 [2, 896, 3584], P(None, ('dp', 'seq'), 'mp')
- gains_first_new: float32 [3, 896], P(None, ('dp', 'seq'))
- self_second_new: float32 [4, 896, 1024], P(None, ('dp', 'seq'), 'mp')
- cross_second_new: float32 [4, 896, 1024], P(None, ('dp', 'seq'), 'mp')
- feed_second_new: float32 [2, 896, 3584], P(None, ('dp', 'seq'), 'mp')
- gains_second_new: float32 [3, 896], P(None, ('dp', 'seq'))
The draws below stay inside these ranges and needn't reach their ends.
Inputs may be any that keep to these rules, and one draw needn't show every extreme that they name: `segment_ids`: segment ids never fall along a row; each of the 8 documents of a row has 1 to 512 tokens. `neighbour_lengths`: the valid tokens of a neighbour are its first ones; in every row, both neighbours of some retrieval block are full.
All inputs are finite; a program needn't handle non-finite values.
Results may differ from the reference program's by a relative error of at most 0.018.
Values may be sent and summed in bfloat16 or wider, within the bound.
No kernel may reach another device: no remote copies, remote signals or barrier semaphores. Data moves between devices by JAX's collectives and lax.ppermute only.
A program may use at most 192 MiB of HBM per device.

```python
import math
import jax
import jax.numpy as jnp
import numpy as np
from jax import lax

D = 896
HEADS = 16
HEAD_DIM = 64
FF = 3584
BLOCK = 64
NEIGHBOURS = 2
NEIGH_LEN = 128
ROW_LEN = 1024
DOCS = 8
STEP = 10
ROWS = 4
SEQ_DEV = 256
BLOCKS_ROW = 16
PARAMS = 13765248


def base_noise(key, shape):
    return jax.random.truncated_normal(key, -3.0, 3.0, shape, jnp.float32)


def draw_tokens(key, part):
    keys = jax.random.split(jax.random.fold_in(key, 3), 3)
    noise = base_noise(keys[0], (ROWS, ROW_LEN, D))
    row_scale = jnp.exp(jax.random.uniform(keys[1], (ROWS, ROW_LEN, 1), jnp.float32, math.log(0.3), math.log(3.0)))
    column_scale = jnp.exp(jax.random.uniform(keys[2], (1, 1, D), jnp.float32, math.log(0.35), math.log(3.5)))
    return (noise * row_scale * column_scale).astype(jnp.bfloat16)


def draw_neighbour_lengths(key, part):
    lengths = jax.random.randint(jax.random.fold_in(key, 11), (ROWS, BLOCKS_ROW, NEIGHBOURS), 1, NEIGH_LEN + 1)
    full_block = jax.random.randint(jax.random.fold_in(key, 12), (ROWS, 1, 1), 0, BLOCKS_ROW)
    block_ids = jnp.arange(BLOCKS_ROW, dtype=jnp.int32)[None, :, None]
    return jnp.where(block_ids == full_block, NEIGH_LEN, lengths).astype(jnp.int32)


def attention_stack(key):
    noise = base_noise(jax.random.fold_in(key, 21), (4, D, HEADS * HEAD_DIM))
    factors = jnp.array([1.0, 1.0, 1.0, 6.0], jnp.float32)[:, None, None] / math.sqrt(D)
    return noise * factors


def draw_self_weights(key, part):
    return attention_stack(key)


def draw_cross_weights(key, part):
    return attention_stack(jax.random.fold_in(key, 5))


def draw_feed_weights(key, part):
    noise = base_noise(jax.random.fold_in(key, 31), (2, D, FF))
    factors = jnp.array([1.0 / math.sqrt(D), 1.5 / math.sqrt(FF)], jnp.float32)[:, None, None]
    return noise * factors


def draw_norm_gains(key, part):
    position = jnp.arange(D, dtype=jnp.float32)[None, :] / D
    ramp = 0.6 * jnp.exp(math.log(2.5) * position)
    rough = jax.random.uniform(jax.random.fold_in(key, 42), (3, D), jnp.float32, 0.75, 1.35)
    return ramp * rough


def block_scale(rng, extent, pieces, least, largest):
    factor_of = 1.0
    for dim, blocks in pieces:
        heights = jax.random.uniform(jax.random.fold_in(jax.random.fold_in(rng, 6), dim), (blocks,), jnp.float32, least / len(pieces), largest / len(pieces))
        factor_of = factor_of * jnp.repeat(jnp.exp(heights), extent[dim] // blocks).reshape((-1,) + (1,) * (len(extent) - 1 - dim))
    return factor_of


def profile(count, total, bound, lean):
    portions = [(1 << 20) // math.isqrt(standing ** lean) + 1 for standing in range(2, count + 1)]
    rest, counts = total - bound - (count - 1), [1] * (count - 1)
    while rest > 0:
        candidates = [i for i in range(count - 1) if counts[i] < bound]
        pool, left = sum([portions[i] for i in candidates]), rest
        for i in candidates:
            more = min(bound - counts[i], max(1, left * portions[i] // pool), rest)
            counts[i] = counts[i] + more
            rest = rest - more
    return np.array([bound] + counts)


def ragged(rng, number_of, total, reach, slope):
    if number_of == 2:
        one = jax.random.randint(rng, (), max(1, total - reach), min(reach, total - 1) + 1)
        return jnp.stack([one, total - one])
    sizes = jnp.asarray(profile(number_of, total, reach, slope), jnp.int32)
    twos = (number_of - 1) // 2
    source_of, receiver = sizes[1:1 + 2 * twos:2], sizes[2:2 + 2 * twos:2]
    room = jnp.minimum(source_of - 1, reach - receiver)
    moved = jax.random.randint(jax.random.fold_in(rng, 1), (twos,), 0, 1 << 20) % (room + 1)
    sizes = sizes.at[1:1 + 2 * twos:2].set(source_of - moved).at[2:2 + 2 * twos:2].set(receiver + moved)
    return sizes[jax.random.permutation(jax.random.fold_in(rng, 2), number_of)]


def gaussian(stream_key, shape, spread, most, cuts=(), held_as=jnp.bfloat16):
    gain = block_scale(stream_key, shape, cuts, -0.22, 0.18) if cuts else 1.0
    entries = jax.random.normal(stream_key, shape, jnp.float32) * spread * gain
    return jnp.minimum(jnp.maximum(entries, -most), most).astype(held_as)


def setup_inputs(seed: int = 0) -> dict:
    splits = jax.random.split(jax.random.key(seed), 18)
    return {
        "tokens": draw_tokens(jax.random.fold_in(splits[17], 71), 0),
        "neighbours": gaussian(splits[1], (ROWS, BLOCKS_ROW, NEIGHBOURS, NEIGH_LEN, D), 1.0, 6.0, ((0, 4), (1, 4))),
        "neighbour_lengths": draw_neighbour_lengths(jax.random.fold_in(splits[17], 71), 0),
        "segment_ids": jax.vmap(lambda own: jnp.searchsorted(jnp.cumsum(ragged(own, DOCS, ROW_LEN, ROW_LEN // 2, 2)), jnp.arange(ROW_LEN), side="right"))(jax.random.split(splits[3], ROWS)).reshape((ROWS, ROW_LEN)).astype(jnp.int32),
        "out_grad": gaussian(splits[4], (ROWS, ROW_LEN, D), 1.0, 6.0, ((0, 4), (1, 4))),
        "self_weights": draw_self_weights(jax.random.fold_in(splits[17], 71), 0),
        "cross_weights": draw_cross_weights(jax.random.fold_in(splits[17], 71), 0),
        "feed_weights": draw_feed_weights(jax.random.fold_in(splits[17], 71), 0),
        "norm_gains": draw_norm_gains(jax.random.fold_in(splits[17], 71), 0),
        "self_first": gaussian(splits[9], (4, D, HEADS * HEAD_DIM), (0.11 / PARAMS ** 0.5), 0.0004272461, ((1, 16), (2, 2)), jnp.float32),
        "cross_first": gaussian(splits[10], (4, D, HEADS * HEAD_DIM), (0.11 / PARAMS ** 0.5), 0.0004272461, ((1, 16), (2, 2)), jnp.float32),
        "feed_first": gaussian(splits[11], (2, D, FF), (0.11 / PARAMS ** 0.5), 0.0004272461, ((1, 16), (2, 2)), jnp.float32),
        "gains_first": gaussian(splits[12], (3, D), (0.33 / PARAMS ** 0.5), 0.0012207031, ((1, 16),), jnp.float32),
        "self_second": jnp.clip(jnp.exp(math.log(2.9058684347660346e-08) - 2.5902672 * jax.random.uniform(splits[13], (4, D, HEADS * HEAD_DIM), jnp.float32) ** block_scale(splits[13], (4, D, HEADS * HEAD_DIM), ((1, 16), (2, 2)), -0.2, 0.2)), 2.179401326074526e-09, 2.9058684347660346e-08),
        "cross_second": jnp.clip(jnp.exp(math.log(2.9058684347660346e-08) - 2.5902672 * jax.random.uniform(splits[14], (4, D, HEADS * HEAD_DIM), jnp.float32) ** block_scale(splits[14], (4, D, HEADS * HEAD_DIM), ((1, 16), (2, 2)), -0.2, 0.2)), 2.179401326074526e-09, 2.9058684347660346e-08),
        "feed_second": jnp.clip(jnp.exp(math.log(2.9058684347660346e-08) - 2.5902672 * jax.random.uniform(splits[15], (2, D, FF), jnp.float32) ** block_scale(splits[15], (2, D, FF), ((1, 16), (2, 2)), -0.2, 0.2)), 2.179401326074526e-09, 2.9058684347660346e-08),
        "gains_second": jnp.clip(jnp.exp(math.log(2.615281573525863e-07) - 2.5902671 * jax.random.uniform(splits[16], (3, D), jnp.float32) ** block_scale(splits[16], (3, D), ((1, 16),), -0.2, 0.2)), 1.961461215671534e-08, 2.615281573525863e-07),
    }


@jax.custom_vjp
def low(v):
    return lax.optimization_barrier(v.astype(jnp.bfloat16)).astype(jnp.float32)

@jax.custom_vjp
def low_back(v):
    return v

def low_keep(v):
    return (low(v), None)

def low_pass(kept, grad):
    return (grad,)

def back_keep(v):
    return (v, None)

def back_low(kept, grad):
    return (low(grad),)
low.defvjp(low_keep, low_pass)
low_back.defvjp(back_keep, back_low)
norm_eps = 1e-05
rope_base = 10000.0
beta_one = 0.9
beta_two = 0.95
adam_eps = 1e-08
weight_decay = 0.1
learn_rate = 0.1
gain_rate = 0.5
clip_limit = 1.0
masked_fill = -1e+30

def dense(left, right):
    return jnp.dot(left, right, precision=lax.Precision.HIGHEST, preferred_element_type=jnp.float32)

def rms_apply(inputs, gain_row):
    factor = lax.rsqrt(lax.optimization_barrier(jnp.mean(inputs * inputs, axis=-1, keepdims=True)) + norm_eps)
    return inputs * factor * gain_row

def rope_apply(field_in, positions):
    half_dim = field_in.shape[-1] // 2
    frequency = rope_base ** (-jnp.arange(half_dim, dtype=jnp.float32) / half_dim)
    angles = positions[:, None] * frequency[None, :]
    cosine = jnp.cos(angles)[:, None, :]
    sine_part = jnp.sin(angles)[:, None, :]
    lead_half = field_in[..., :half_dim]
    tail_half = field_in[..., half_dim:]
    return jnp.concatenate([lead_half * cosine - tail_half * sine_part, lead_half * sine_part + tail_half * cosine], axis=-1)

def attend(queries, keys, values, allowed):
    scores = low_back(jnp.einsum('...qhd,...khd->...hqk', queries, keys, precision=lax.Precision.HIGHEST) * HEAD_DIM ** (-0.5))
    row_max = lax.optimization_barrier(jnp.max(jnp.where(allowed, scores, masked_fill), axis=-1, keepdims=True))
    row_total = lax.optimization_barrier(jnp.sum(jnp.where(allowed, jnp.exp(scores - row_max), 0.0), axis=-1, keepdims=True))
    log_total = row_max + jnp.log(row_total)
    prob_full = jnp.where(allowed, jnp.exp(scores - log_total), 0.0)
    return jnp.einsum('...hqk,...khd->...qhd', low(prob_full), values, precision=lax.Precision.HIGHEST)

def self_attention(queries, keys, values, seg_row):
    block_rows = SEQ_DEV
    block_count = ROW_LEN // block_rows
    key_pos = jnp.arange(ROW_LEN, dtype=jnp.int32)

    def one_block(pair):
        query_block, start_row = pair
        query_pos = start_row + jnp.arange(block_rows, dtype=jnp.int32)
        query_seg = lax.dynamic_slice_in_dim(seg_row, start_row.astype(jnp.int32), block_rows)
        allowed = jnp.logical_and(key_pos[None, :] <= query_pos[:, None], seg_row[None, :] == query_seg[:, None])
        return attend(query_block, keys, values, allowed[None])
    starts = (jnp.arange(block_count, dtype=jnp.int32) * block_rows).astype(jnp.int32)
    blocks_out = lax.map(jax.checkpoint(one_block), (queries.reshape(block_count, block_rows, HEADS, HEAD_DIM), starts))
    return blocks_out.reshape(ROW_LEN, HEADS * HEAD_DIM)

def cross_attention(queries, keys, values, lengths, seg_row):
    shifted = jnp.concatenate([queries[BLOCK - 1:], jnp.zeros((BLOCK - 1, HEADS, HEAD_DIM), jnp.float32)], axis=0)
    blocks_in = shifted.reshape(BLOCKS_ROW, BLOCK, HEADS, HEAD_DIM)
    key_valid = (jnp.arange(NEIGH_LEN, dtype=jnp.int32)[None, None, :] < lengths[:, :, None]).reshape(BLOCKS_ROW, NEIGHBOURS * NEIGH_LEN)
    blocks_out = attend(blocks_in, keys, values, key_valid[:, None, None, :])
    seg_shift = jnp.concatenate([seg_row[BLOCK - 1:], jnp.zeros((BLOCK - 1,), jnp.int32)], axis=0).reshape(BLOCKS_ROW, BLOCK)
    keep_rows = (seg_shift == seg_shift[:, :1]).astype(jnp.float32).reshape(ROW_LEN, 1)
    attended = blocks_out.reshape(ROW_LEN, HEADS * HEAD_DIM) * keep_rows
    return jnp.concatenate([jnp.zeros((BLOCK - 1, HEADS * HEAD_DIM), jnp.float32), attended[:ROW_LEN - BLOCK + 1]], axis=0)

def row_forward(params, inputs, neigh_rows, lengths, seg_row):
    self_low = low(params[0])
    cross_low = low(params[1])
    feed_low = low(params[2])
    gain_low = low(params[3])
    positions = jnp.arange(ROW_LEN, dtype=jnp.int32).astype(jnp.float32)
    head_shape = (ROW_LEN, HEADS, HEAD_DIM)
    normed_one = low(rms_apply(inputs, gain_low[0]))
    query_self = low(rope_apply(low_back(dense(normed_one, self_low[0])).reshape(head_shape), positions))
    key_self = low(rope_apply(low_back(dense(normed_one, self_low[1])).reshape(head_shape), positions))
    value_self = low(low_back(dense(normed_one, self_low[2]))).reshape(head_shape)
    attn_out = low(low_back(self_attention(query_self, key_self, value_self, seg_row)))
    hidden_one = inputs + low_back(dense(attn_out, self_low[3].T))
    normed_two = low(rms_apply(hidden_one, gain_low[1]))
    query_cross = low(low_back(dense(normed_two, cross_low[0]))).reshape(head_shape)
    neigh_flat = neigh_rows.reshape(-1, D)
    key_shape = (BLOCKS_ROW, NEIGHBOURS * NEIGH_LEN, HEADS, HEAD_DIM)
    key_cross = low(low_back(dense(neigh_flat, cross_low[1]))).reshape(key_shape)
    value_cross = low(low_back(dense(neigh_flat, cross_low[2]))).reshape(key_shape)
    cross_out = low(low_back(cross_attention(query_cross, key_cross, value_cross, lengths, seg_row)))
    hidden_two = hidden_one + low_back(dense(cross_out, cross_low[3].T))
    normed_three = low(rms_apply(hidden_two, gain_low[2]))
    upward = low_back(dense(normed_three, feed_low[0]))
    active = low(jax.nn.gelu(upward, approximate=True))
    return hidden_two + low_back(dense(active, feed_low[1].T))

def adam_step(weight, gradient, first_old, second_old, factor, step_rate, decay_coef):
    clipped = gradient * factor
    first_new = beta_one * first_old + (1.0 - beta_one) * clipped
    second_new = beta_two * second_old + (1.0 - beta_two) * clipped * clipped
    first_hat = first_new / (1.0 - beta_one ** STEP)
    second_hat = second_new / (1.0 - beta_two ** STEP)
    weight_new = weight - step_rate * (first_hat / (jnp.sqrt(second_hat) + adam_eps) + decay_coef * weight)
    return (weight_new, first_new, second_new)

def reference(tokens, neighbours, neighbour_lengths, segment_ids, out_grad, self_weights, cross_weights, feed_weights, norm_gains, self_first, cross_first, feed_first, gains_first, self_second, cross_second, feed_second, gains_second):
    params = (self_weights, cross_weights, feed_weights, norm_gains)
    zero_grads = jax.tree.map(lambda array_in: jnp.zeros(array_in.shape, jnp.float32), params)

    def row_step(grad_total, row_data):
        row_tokens, row_neigh, row_lengths, row_seg, row_cot = row_data
        neigh_float = row_neigh.astype(jnp.float32)

        def forward(param_set, row_inputs):
            return row_forward(param_set, row_inputs, neigh_float, row_lengths, row_seg)
        result, pullback = jax.vjp(forward, params, row_tokens.astype(jnp.float32))
        param_grads, input_grad = pullback(row_cot.astype(jnp.float32))
        grad_total = jax.tree.map(jnp.add, grad_total, param_grads)
        return (grad_total, (result.astype(jnp.bfloat16), input_grad))
    grads, (out_rows, in_rows) = lax.scan(row_step, zero_grads, (tokens, neighbours, neighbour_lengths, segment_ids, out_grad))
    squares = jnp.sum(grads[0] * grads[0]) + jnp.sum(grads[1] * grads[1]) + jnp.sum(grads[2] * grads[2]) + jnp.sum(grads[3] * grads[3])
    grad_norm = jnp.sqrt(squares)
    factor = jnp.minimum(1.0, clip_limit / (grad_norm + 1e-06))
    self_new, self_first_new, self_second_new = adam_step(self_weights, grads[0], self_first, self_second, factor, learn_rate, weight_decay)
    cross_new, cross_first_new, cross_second_new = adam_step(cross_weights, grads[1], cross_first, cross_second, factor, learn_rate, weight_decay)
    feed_new, feed_first_new, feed_second_new = adam_step(feed_weights, grads[2], feed_first, feed_second, factor, learn_rate, weight_decay)
    gains_new, gains_first_new, gains_second_new = adam_step(norm_gains, grads[3], gains_first, gains_second, factor, gain_rate, 0.0)
    return (out_rows, in_rows, grad_norm, self_new, cross_new, feed_new, gains_new, self_first_new, cross_first_new, feed_first_new, gains_first_new, self_second_new, cross_second_new, feed_second_new, gains_second_new)
```

```python
from functools import partial

import jax
import jax.numpy as jnp
from jax import lax
from jax.sharding import PartitionSpec as P

HEAD_DIM = 64
BLOCK = 64
NEIGHBOURS = 2
NEIGH_LEN = 128
STEP = 10
DOC_MAX = 512

norm_eps = 1e-05
rope_base = 10000.0
beta_one = 0.9
beta_two = 0.95
adam_eps = 1e-08
weight_decay = 0.1
learn_rate = 0.1
gain_rate = 0.5
clip_limit = 1.0
masked_fill = -1e30

f32 = jnp.float32
bf16 = jnp.bfloat16


def to_low(array_in):
    return array_in.astype(bf16)


def shifted(value, axis, by):
    count = lax.axis_size(axis)
    return lax.ppermute(value, axis, [(i, i + by) for i in range(count) if 0 <= i + by < count])


def rotated(value, axis, by):
    count = lax.axis_size(axis)
    return lax.ppermute(value, axis, [(i, (i + by) % count) for i in range(count)])


def swapped(value, axis, by):
    count = lax.axis_size(axis)
    return lax.ppermute(value, axis, [(i, i ^ by) for i in range(count)])


def butterfly(value, axes):
    for axis in axes:
        step = 1
        while step < lax.axis_size(axis):
            value = value + swapped(value, axis, step)
            step *= 2
    return value


def core_sum(partial_out):
    return partial_out + swapped(partial_out, "mp", 1)


def small_mesh():
    return lax.axis_size("dp") == 4 and lax.axis_size("seq") == 4


def put(buffer, piece, starts):
    return lax.dynamic_update_slice(buffer, piece, starts)


def gather_rows(block):
    if not small_mesh():
        return lax.all_gather(block, ("dp", "seq"), axis=0, tiled=True)
    rows, cols = block.shape
    half = cols // 256 * 128
    z = lax.axis_index("dp")
    s = lax.axis_index("seq")
    pieces = [block] + [rotated(block, "dp", k) for k in (1, 2, 3)]
    column = jnp.zeros((4, rows, cols), block.dtype)
    for k, piece in enumerate(pieces):
        column = put(column, piece[None], ((z - k) % 4, 0, 0))
    from_x = swapped(column, "seq", 1)
    from_y = swapped(column, "seq", 2)
    diag_a = swapped(from_y[..., :half], "seq", 1)
    diag_b = swapped(from_x[..., half:], "seq", 2)
    out = jnp.zeros((4, 4, rows, cols), block.dtype)
    out = put(out, column[:, None], (0, s, 0, 0))
    out = put(out, from_x[:, None], (0, s ^ 1, 0, 0))
    out = put(out, from_y[:, None], (0, s ^ 2, 0, 0))
    out = put(out, diag_a[:, None], (0, s ^ 3, 0, 0))
    out = put(out, diag_b[:, None], (0, s ^ 3, 0, half))
    return out.reshape(16 * rows, cols)


def take(array_in, index, axis):
    return lax.dynamic_index_in_dim(array_in, index, axis, keepdims=False)


def scatter_rows(grads):
    low = to_low(grads)
    if not small_mesh():
        return lax.psum_scatter(low, ("dp", "seq"), scatter_dimension=0, tiled=True).astype(f32)
    rows, cols = low.shape[0] // 16, low.shape[1]
    half = cols // 256 * 128
    z = lax.axis_index("dp")
    s = lax.axis_index("seq")
    x, y = s % 2, s // 2
    view = low.reshape(4, 2, 2, rows, cols)
    left, right = view[..., :half], view[..., half:]
    got_a = swapped(take(left, 1 - x, 2), "seq", 1)
    got_b = swapped(take(right, 1 - y, 1), "seq", 2)
    sum_a = take(left, x, 2).astype(f32) + got_a.astype(f32)
    sum_b = take(right, y, 1).astype(f32) + got_b.astype(f32)
    got_a = swapped(to_low(take(sum_a, 1 - y, 1)), "seq", 2)
    got_b = swapped(to_low(take(sum_b, 1 - x, 1)), "seq", 1)
    sum_a = take(sum_a, y, 1) + got_a.astype(f32)
    sum_b = take(sum_b, x, 1) + got_b.astype(f32)
    column = jnp.concatenate([sum_a, sum_b], axis=-1)
    column_low = to_low(column)
    total = take(column, z, 0)
    for k in (1, 2, 3):
        total = total + rotated(take(column_low, (z + k) % 4, 0), "dp", k).astype(f32)
    return total


def rms_apply(inputs, gain_row):
    factor = lax.rsqrt(jnp.mean(inputs * inputs, axis=-1, keepdims=True) + norm_eps)
    return inputs * factor * gain_row


def rope_apply(field_in, positions):
    half_dim = field_in.shape[-1] // 2
    frequency = rope_base ** (-jnp.arange(half_dim, dtype=f32) / half_dim)
    angles = positions[:, None] * frequency[None, :]
    cosine = jnp.cos(angles)[:, None, :]
    sine_part = jnp.sin(angles)[:, None, :]
    lead_half = field_in[..., :half_dim]
    tail_half = field_in[..., half_dim:]
    return jnp.concatenate(
        [lead_half * cosine - tail_half * sine_part, lead_half * sine_part + tail_half * cosine],
        axis=-1,
    )


def adam_step(weight, gradient, first_old, second_old, factor, step_rate, decay_coef):
    clipped = gradient * factor
    first_new = beta_one * first_old + (1.0 - beta_one) * clipped
    second_new = beta_two * second_old + (1.0 - beta_two) * clipped * clipped
    first_hat = first_new / (1.0 - beta_one**STEP)
    second_hat = second_new / (1.0 - beta_two**STEP)
    weight_new = weight - step_rate * (
        first_hat / (jnp.sqrt(second_hat) + adam_eps) + decay_coef * weight
    )
    return (weight_new, first_new, second_new)


def per_device(
    tokens,
    neighbours,
    neighbour_lengths,
    segment_ids,
    out_grad,
    self_weights,
    cross_weights,
    feed_weights,
    norm_gains,
    self_first,
    cross_first,
    feed_first,
    gains_first,
    self_second,
    cross_second,
    feed_second,
    gains_second,
):
    row_count, span_len, model_width = tokens.shape
    local_width = self_weights.shape[2]
    hidden_width = feed_weights.shape[2]
    shard_rows = self_weights.shape[1]
    heads = local_width // HEAD_DIM
    score_scale = HEAD_DIM ** (-0.5)
    blocks_here = span_len // BLOCK
    key_count = NEIGHBOURS * NEIGH_LEN
    halo = min(-(-(DOC_MAX - 1) // span_len), lax.axis_size("seq") - 1)
    s_index = lax.axis_index("seq")

    def columns(*parts):
        return jnp.concatenate([to_low(p) for p in parts], axis=1)

    gain_cols = jnp.zeros((shard_rows, 128), f32).at[:, :3].set(norm_gains.T)
    full_qkv = gather_rows(columns(self_weights[0], self_weights[1], self_weights[2], gain_cols))
    full_kv2 = gather_rows(columns(cross_weights[1], cross_weights[2]))
    full_att = gather_rows(columns(self_weights[3], cross_weights[0], cross_weights[3]))
    full_up = gather_rows(to_low(feed_weights[0]))
    full_down = gather_rows(to_low(feed_weights[1]))
    w_qkv = full_qkv[:, : 3 * local_width]
    gain_values = full_qkv[:, 3 * local_width : 3 * local_width + 3].T.astype(f32)
    w_so = full_att[:, :local_width]
    w_cq = full_att[:, local_width : 2 * local_width]
    w_co = full_att[:, 2 * local_width :]

    def mm(a, b):
        return jnp.dot(a, b, preferred_element_type=f32)

    def mm_t(a, b):
        return lax.dot_general(a, b, (((1,), (1,)), ((), ())), preferred_element_type=f32)

    def t_mm(a, b):
        return lax.dot_general(a, b, (((0,), (0,)), ((), ())), preferred_element_type=f32)

    inputs = tokens.astype(f32).reshape(span_len, model_width)
    query_pos = s_index * span_len + jnp.arange(span_len, dtype=jnp.int32)
    angle_pos = query_pos.astype(f32)
    normed_one, norm_back_one = jax.vjp(rms_apply, inputs, gain_values[0])
    normed_one = to_low(normed_one)
    projected = mm(normed_one, w_qkv)
    head_shape = (span_len, heads, HEAD_DIM)
    query_raw = projected[:, :local_width].reshape(head_shape)
    query_rot, rope_back = jax.vjp(lambda field_in: rope_apply(field_in, angle_pos), query_raw)
    key_rot = rope_apply(projected[:, local_width : 2 * local_width].reshape(head_shape), angle_pos)
    query_low = to_low(query_rot)
    key_low = to_low(key_rot).reshape(span_len, local_width)
    value_low = to_low(projected[:, 2 * local_width :])
    kv_low = jnp.concatenate([key_low, value_low], axis=1)
    seg_here = segment_ids.reshape(1, span_len) + 1
    kv_pieces = [kv_low] + [shifted(kv_low, "seq", k) for k in range(1, halo + 1)]
    seg_pieces = [seg_here] + [shifted(seg_here, "seq", k) for k in range(1, halo + 1)]
    kv_all = jnp.concatenate(kv_pieces, axis=0)
    seg_all = jnp.concatenate(seg_pieces, axis=1)
    keys_all = kv_all[:, :local_width].reshape(-1, heads, HEAD_DIM)
    values_all = kv_all[:, local_width:].reshape(-1, heads, HEAD_DIM)
    offsets = jnp.concatenate(
        [jnp.arange(span_len, dtype=jnp.int32) - k * span_len for k in range(halo + 1)]
    )
    allowed = jnp.logical_and(
        offsets[None, :] <= jnp.arange(span_len, dtype=jnp.int32)[:, None],
        seg_all == seg_here.reshape(span_len, 1),
    )[None]

    def self_scores():
        return jnp.einsum("qhd,khd->hqk", query_low, keys_all, preferred_element_type=f32) * score_scale

    scores = jnp.where(allowed, self_scores(), masked_fill)
    row_max = jnp.max(scores, axis=-1, keepdims=True)
    row_total = jnp.sum(jnp.exp(scores - row_max), axis=-1, keepdims=True)
    self_lse = row_max + jnp.log(row_total)
    self_prob = jnp.where(allowed, jnp.exp(scores - self_lse), 0.0)
    attn_low = to_low(
        jnp.einsum("hqk,khd->qhd", to_low(self_prob), values_all, preferred_element_type=f32)
    ).reshape(span_len, local_width)
    hidden_one = inputs + core_sum(mm_t(attn_low, w_so))
    normed_two, norm_back_two = jax.vjp(rms_apply, hidden_one, gain_values[1])
    normed_two = to_low(normed_two)
    cross_query = to_low(mm(normed_two, w_cq)).reshape(head_shape)
    flat = neighbours.reshape(-1, model_width)
    edge = shifted(flat[-key_count:], "seq", 1)
    flat_all = jnp.concatenate([edge, flat], axis=0)
    kv2 = to_low(mm(flat_all, full_kv2))
    block_keys = kv2[:, :local_width].reshape(blocks_here + 1, key_count, heads, HEAD_DIM)
    block_values = kv2[:, local_width:].reshape(blocks_here + 1, key_count, heads, HEAD_DIM)
    lengths = neighbour_lengths.reshape(blocks_here, NEIGHBOURS)
    prev_info = shifted(jnp.concatenate([lengths[-1], seg_here[0, -1:]]), "seq", 1)
    lengths_all = jnp.concatenate([prev_info[None, :NEIGHBOURS], lengths], axis=0)
    key_valid = jnp.arange(NEIGH_LEN, dtype=jnp.int32)[None, None, :] < lengths_all[:, :, None]
    allowed_cross = key_valid.reshape(blocks_here + 1, 1, 1, key_count)
    seg_pad = jnp.concatenate(
        [prev_info[NEIGHBOURS:], seg_here[0], jnp.zeros((BLOCK - 1,), jnp.int32)]
    ).reshape(blocks_here + 1, BLOCK)
    keep_mask = seg_pad == seg_pad[:, :1]
    keep_float = keep_mask.astype(f32)[:, :, None, None]
    keep_low = keep_mask.astype(bf16)[:, :, None, None]

    def to_blocks(field_in):
        padded = jnp.pad(field_in, ((1, BLOCK - 1), (0, 0), (0, 0)))
        return padded.reshape(blocks_here + 1, BLOCK, heads, HEAD_DIM)

    def from_blocks(blocks_in):
        return blocks_in.reshape((blocks_here + 1) * BLOCK, heads, HEAD_DIM)[1 : span_len + 1]

    query_blocks = to_blocks(cross_query)
    scores = (
        jnp.einsum("bqhd,bkhd->bhqk", query_blocks, block_keys, preferred_element_type=f32)
        * score_scale
    )
    scores = jnp.where(allowed_cross, scores, masked_fill)
    cross_max = jnp.max(scores, axis=-1, keepdims=True)
    cross_total = jnp.sum(jnp.exp(scores - cross_max), axis=-1, keepdims=True)
    cross_lse = cross_max + jnp.log(cross_total)
    cross_prob = jnp.where(allowed_cross, jnp.exp(scores - cross_lse), 0.0)
    cross_out = from_blocks(
        jnp.einsum("bhqk,bkhd->bqhd", to_low(cross_prob), block_values, preferred_element_type=f32)
        * keep_float
    )
    cross_low = to_low(cross_out).reshape(span_len, local_width)
    hidden_two = hidden_one + core_sum(mm_t(cross_low, w_co))
    normed_three, norm_back_three = jax.vjp(rms_apply, hidden_two, gain_values[2])
    normed_three = to_low(normed_three)
    upward = mm(normed_three, full_up)
    active, gelu_back = jax.vjp(partial(jax.nn.gelu, approximate=True), upward)
    active_low = to_low(active)
    result = hidden_two + core_sum(mm_t(active_low, full_down))
    out = to_low(result).reshape(row_count, span_len, model_width)

    cot_low = out_grad.reshape(span_len, model_width)
    cotangent = cot_low.astype(f32)
    grad_active = mm(cot_low, full_down)
    grad_upward = to_low(gelu_back(grad_active)[0])
    down_part = scatter_rows(t_mm(cot_low, active_low))
    up_part = scatter_rows(t_mm(normed_three, grad_upward))
    from_norm, grad_gain_three = norm_back_three(core_sum(mm_t(grad_upward, full_up)))
    grad_two = cotangent + from_norm
    resid_low = to_low(grad_two)
    grad_cross_att = to_low(mm(resid_low, w_co)).reshape(head_shape)
    grad_blocks = to_blocks(grad_cross_att) * keep_low
    grad_prob = jnp.einsum("bqhd,bkhd->bhqk", grad_blocks, block_values, preferred_element_type=f32)
    dot_sum = jnp.sum(cross_prob * grad_prob, axis=-1, keepdims=True)
    grad_score = to_low(cross_prob * (grad_prob - dot_sum))
    grad_cross_query = (
        from_blocks(
            jnp.einsum("bhqk,bkhd->bqhd", grad_score, block_keys, preferred_element_type=f32)
        )
        * score_scale
    )
    grad_keys = to_low(
        jnp.einsum("bhqk,bqhd->bkhd", grad_score, query_blocks, preferred_element_type=f32)
        * score_scale
    ).reshape(-1, local_width)
    grad_values = to_low(
        jnp.einsum("bhqk,bqhd->bkhd", to_low(cross_prob), grad_blocks, preferred_element_type=f32)
    ).reshape(-1, local_width)
    grad_cq_low = to_low(grad_cross_query).reshape(span_len, local_width)
    from_norm, grad_gain_two = norm_back_two(core_sum(mm_t(grad_cq_low, w_cq)))
    cross_part = scatter_rows(
        jnp.concatenate(
            [
                to_low(t_mm(normed_two, grad_cq_low)),
                to_low(t_mm(flat_all, grad_keys)),
                to_low(t_mm(flat_all, grad_values)),
                to_low(t_mm(resid_low, cross_low)),
            ],
            axis=1,
        )
    )
    grad_one = grad_two + from_norm
    att_grad_low = to_low(grad_one)
    grad_attn = to_low(mm(att_grad_low, w_so)).reshape(head_shape)
    so_grad = to_low(t_mm(att_grad_low, attn_low))
    grad_piece = jnp.einsum("qhd,khd->hqk", grad_attn, values_all, preferred_element_type=f32)
    self_dot = jnp.sum(self_prob * grad_piece, axis=-1, keepdims=True)
    score_grad = to_low(self_prob * (grad_piece - self_dot))
    grad_query = jnp.einsum("hqk,khd->qhd", score_grad, keys_all, preferred_element_type=f32)
    key_terms = (
        jnp.einsum("hqk,qhd->khd", score_grad, query_low, preferred_element_type=f32) * score_scale
    ).reshape(-1, local_width)
    value_terms = jnp.einsum(
        "hqk,qhd->khd", to_low(self_prob), grad_attn, preferred_element_type=f32
    ).reshape(-1, local_width)
    terms = jnp.concatenate([key_terms, value_terms], axis=1)
    own_terms = terms[:span_len]
    for k in range(1, halo + 1):
        sent = to_low(terms[k * span_len : (k + 1) * span_len])
        own_terms = own_terms + shifted(sent, "seq", -k).astype(f32)
    grad_q_low = to_low(rope_back(grad_query * score_scale)[0]).reshape(span_len, local_width)
    grad_k_low = to_low(rope_back(own_terms[:, :local_width].reshape(head_shape))[0]).reshape(
        span_len, local_width
    )
    grad_v_low = to_low(own_terms[:, local_width:])
    proj_grads = jnp.concatenate([grad_q_low, grad_k_low, grad_v_low], axis=1)
    qkv_grad = to_low(t_mm(normed_one, proj_grads))
    self_part = scatter_rows(jnp.concatenate([qkv_grad, so_grad], axis=1))
    from_norm, grad_gain_one = norm_back_one(core_sum(mm_t(proj_grads, w_qkv)))
    in_grad = (grad_one + from_norm).reshape(row_count, span_len, model_width)

    gain_grads = butterfly(
        jnp.stack([grad_gain_one, grad_gain_two, grad_gain_three]), ("seq", "dp")
    )
    shard = lax.axis_index("dp") * lax.axis_size("seq") + s_index
    gains_part = lax.dynamic_slice_in_dim(gain_grads, shard * shard_rows, shard_rows, axis=1)
    first_model = (lax.axis_index("mp") == 0).astype(f32)
    local_squares = (
        jnp.sum(self_part * self_part)
        + jnp.sum(cross_part * cross_part)
        + jnp.sum(up_part * up_part)
        + jnp.sum(down_part * down_part)
        + first_model * jnp.sum(gains_part * gains_part)
    )
    grad_norm = jnp.sqrt(butterfly(local_squares.reshape(1, 1), ("mp", "seq", "dp")).reshape(()))
    factor = jnp.minimum(1.0, clip_limit / (grad_norm + 1e-06))

    def split_update(weights, part, first, second, width):
        news = [
            adam_step(
                weights[j],
                part[j],
                first[j],
                second[j],
                factor,
                learn_rate,
                weight_decay,
            )
            for j in range(weights.shape[0])
        ]
        return tuple(jnp.stack([n[i] for n in news]) for i in range(3))

    def cols_of(part, count):
        return [part[:, j * local_width : (j + 1) * local_width] for j in range(count)]

    self_new, self_first_new, self_second_new = split_update(
        self_weights, cols_of(self_part, 4), self_first, self_second, local_width
    )
    cross_new, cross_first_new, cross_second_new = split_update(
        cross_weights, cols_of(cross_part, 4), cross_first, cross_second, local_width
    )
    feed_new, feed_first_new, feed_second_new = split_update(
        feed_weights, [up_part, down_part], feed_first, feed_second, hidden_width
    )
    gains_new, gains_first_new, gains_second_new = adam_step(
        norm_gains, gains_part, gains_first, gains_second, factor, gain_rate, 0.0
    )
    return (
        out,
        in_grad,
        grad_norm,
        self_new,
        cross_new,
        feed_new,
        gains_new,
        self_first_new,
        cross_first_new,
        feed_first_new,
        gains_first_new,
        self_second_new,
        cross_second_new,
        feed_second_new,
        gains_second_new,
    )


def solution(mesh):
    tok = P("dp", "seq", None)
    mat = P(None, ("dp", "seq"), "mp")
    vec = P(None, ("dp", "seq"))
    in_specs = (
        tok,
        P("dp", "seq", None, None, None),
        tok,
        P("dp", "seq"),
        tok,
    ) + (mat, mat, mat, vec) * 3
    out_specs = (tok, tok, P()) + (mat, mat, mat, vec) * 3
    return jax.shard_map(
        per_device, mesh=mesh, in_specs=in_specs, out_specs=out_specs, check_vma=False
    )
```

```python
import jax
import jax.numpy as jnp
from jax import lax
from jax.experimental import pallas as pl
from jax.experimental.pallas import tpu as pltpu
from jax.sharding import PartitionSpec as P

HEAD_DIM = 64
PAIR = 128
BLOCK = 64
NEIGHBOURS = 2
NEIGH_LEN = 128
KEYS = NEIGHBOURS * NEIGH_LEN
STEP = 10
DOC_MAX = 512
CHUNK = 256

norm_eps = 1e-05
rope_base = 10000.0
beta_one = 0.9
beta_two = 0.95
adam_eps = 1e-08
weight_decay = 0.1
learn_rate = 0.1
gain_rate = 0.5
clip_limit = 1.0
masked_fill = -1e30
score_scale = HEAD_DIM ** (-0.5)
gelu_c = 0.7978845608028654
gelu_k = 0.044715

f32 = jnp.float32
bf16 = jnp.bfloat16


def to_low(array_in):
    return array_in.astype(bf16)


def shifted(value, axis, by):
    count = lax.axis_size(axis)
    return lax.ppermute(value, axis, [(i, i + by) for i in range(count) if 0 <= i + by < count])


def rotated(value, axis, by):
    count = lax.axis_size(axis)
    return lax.ppermute(value, axis, [(i, (i + by) % count) for i in range(count)])


def swapped(value, axis, by):
    count = lax.axis_size(axis)
    return lax.ppermute(value, axis, [(i, i ^ by) for i in range(count)])


def butterfly(value, axes):
    for axis in axes:
        step = 1
        while step < lax.axis_size(axis):
            value = value + swapped(value, axis, step)
            step *= 2
    return value


def core_sum(partial_out):
    return partial_out + swapped(partial_out, "mp", 1)


def small_mesh():
    return lax.axis_size("dp") == 4 and lax.axis_size("seq") == 4


def put(buffer, piece, starts):
    return lax.dynamic_update_slice(buffer, piece, starts)


def gather_rows(block):
    if not small_mesh():
        return lax.all_gather(block, ("dp", "seq"), axis=0, tiled=True)
    rows, cols = block.shape
    half = cols // 256 * 128
    z = lax.axis_index("dp")
    s = lax.axis_index("seq")
    pieces = [block] + [rotated(block, "dp", k) for k in (1, 2, 3)]
    column = jnp.zeros((4, rows, cols), block.dtype)
    for k, piece in enumerate(pieces):
        column = put(column, piece[None], ((z - k) % 4, 0, 0))
    from_x = swapped(column, "seq", 1)
    from_y = swapped(column, "seq", 2)
    diag_a = swapped(from_y[..., :half], "seq", 1)
    diag_b = swapped(from_x[..., half:], "seq", 2)
    out = jnp.zeros((4, 4, rows, cols), block.dtype)
    out = put(out, column[:, None], (0, s, 0, 0))
    out = put(out, from_x[:, None], (0, s ^ 1, 0, 0))
    out = put(out, from_y[:, None], (0, s ^ 2, 0, 0))
    out = put(out, diag_a[:, None], (0, s ^ 3, 0, 0))
    out = put(out, diag_b[:, None], (0, s ^ 3, 0, half))
    return out.reshape(16 * rows, cols)


def take(array_in, index, axis):
    return lax.dynamic_index_in_dim(array_in, index, axis, keepdims=False)


def z_sum(column):
    z = lax.axis_index("dp")
    low = to_low(column)
    total = take(column, z, 0).astype(f32)
    for k in (1, 2, 3):
        total = total + rotated(take(low, (z + k) % 4, 0), "dp", k).astype(f32)
    return total


def scatter_rows(left, right):
    if not small_mesh():
        low = jnp.concatenate(left + right, axis=1)
        return lax.psum_scatter(low, ("dp", "seq"), scatter_dimension=0, tiled=True).astype(f32)
    rows = left[0].shape[0] // 16
    s = lax.axis_index("seq")
    x, y = s % 2, s // 2

    def pick(parts, index, axis):
        return jnp.concatenate(
            [take(p.reshape(4, 2, 2, rows, p.shape[1]), index, axis) for p in parts], axis=-1
        )

    got_a = swapped(pick(left, 1 - x, 2), "seq", 1)
    got_b = swapped(pick(right, 1 - y, 1), "seq", 2)
    sum_a = pick(left, x, 2).astype(f32) + got_a.astype(f32)
    sum_b = pick(right, y, 1).astype(f32) + got_b.astype(f32)
    got_a = swapped(to_low(take(sum_a, 1 - y, 1)), "seq", 2)
    got_b = swapped(to_low(take(sum_b, 1 - x, 1)), "seq", 1)
    sum_a = take(sum_a, y, 1) + got_a.astype(f32)
    sum_b = take(sum_b, x, 1) + got_b.astype(f32)
    return z_sum(jnp.concatenate([sum_a, sum_b], axis=-1))


def scatter_feed(parts):
    if not small_mesh():
        low = jnp.concatenate(parts, axis=1)
        return lax.psum_scatter(low, ("dp", "seq"), scatter_dimension=0, tiled=True).astype(f32)
    rows = parts[0].shape[0] // 16
    sums = [
        lax.psum_scatter(
            p.reshape(4, 4, rows, p.shape[1]), "seq", scatter_dimension=1, tiled=True
        )[:, 0]
        for p in parts
    ]
    return z_sum(jnp.concatenate(sums, axis=-1))


def adam_step(weight, gradient, first_old, second_old, factor, step_rate, decay_coef):
    clipped = gradient * factor
    first_new = beta_one * first_old + (1.0 - beta_one) * clipped
    second_new = beta_two * second_old + (1.0 - beta_two) * clipped * clipped
    first_hat = first_new / (1.0 - beta_one**STEP)
    second_hat = second_new / (1.0 - beta_two**STEP)
    weight_new = weight - step_rate * (
        first_hat / (jnp.sqrt(second_hat) + adam_eps) + decay_coef * weight
    )
    return (weight_new, first_new, second_new)


def call(kernel, grid, ins, outs, args, scratch=(), prefetch=0):
    specs = [
        i if isinstance(i, pl.BlockSpec) else pl.BlockSpec(i[0], i[1]) for i in ins
    ]
    return pl.pallas_call(
        kernel,
        out_shape=[jax.ShapeDtypeStruct(o[2], o[3]) for o in outs],
        grid_spec=pltpu.PrefetchScalarGridSpec(
            num_scalar_prefetch=prefetch,
            grid=grid,
            in_specs=specs,
            out_specs=[pl.BlockSpec(o[0], o[1]) for o in outs],
            scratch_shapes=list(scratch),
        ),
        compiler_params=pltpu.CompilerParams(
            dimension_semantics=("arbitrary",) * len(grid), vmem_limit_bytes=56 << 20
        ),
    )(*args)


def dot(a, b):
    return jnp.dot(a, b, preferred_element_type=f32)


def dot_t(a, b):
    return lax.dot_general(a, b, (((1,), (1,)), ((), ())), preferred_element_type=f32)


def t_dot(a, b):
    return lax.dot_general(a, b, (((0,), (0,)), ((), ())), preferred_element_type=f32)


def rms_factor(z):
    return lax.rsqrt(jnp.mean(z * z, axis=-1, keepdims=True) + norm_eps)


def rms_back(z, gain, grad):
    factor = rms_factor(z)
    scaled = grad * gain
    inner = jnp.mean(scaled * z, axis=-1, keepdims=True)
    return factor * scaled - z * (factor * factor * factor * inner), grad * z * factor


def lane_in_head(shape):
    return lax.broadcasted_iota(jnp.int32, shape, 1)


def rope(z, cos, sin, sign):
    lane = lane_in_head(z.shape)
    lead = lane % HEAD_DIM < HEAD_DIM // 2
    partner = jnp.where(lead, -pltpu.roll(z, PAIR - 32, 1), pltpu.roll(z, 32, 1))
    return z * cos + partner * (sin * sign)


def split_heads(z):
    first = lane_in_head(z.shape) < HEAD_DIM
    zero = jnp.zeros_like(z)
    return jnp.where(first, z, zero), jnp.where(first, zero, z)


def join_heads(a, b):
    return jnp.where(lane_in_head(a.shape) < HEAD_DIM, a, b)


def qkv_kernel(x_ref, g_ref, w_ref, cos_ref, sin_ref, n_ref, q_ref, k_ref, v_ref):
    x = x_ref[...].astype(f32)
    width = q_ref.shape[1]
    normed = to_low(x * rms_factor(x) * g_ref[...])
    n_ref[...] = normed
    cos, sin = cos_ref[...], sin_ref[...]

    def turned(raw):
        return jnp.concatenate(
            [
                to_low(rope(raw[:, c : c + PAIR], cos, sin, 1.0))
                for c in range(0, width, PAIR)
            ],
            axis=1,
        )

    k_ref[...] = turned(dot(normed, w_ref[:, width : 2 * width]))
    v_ref[...] = to_low(dot(normed, w_ref[:, 2 * width : 3 * width]))

    @pl.when(pl.program_id(0) == pl.num_programs(0) - 1)
    def _():
        q_ref[...] = turned(dot(normed, w_ref[:, :width]))


def qkv_call(x_ext, gain, w, cos, sin, span, width):
    rows, model = x_ext.shape
    steps = rows // span
    row = lambda i: (i, 0)
    fix = lambda i: (0, 0)
    return call(
        qkv_kernel,
        (steps,),
        [
            ((span, model), row),
            ((1, model), fix),
            ((model, 3 * width), fix),
            ((span, PAIR), row),
            ((span, PAIR), row),
        ],
        [
            ((span, model), row, (rows, model), bf16),
            ((span, width), fix, (span, width), bf16),
            ((span, width), row, (rows, width), bf16),
            ((span, width), row, (rows, width), bf16),
        ],
        (x_ext, gain, w, cos, sin),
    )


def self_bias(segq_ref, segk_ref, bias_ref):
    keys, span = bias_ref.shape
    key_pos = lax.broadcasted_iota(jnp.int32, (keys, span), 0) - (keys - span)
    query_pos = lax.broadcasted_iota(jnp.int32, (keys, span), 1)
    ok = jnp.logical_and(key_pos <= query_pos, segk_ref[...] == segq_ref[...])
    bias_ref[...] = jnp.where(ok, 0.0, masked_fill)


def self_kernel(q_ref, k_ref, v_ref, segq_ref, segk_ref, w_ref, o_ref, lse_ref, part_ref, bias_ref):
    @pl.when(pl.program_id(0) == 0)
    def _():
        self_bias(segq_ref, segk_ref, bias_ref)
        part_ref[...] = jnp.zeros_like(part_ref)

    k, v, bias = k_ref[...], v_ref[...], bias_ref[...]
    outs, lses = [], []
    for qh in split_heads(q_ref[...] * score_scale):
        s = dot_t(k, qh) + bias
        top = jnp.max(s, axis=0, keepdims=True)
        e = jnp.exp(s - top)
        total = jnp.sum(e, axis=0, keepdims=True)
        lses.append(top + jnp.log(total))
        outs.append(t_dot(to_low(e * (1.0 / total)), v))
    o = to_low(join_heads(outs[0], outs[1]))
    o_ref[...] = o
    lse_ref[0] = jnp.concatenate(lses, axis=0)
    part_ref[...] += dot_t(o, w_ref[...])


def self_call(q, k, v, segq, segk, w_att, at, model):
    span, width = q.shape
    keys = k.shape[0]
    pair = lambda p: (0, p)
    fix = lambda p: (0, 0)
    return call(
        self_kernel,
        (width // PAIR,),
        [
            ((span, PAIR), pair),
            ((keys, PAIR), pair),
            ((keys, PAIR), pair),
            ((1, span), fix),
            ((keys, 1), fix),
            ((model, PAIR), lambda p: (0, at + p)),
        ],
        [
            ((span, PAIR), pair, (span, width), bf16),
            ((1, 2, span), lambda p: (p, 0, 0), (width // PAIR, 2, span), f32),
            ((span, model), fix, (span, model), f32),
        ],
        (q, k, v, segq, segk, w_att),
        scratch=[pltpu.VMEM((keys, span), f32)],
    )


def block_bias(len_ref, block, rows):
    lane = lax.broadcasted_iota(jnp.int32, (rows, KEYS), 1)
    limit = jnp.where(lane < NEIGH_LEN, len_ref[block, 0], len_ref[block, 1])
    return jnp.where(lane % NEIGH_LEN < limit, 0.0, masked_fill)


def tile_bias(len_ref, tile, tiles):
    if tile:
        return block_bias(len_ref, tile, BLOCK)
    row = lax.broadcasted_iota(jnp.int32, (BLOCK, KEYS), 0)
    lead = jnp.where(row > 0, block_bias(len_ref, 0, BLOCK), masked_fill)
    last = jnp.where(row > 0, masked_fill, block_bias(len_ref, tiles, BLOCK))
    return jnp.concatenate([lead, last], axis=1)


def tile_keys(ref, tile, tiles):
    own = ref[tile * KEYS : (tile + 1) * KEYS, :]
    if tile:
        return own
    return jnp.concatenate([own, ref[tiles * KEYS : (tiles + 1) * KEYS, :]], axis=0)


def cross_kernel(
    len_ref, x_ref, pa_ref, pb_ref, g_ref, wq_ref, k_ref, v_ref, keep_ref, wo_ref,
    h_ref, n_ref, q_ref, o_ref, lse_ref, part_ref, acc_ref,
):
    span = x_ref.shape[0]
    tiles = span // BLOCK

    @pl.when(pl.program_id(0) == 0)
    def _():
        h = x_ref[...].astype(f32) + (pa_ref[...] + pb_ref[...])
        h_ref[...] = h
        n_ref[...] = to_low(h * rms_factor(h) * g_ref[...])
        part_ref[...] = jnp.zeros_like(part_ref)

    turned = pltpu.roll(to_low(dot(n_ref[...], wq_ref[...])).astype(f32), 1, 0)
    q = to_low(turned * score_scale)
    q_ref[...] = q
    for tile in range(tiles):
        rows = slice(tile * BLOCK, (tile + 1) * BLOCK)
        k, v = tile_keys(k_ref, tile, tiles), tile_keys(v_ref, tile, tiles)
        bias = tile_bias(len_ref, tile, tiles)
        outs, lses = [], []
        for qh in split_heads(q[rows]):
            s = dot_t(qh, k) + bias
            top = jnp.max(s, axis=1, keepdims=True)
            e = jnp.exp(s - top)
            total = jnp.sum(e, axis=1, keepdims=True)
            lses.append(top + jnp.log(total))
            outs.append(dot(to_low(e * (1.0 / total)), v))
        acc_ref[rows, :] = join_heads(outs[0], outs[1])
        lse_ref[rows, :] = join_heads(
            jnp.broadcast_to(lses[0], (BLOCK, PAIR)), jnp.broadcast_to(lses[1], (BLOCK, PAIR))
        )
    o = to_low(pltpu.roll(acc_ref[...] * keep_ref[...], span - 1, 0))
    o_ref[...] = o
    part_ref[...] += dot_t(o, wo_ref[...])


def cross_call(lens, x, pa, pb, gain, w_att, at_q, at_o, kv2, keep):
    span, model = x.shape
    keys, width = kv2.shape[0], kv2.shape[1] // 2
    pairs = width // PAIR
    pair = lambda p, *_: (0, p)
    fix = lambda p, *_: (0, 0)
    return call(
        cross_kernel,
        (pairs,),
        [
            ((span, model), fix),
            ((span, model), fix),
            ((span, model), fix),
            ((1, model), fix),
            ((model, PAIR), lambda p, *_: (0, at_q + p)),
            ((keys, PAIR), pair),
            ((keys, PAIR), lambda p, *_: (0, pairs + p)),
            ((span, 1), fix),
            ((model, PAIR), lambda p, *_: (0, at_o + p)),
        ],
        [
            ((span, model), fix, (span, model), f32),
            ((span, model), fix, (span, model), bf16),
            ((span, PAIR), pair, (span, width), bf16),
            ((span, PAIR), pair, (span, width), bf16),
            ((span, PAIR), pair, (span, width), f32),
            ((span, model), fix, (span, model), f32),
        ],
        (lens, x, pa, pb, gain, w_att, kv2, kv2, keep, w_att),
        scratch=[pltpu.VMEM((span, PAIR), f32)],
        prefetch=1,
    )


def feed_kernel(h1_ref, pa_ref, pb_ref, g_ref, cot_ref, up_ref, down_ref,
                h_ref, n_ref, act_ref, du_ref, y_ref, dn_ref):
    @pl.when(pl.program_id(0) == 0)
    def _():
        h = h1_ref[...] + (pa_ref[...] + pb_ref[...])
        h_ref[...] = h
        n_ref[...] = to_low(h * rms_factor(h) * g_ref[...])
        y_ref[...] = jnp.zeros_like(y_ref)
        dn_ref[...] = jnp.zeros_like(dn_ref)

    up, down = up_ref[...], down_ref[...]
    u = dot(n_ref[...], up)
    t = jnp.tanh(gelu_c * (u + gelu_k * (u * u * u)))
    act = to_low(0.5 * u * (1.0 + t))
    slope = 0.5 * (1.0 + t) + 0.5 * u * (1.0 - t * t) * (gelu_c * (1.0 + 3.0 * gelu_k * (u * u)))
    du = to_low(dot(cot_ref[...], down) * slope)
    act_ref[...] = act
    du_ref[...] = du
    y_ref[...] += dot_t(act, down)
    dn_ref[...] += dot_t(du, up)


def feed_call(h1, pa, pb, gain, cot, w_feed, hidden):
    span, model = h1.shape
    steps = hidden // CHUNK
    fix = lambda c: (0, 0)
    col = lambda c: (0, c)
    return call(
        feed_kernel,
        (steps,),
        [
            ((span, model), fix),
            ((span, model), fix),
            ((span, model), fix),
            ((1, model), fix),
            ((span, model), fix),
            ((model, CHUNK), col),
            ((model, CHUNK), lambda c: (0, steps + c)),
        ],
        [
            ((span, model), fix, (span, model), f32),
            ((span, model), fix, (span, model), bf16),
            ((span, CHUNK), col, (span, hidden), bf16),
            ((span, CHUNK), col, (span, hidden), bf16),
            ((span, model), fix, (span, model), f32),
            ((span, model), fix, (span, model), f32),
        ],
        (h1, pa, pb, gain, cot, w_feed, w_feed),
    )


def cross_back_kernel(
    len_ref, base_ref, h_ref, da_ref, db_ref, g_ref, wo_ref, q_ref, k_ref, v_ref, lse_ref,
    keep_ref, wq_ref,
    grad_ref, low_ref, gain_ref, dq_ref, dk_ref, dv_ref, dn_ref, acc_ref,
):
    span = h_ref.shape[0]
    tiles = span // BLOCK

    @pl.when(pl.program_id(0) == 0)
    def _():
        back, gains = rms_back(h_ref[...], g_ref[...], da_ref[...] + db_ref[...])
        grad = base_ref[...].astype(f32) + back
        grad_ref[...] = grad
        low_ref[...] = to_low(grad)
        gain_ref[...] = jnp.sum(gains, axis=0, keepdims=True)
        dn_ref[...] = jnp.zeros_like(dn_ref)

    do = to_low(dot(low_ref[...], wo_ref[...])).astype(f32)
    do = to_low(pltpu.roll(do, 1, 0) * keep_ref[...])
    q = q_ref[...]
    for tile in range(tiles):
        rows = slice(tile * BLOCK, (tile + 1) * BLOCK)
        k, v = tile_keys(k_ref, tile, tiles), tile_keys(v_ref, tile, tiles)
        bias = tile_bias(len_ref, tile, tiles)
        dqs, scores, probs = [], [], []
        qs, dos = split_heads(q[rows]), split_heads(do[rows])
        for h in range(2):
            p = jnp.exp(dot_t(qs[h], k) + bias - lse_ref[rows, h * HEAD_DIM : h * HEAD_DIM + 1])
            dp = dot_t(dos[h], v)
            ds = to_low(p * (dp - jnp.sum(p * dp, axis=1, keepdims=True)))
            dqs.append(dot(ds, k))
            scores.append(ds)
            probs.append(to_low(p))
        acc_ref[rows, :] = join_heads(dqs[0], dqs[1])
        dk = to_low(t_dot(scores[0], qs[0]) + t_dot(scores[1], qs[1]))
        dv = to_low(t_dot(probs[0], dos[0]) + t_dot(probs[1], dos[1]))
        own = slice(tile * KEYS, (tile + 1) * KEYS)
        dk_ref[own, :] = dk[:KEYS]
        dv_ref[own, :] = dv[:KEYS]
        if not tile:
            last = slice(tiles * KEYS, (tiles + 1) * KEYS)
            dk_ref[last, :] = dk[KEYS:]
            dv_ref[last, :] = dv[KEYS:]
    dq = to_low(pltpu.roll(acc_ref[...] * score_scale, span - 1, 0))
    dq_ref[...] = dq
    dn_ref[...] += dot_t(dq, wq_ref[...])


def cross_back_call(lens, base, h, da, db, gain, w_att, at_q, at_o, q, kv2, lse, keep):
    span, model = h.shape
    keys, width = kv2.shape[0], kv2.shape[1] // 2
    pairs = width // PAIR
    pair = lambda p, *_: (0, p)
    fix = lambda p, *_: (0, 0)
    return call(
        cross_back_kernel,
        (pairs,),
        [
            ((span, model), fix),
            ((span, model), fix),
            ((span, model), fix),
            ((span, model), fix),
            ((1, model), fix),
            ((model, PAIR), lambda p, *_: (0, at_o + p)),
            ((span, PAIR), pair),
            ((keys, PAIR), pair),
            ((keys, PAIR), lambda p, *_: (0, pairs + p)),
            ((span, PAIR), pair),
            ((span, 1), fix),
            ((model, PAIR), lambda p, *_: (0, at_q + p)),
        ],
        [
            ((span, model), fix, (span, model), f32),
            ((span, model), fix, (span, model), bf16),
            ((1, model), fix, (1, model), f32),
            ((span, PAIR), pair, (span, width), bf16),
            ((keys, PAIR), pair, (keys, width), bf16),
            ((keys, PAIR), pair, (keys, width), bf16),
            ((span, model), fix, (span, model), f32),
        ],
        (lens, base, h, da, db, gain, w_att, q, kv2, kv2, lse, keep, w_att),
        scratch=[pltpu.VMEM((span, PAIR), f32)],
        prefetch=1,
    )


def self_back_kernel(
    base_ref, h_ref, da_ref, db_ref, g_ref, w_ref, q_ref, k_ref, v_ref, lse_ref, segq_ref,
    segk_ref, cos_ref, sin_ref,
    grad_ref, low_ref, gain_ref, dq_ref, dk_ref, dv_ref, bias_ref,
):
    span = h_ref.shape[0]
    keys = k_ref.shape[0]

    @pl.when(pl.program_id(0) == 0)
    def _():
        back, gains = rms_back(h_ref[...], g_ref[...], da_ref[...] + db_ref[...])
        grad = base_ref[...] + back
        grad_ref[...] = grad
        low_ref[...] = to_low(grad)
        gain_ref[...] = jnp.sum(gains, axis=0, keepdims=True)
        self_bias(segq_ref, segk_ref, bias_ref)

    do = to_low(dot(low_ref[...], w_ref[...]))
    k, v, bias = k_ref[...], v_ref[...], bias_ref[...]
    qs, dos = split_heads(q_ref[...] * score_scale), split_heads(do)
    dqs, dk, dv = [], 0.0, 0.0
    for h in range(2):
        p = jnp.exp(dot_t(k, qs[h]) + bias - lse_ref[0, h : h + 1, :])
        dp = dot_t(v, dos[h])
        ds = to_low(p * (dp - jnp.sum(p * dp, axis=0, keepdims=True)))
        dqs.append(t_dot(ds, k))
        dk = dk + dot(ds, qs[h])
        dv = dv + dot(to_low(p), dos[h])
    cos, sin = cos_ref[...], sin_ref[...]
    dq = join_heads(dqs[0], dqs[1]) * score_scale
    dq_ref[...] = to_low(rope(dq, cos[keys - span :], sin[keys - span :], -1.0))
    dk_ref[...] = to_low(rope(dk, cos, sin, -1.0))
    dv_ref[...] = to_low(dv)


def self_back_call(base, h, da, db, gain, w_att, at, q, k, v, lse, segq, segk, cos, sin):
    span, model = h.shape
    keys, width = k.shape
    pair = lambda p: (0, p)
    fix = lambda p: (0, 0)
    return call(
        self_back_kernel,
        (width // PAIR,),
        [
            ((span, model), fix),
            ((span, model), fix),
            ((span, model), fix),
            ((span, model), fix),
            ((1, model), fix),
            ((model, PAIR), lambda p: (0, at + p)),
            ((span, PAIR), pair),
            ((keys, PAIR), pair),
            ((keys, PAIR), pair),
            ((1, 2, span), lambda p: (p, 0, 0)),
            ((1, span), fix),
            ((keys, 1), fix),
            ((keys, PAIR), fix),
            ((keys, PAIR), fix),
        ],
        [
            ((span, model), fix, (span, model), f32),
            ((span, model), fix, (span, model), bf16),
            ((1, model), fix, (1, model), f32),
            ((span, PAIR), pair, (span, width), bf16),
            ((keys, PAIR), pair, (keys, width), bf16),
            ((keys, PAIR), pair, (keys, width), bf16),
        ],
        (base, h, da, db, gain, w_att, q, k, v, lse, segq, segk, cos, sin),
        scratch=[pltpu.VMEM((keys, span), f32)],
    )


def inner_kernel(x_ref, dq_ref, dk_ref, dv_ref, w_ref, dn_ref, gain_ref):
    step = pl.program_id(0)
    last = pl.num_programs(0) - 1
    width = dk_ref.shape[1]

    @pl.when(step == 0)
    def _():
        gain_ref[...] = jnp.zeros_like(gain_ref)

    dn_ref[...] = dot_t(dk_ref[...], w_ref[:, width : 2 * width]) + dot_t(
        dv_ref[...], w_ref[:, 2 * width : 3 * width]
    )

    @pl.when(step == last)
    def _():
        dn_ref[...] += dot_t(dq_ref[...], w_ref[:, :width])

    x = x_ref[...].astype(f32)
    gain_ref[...] += jnp.sum(dn_ref[...] * x * rms_factor(x), axis=0, keepdims=True)


def inner_call(x_ext, dq, dk, dv, w):
    rows, model = x_ext.shape
    span, width = dq.shape
    row = lambda i: (i, 0)
    fix = lambda i: (0, 0)
    return call(
        inner_kernel,
        (rows // span,),
        [
            ((span, model), row),
            ((span, width), fix),
            ((span, width), row),
            ((span, width), row),
            ((model, 3 * width), fix),
        ],
        [
            ((span, model), row, (rows, model), f32),
            ((1, model), fix, (1, model), f32),
        ],
        (x_ext, dq, dk, dv, w),
    )


def adam_kernel(factor_ref, w_ref, g_ref, m_ref, v_ref, wo_ref, mo_ref, vo_ref):
    wo_ref[0], mo_ref[0], vo_ref[0] = adam_step(
        w_ref[0], g_ref[...], m_ref[0], v_ref[0], factor_ref[0], learn_rate, weight_decay
    )


def adam_call(factor, weights, grads, first, second, order):
    count, rows, width = weights.shape
    each = lambda j, *_: (j, 0, 0)
    block = ((1, rows, width), each)
    out = ((1, rows, width), each, weights.shape, f32)
    return call(
        adam_kernel,
        (count,),
        [block, ((rows, width), lambda j, *_: (0, order(j))), block, block],
        [out, out, out],
        (factor, weights, grads, first, second),
        prefetch=1,
    )


def rows_kernel(a_ref, w_ref, o_ref):
    o_ref[...] = to_low(dot(a_ref[...], w_ref[...]))


def rows_call(a, w, width):
    rows, model = a.shape
    return call(
        rows_kernel,
        (rows // KEYS,),
        [((KEYS, model), lambda i: (i, 0)), ((model, width), lambda i: (0, 0))],
        [((KEYS, width), lambda i: (i, 0), (rows, width), bf16)],
        (a, w),
    )[0]


def per_device(
    tokens,
    neighbours,
    neighbour_lengths,
    segment_ids,
    out_grad,
    self_weights,
    cross_weights,
    feed_weights,
    norm_gains,
    self_first,
    cross_first,
    feed_first,
    gains_first,
    self_second,
    cross_second,
    feed_second,
    gains_second,
):
    row_count, span, model = tokens.shape
    width = self_weights.shape[2]
    hidden = feed_weights.shape[2]
    shard_rows = self_weights.shape[1]
    pairs = width // PAIR
    blocks = span // BLOCK
    halo = min(-(-(DOC_MAX - 1) // span), lax.axis_size("seq") - 1)
    s_index = lax.axis_index("seq")
    core = lax.axis_index("mp")

    def columns(*parts):
        return jnp.concatenate([to_low(p) for p in parts], axis=1)

    gain_cols = jnp.zeros((shard_rows, 128), f32).at[:, :3].set(norm_gains.T)
    full_feed = lax.all_gather(
        columns(feed_weights[0], feed_weights[1]), ("dp", "seq"), axis=0, tiled=True
    )
    full_qkv = gather_rows(columns(self_weights[0], self_weights[1], self_weights[2], gain_cols))
    full_att = gather_rows(
        columns(cross_weights[1], cross_weights[2], self_weights[3], cross_weights[0], cross_weights[3])
    )
    at_so, at_cq, at_co = 2 * pairs, 3 * pairs, 4 * pairs
    gains = full_qkv[:, 3 * width : 3 * width + 3].T.astype(f32)

    x = tokens.reshape(span, model)
    flat = neighbours.reshape(-1, model)
    half = span // 2
    pad = KEYS // 2
    mine = lax.dynamic_slice_in_dim(x, core * half, half, 0)
    edge = lax.dynamic_slice_in_dim(flat, flat.shape[0] - KEYS + core * pad, pad, 0)
    got = shifted(jnp.concatenate([mine, edge], axis=0), "seq", 1)
    far = [shifted(mine, "seq", k) for k in range(2, halo + 1)]
    got = jnp.concatenate([got] + far, axis=0)
    other = swapped(got, "mp", 1)
    low_half = jnp.where(core == 0, got, other)
    high_half = jnp.where(core == 0, other, got)

    def whole(start, size):
        return [low_half[start : start + size], high_half[start : start + size]]

    pieces = []
    for k in range(halo, 1, -1):
        pieces += whole(half + pad + (k - 2) * half, half)
    x_ext = jnp.concatenate(pieces + whole(0, half) + [x], axis=0)
    flat_ext = jnp.concatenate(whole(half, pad) + [flat], axis=0)

    seg_here = segment_ids.reshape(1, span) + 1
    lengths = neighbour_lengths.reshape(blocks, NEIGHBOURS)
    ints = jnp.concatenate([seg_here[0], lengths[-1]])[None]
    ints_prev = [shifted(ints, "seq", k) for k in range(1, halo + 1)]
    seg_keys = jnp.concatenate([p[:, :span] for p in ints_prev[::-1]] + [seg_here], axis=1)
    seg_keys = seg_keys.reshape(-1, 1)
    lens = jnp.concatenate([ints_prev[0][:, span:], lengths], axis=0)
    before = jnp.concatenate([ints_prev[0][0, span - 1 : span], seg_here[0, : span - 1]])
    heads_of = jnp.repeat(before[::BLOCK], BLOCK)
    keep = (before == heads_of).at[0].set(True)
    valid_from = jnp.where(s_index == 0, BLOCK, 0)
    spot = jnp.arange(span)
    keep = jnp.where(jnp.logical_or(spot == 0, spot >= valid_from), keep, False)
    keep = keep.astype(f32).reshape(span, 1)

    frequency = rope_base ** (-(jnp.arange(PAIR) % (HEAD_DIM // 2)).astype(f32) / (HEAD_DIM // 2))
    places = (s_index - halo) * span + jnp.arange((halo + 1) * span)
    angles = places.astype(f32)[:, None] * frequency[None, :]
    cos, sin = jnp.cos(angles), jnp.sin(angles)

    n1, q, k, v = qkv_call(x_ext, gains[:1], full_qkv, cos, sin, span, width)
    attn, lse, part = self_call(q, k, v, seg_here, seg_keys, full_att, at_so, model)
    kv2 = rows_call(flat_ext, full_att, 2 * width)
    h1, n2, q2, cross, lse2, part2 = cross_call(
        lens, x, part, swapped(part, "mp", 1), gains[1:2], full_att, at_cq, at_co, kv2, keep
    )
    cot = out_grad.reshape(span, model)
    h2, n3, act, du, y, dn3 = feed_call(
        h1, part2, swapped(part2, "mp", 1), gains[2:3], cot, full_feed, hidden
    )
    out = to_low(h2 + core_sum(y)).reshape(row_count, span, model)
    feed_part = scatter_feed([to_low(t_dot(n3, du)), to_low(t_dot(cot, act))])
    g2, low2, dgain3, dq2, dk2, dv2, dn2 = cross_back_call(
        lens, cot, h2, dn3, swapped(dn3, "mp", 1), gains[2:3], full_att, at_cq, at_co,
        q2, kv2, lse2, keep,
    )
    cross_part = scatter_rows(
        [to_low(t_dot(n2, dq2)), to_low(t_dot(low2, cross))],
        [to_low(t_dot(flat_ext, dk2)), to_low(t_dot(flat_ext, dv2))],
    )
    g1, low1, dgain2, dq, dk, dv = self_back_call(
        g2, h1, dn2, swapped(dn2, "mp", 1), gains[1:2], full_att, at_so,
        q, k, v, lse, seg_here, seg_keys, cos, sin,
    )
    self_part = scatter_rows(
        [to_low(t_dot(n1[halo * span :], dq)), to_low(t_dot(low1, attn))],
        [to_low(t_dot(n1, dk)), to_low(t_dot(n1, dv))],
    )
    dn1, dgain1 = inner_call(x_ext, dq, dk, dv, full_qkv)
    own = dn1[halo * span :]
    for k_off in range(1, halo + 1):
        start = (halo - k_off) * span
        own = own + shifted(to_low(dn1[start : start + span]), "seq", -k_off).astype(f32)
    back, _ = rms_back(x.astype(f32), gains[:1], core_sum(own))
    in_grad = (g1 + back).reshape(row_count, span, model)

    gain_grads = butterfly(
        jnp.concatenate([dgain1, 0.5 * dgain2, 0.5 * dgain3], axis=0), ("mp", "seq", "dp")
    )
    shard = lax.axis_index("dp") * lax.axis_size("seq") + s_index
    gains_part = lax.dynamic_slice_in_dim(gain_grads, shard * shard_rows, shard_rows, axis=1)
    first_model = (core == 0).astype(f32)
    local_squares = (
        jnp.sum(self_part * self_part)
        + jnp.sum(cross_part * cross_part)
        + jnp.sum(feed_part * feed_part)
        + first_model * jnp.sum(gains_part * gains_part)
    )
    grad_norm = jnp.sqrt(butterfly(local_squares.reshape(1, 1), ("mp", "seq", "dp")).reshape(()))
    factor = jnp.minimum(1.0, clip_limit / (grad_norm + 1e-06))
    scalar = factor.reshape(1)
    mixed = lambda j: jnp.where(j == 0, 0, jnp.where(j == 3, 1, j + 1))
    plain = lambda j: j
    self_new, self_first_new, self_second_new = adam_call(
        scalar, self_weights, self_part, self_first, self_second, mixed
    )
    cross_new, cross_first_new, cross_second_new = adam_call(
        scalar, cross_weights, cross_part, cross_first, cross_second, mixed
    )
    feed_new, feed_first_new, feed_second_new = adam_call(
        scalar, feed_weights, feed_part, feed_first, feed_second, plain
    )
    gains_new, gains_first_new, gains_second_new = adam_step(
        norm_gains, gains_part, gains_first, gains_second, factor, gain_rate, 0.0
    )
    return (
        out,
        in_grad,
        grad_norm,
        self_new,
        cross_new,
        feed_new,
        gains_new,
        self_first_new,
        cross_first_new,
        feed_first_new,
        gains_first_new,
        self_second_new,
        cross_second_new,
        feed_second_new,
        gains_second_new,
    )


def solution(mesh):
    tok = P("dp", "seq", None)
    mat = P(None, ("dp", "seq"), "mp")
    vec = P(None, ("dp", "seq"))
    in_specs = (
        tok,
        P("dp", "seq", None, None, None),
        tok,
        P("dp", "seq"),
        tok,
    ) + (mat, mat, mat, vec) * 3
    out_specs = (tok, tok, P()) + (mat, mat, mat, vec) * 3
    return jax.shard_map(
        per_device, mesh=mesh, in_specs=in_specs, out_specs=out_specs, check_vma=False
    )
```

```python
import jax
import jax.numpy as jnp
from jax import lax
from jax.experimental import pallas as pl
from jax.experimental.pallas import tpu as pltpu
from jax.sharding import PartitionSpec as P

HEAD_DIM = 64
PAIR = 128
BLOCK = 64
NEIGHBOURS = 2
NEIGH_LEN = 128
KEYS = NEIGHBOURS * NEIGH_LEN
STEP = 10
DOC_MAX = 512
CHUNK = 256
TOKENS = 512

norm_eps = 1e-05
rope_base = 10000.0
beta_one = 0.9
beta_two = 0.95
adam_eps = 1e-08
weight_decay = 0.1
learn_rate = 0.1
gain_rate = 0.5
clip_limit = 1.0
masked_fill = -1e30
score_scale = HEAD_DIM ** (-0.5)
gelu_c = 0.7978845608028654
gelu_k = 0.044715

f32 = jnp.float32
bf16 = jnp.bfloat16


def to_low(array_in):
    return array_in.astype(bf16)


def shifted(value, axis, by):
    count = lax.axis_size(axis)
    return lax.ppermute(value, axis, [(i, i + by) for i in range(count) if 0 <= i + by < count])


def rotated(value, axis, by):
    count = lax.axis_size(axis)
    return lax.ppermute(value, axis, [(i, (i + by) % count) for i in range(count)])


def swapped(value, axis, by):
    count = lax.axis_size(axis)
    return lax.ppermute(value, axis, [(i, i ^ by) for i in range(count)])


def butterfly(value, axes):
    for axis in axes:
        step = 1
        while step < lax.axis_size(axis):
            value = value + swapped(value, axis, step)
            step *= 2
    return value


def sum_everywhere(value):
    axes = ("dp", "seq", "mp")
    if not small_mesh():
        return butterfly(value, axes)
    count = lax.axis_size("dp") * lax.axis_size("seq") * lax.axis_size("mp")
    spread = jnp.broadcast_to(value, (count, 8, PAIR))
    return jnp.sum(lax.all_to_all(spread, axes, 0, 0, tiled=True)[:, :1, :1], axis=0)


def core_sum(partial_out):
    return partial_out + swapped(partial_out, "mp", 1)


def small_mesh():
    return lax.axis_size("dp") == 4 and lax.axis_size("seq") == 4


def put(buffer, piece, starts):
    return lax.dynamic_update_slice(buffer, piece, starts)


def meet(*values):
    return lax.optimization_barrier(values)


def token_of(array_in):
    return array_in[:8, :PAIR]


ORDER = (0, 2, 1, 3)


def own_order(model, s):
    rows = model // 16
    spot = jnp.arange(model)
    near, z, inner = spot // (4 * rows), spot // rows % 4, spot % rows
    flip = (near % 2) * 2 + near // 2
    source = (z * 4 + (s ^ flip)) * rows + inner
    return (spot[:, None] == source[None, :]).astype(bf16)


def plane_sum(pieces):
    return (pieces[0] + pieces[1].astype(f32)) + (pieces[2].astype(f32) + pieces[3].astype(f32))


def take(array_in, index, axis):
    return lax.dynamic_index_in_dim(array_in, index, axis, keepdims=False)


def wide_for_dp(block):
    rows, cols = block.shape
    return jnp.broadcast_to(block[None], (4, rows, cols)).reshape(4 * rows, cols)


def exchanged(array_in, axis):
    return lax.all_to_all(array_in, axis, 0, 0, tiled=True)


def from_seq(column):
    return [swapped(column, "seq", k) for k in ORDER[1:]]


def weight(pieces, start):
    return [(p, start) for p in pieces]


def reduce_first(sent):
    return swapped(sent[0], "seq", 1), swapped(sent[1], "seq", 2)


def reduce_second(kept, got):
    keep_a, keep_b, sent_a, sent_b = half_sum_call(kept, got)
    return (keep_a, keep_b), (swapped(sent_a, "seq", 2), swapped(sent_b, "seq", 1))


def last_sum(kept, got):
    return jnp.concatenate(
        [to_low(k.astype(f32) + g.astype(f32)) for k, g in zip(kept, got)], axis=1
    )


def reduce_last(got):
    rows, cols = got.shape
    return jnp.sum(got.reshape(4, rows // 4, cols).astype(f32), axis=0)


def reduce_plain(grads):
    return lax.psum_scatter(
        jnp.concatenate(grads, axis=1), ("dp", "seq"), scatter_dimension=0, tiled=True
    ).astype(f32)


def halves(left, right):
    if not small_mesh():
        return None, [jnp.concatenate([to_low(t_dot(a, b)) for a, b in left + right], axis=1)]

    def products(pairs, pick):
        parts = [to_low(t_dot(pick(a), b)) for a, b in pairs]
        return parts[0] if len(parts) == 1 else jnp.concatenate(parts, axis=1)

    def second(a, first):
        quarter = a.shape[1] // 4
        return jnp.concatenate(
            [
                a[:, first * quarter : (first + 1) * quarter],
                a[:, (first + 2) * quarter : (first + 3) * quarter],
            ],
            axis=1,
        )

    mid = left[0][0].shape[1] // 2
    sent = (products(left, lambda a: a[:, mid:]), products(right, lambda a: second(a, 1)))
    kept = (products(left, lambda a: a[:, :mid]), products(right, lambda a: second(a, 0)))
    return sent, kept


def adam_step(weight, gradient, first_old, second_old, factor, step_rate, decay_coef):
    clipped = gradient * factor
    first_new = beta_one * first_old + (1.0 - beta_one) * clipped
    second_new = beta_two * second_old + (1.0 - beta_two) * clipped * clipped
    first_hat = first_new / (1.0 - beta_one**STEP)
    second_hat = second_new / (1.0 - beta_two**STEP)
    weight_new = weight - step_rate * (
        first_hat / (jnp.sqrt(second_hat) + adam_eps) + decay_coef * weight
    )
    return (weight_new, first_new, second_new)


def call(kernel, grid, ins, outs, args, scratch=(), prefetch=0):
    specs, flat, counts = [], list(args[:prefetch]), [1] * prefetch
    for (shape, index), arg in zip(ins, args[prefetch:]):
        if not isinstance(arg, list):
            specs.append(pl.BlockSpec(shape, index))
            flat.append(arg)
            counts.append(1)
            continue
        for array_in, start in arg:
            place = lambda *ids, at=start // shape, f=index: (0, f(ids[0]) + at)
            specs.append(pl.BlockSpec((array_in.shape[0], shape), place))
            flat.append(array_in)
        counts.append(-len(arg))

    def body(*refs):
        refs, grouped = list(refs), []
        for count in counts:
            grouped.append(refs.pop(0) if count > 0 else [refs.pop(0) for _ in range(-count)])
        kernel(*grouped, *refs)

    return pl.pallas_call(
        body,
        out_shape=[jax.ShapeDtypeStruct(o[2], o[3]) for o in outs],
        grid_spec=pltpu.PrefetchScalarGridSpec(
            num_scalar_prefetch=prefetch,
            grid=grid,
            in_specs=specs,
            out_specs=[pl.BlockSpec(o[0], o[1]) for o in outs],
            scratch_shapes=list(scratch),
        ),
        compiler_params=pltpu.CompilerParams(
            dimension_semantics=("arbitrary",) * len(grid), vmem_limit_bytes=56 << 20
        ),
        name=kernel.__name__,
    )(*flat)


def whole_weight(refs):
    pieces = [r[...] for r in refs]
    return pieces[0] if len(pieces) == 1 else jnp.concatenate(pieces, axis=0)


first_block = lambda i: 0
each_block = lambda i: i


def dot(a, b):
    return jnp.dot(a, b, preferred_element_type=f32)


def dot_t(a, b):
    return lax.dot_general(a, b, (((1,), (1,)), ((), ())), preferred_element_type=f32)


def t_dot(a, b):
    return lax.dot_general(a, b, (((0,), (0,)), ((), ())), preferred_element_type=f32)


def rms_factor(z):
    return lax.rsqrt(jnp.mean(z * z, axis=-1, keepdims=True) + norm_eps)


def rms_back(z, gain, grad):
    factor = rms_factor(z)
    scaled = grad * gain
    inner = jnp.mean(scaled * z, axis=-1, keepdims=True)
    return factor * scaled - z * (factor * factor * factor * inner), grad * z * factor


def lane_in_head(shape):
    return lax.broadcasted_iota(jnp.int32, shape, 1)


def rope(z, cos, sin, sign):
    lane = lane_in_head(z.shape)
    lead = lane % HEAD_DIM < HEAD_DIM // 2
    partner = jnp.where(lead, -pltpu.roll(z, PAIR - 32, 1), pltpu.roll(z, 32, 1))
    return z * cos + partner * (sin * sign)


def split_heads(z):
    first = lane_in_head(z.shape) < HEAD_DIM
    zero = jnp.zeros_like(z)
    return jnp.where(first, z, zero), jnp.where(first, zero, z)


def join_heads(a, b):
    return jnp.where(lane_in_head(a.shape) < HEAD_DIM, a, b)


def qkv_kernel(x_ref, g_ref, wq, wk, wv, cos_ref, sin_ref, n_ref, q_ref, k_ref, v_ref):
    rows, span = n_ref.shape[0], q_ref.shape[0]

    @pl.when(pl.program_id(0) == 0)
    def _():
        x = x_ref[...].astype(f32)
        n_ref[...] = to_low(x * rms_factor(x) * g_ref[...])

    normed, cos, sin = n_ref[...], cos_ref[...], sin_ref[...]

    def turned(raw, cos, sin):
        return jnp.concatenate(
            [
                to_low(rope(raw[:, c : c + PAIR], cos, sin, 1.0))
                for c in range(0, raw.shape[1], PAIR)
            ],
            axis=1,
        )

    k_ref[...] = turned(dot(normed, whole_weight(wk)), cos, sin)
    v_ref[...] = to_low(dot(normed, whole_weight(wv)))
    own = rows - span
    q_ref[...] = turned(dot(normed[own:], whole_weight(wq)), cos[own:], sin[own:])


def qkv_call(x_ext, gain, wq, wk, wv, cos, sin, span, width):
    rows, model = x_ext.shape
    fix = lambda i: (0, 0)
    col = lambda i: (0, i)
    return call(
        qkv_kernel,
        (width // CHUNK,),
        [
            ((rows, model), fix),
            ((1, model), fix),
            (CHUNK, each_block),
            (CHUNK, each_block),
            (CHUNK, each_block),
            ((rows, PAIR), fix),
            ((rows, PAIR), fix),
        ],
        [
            ((rows, model), fix, (rows, model), bf16),
            ((span, CHUNK), col, (span, width), bf16),
            ((rows, CHUNK), col, (rows, width), bf16),
            ((rows, CHUNK), col, (rows, width), bf16),
        ],
        (x_ext, gain, wq, wk, wv, cos, sin),
    )


def self_bias(segq_ref, segk_ref, bias_ref):
    keys, span = bias_ref.shape
    key_pos = lax.broadcasted_iota(jnp.int32, (keys, span), 0) - (keys - span)
    query_pos = lax.broadcasted_iota(jnp.int32, (keys, span), 1)
    ok = jnp.logical_and(key_pos <= query_pos, segk_ref[...] == segq_ref[...])
    bias_ref[...] = jnp.where(ok, 0.0, masked_fill)


def self_kernel(q_ref, k_ref, v_ref, segq_ref, segk_ref, wo, o_ref, lse_ref, part_ref, bias_ref):
    @pl.when(pl.program_id(0) == 0)
    def _():
        self_bias(segq_ref, segk_ref, bias_ref)
        part_ref[...] = jnp.zeros_like(part_ref)

    k, v, bias = k_ref[...], v_ref[...], bias_ref[...]
    outs, lses = [], []
    for qh in split_heads(q_ref[...] * score_scale):
        s = dot_t(k, qh) + bias
        top = jnp.max(s, axis=0, keepdims=True)
        e = jnp.exp(s - top)
        total = jnp.sum(e, axis=0, keepdims=True)
        lses.append(top + jnp.log(total))
        outs.append(t_dot(to_low(e * (1.0 / total)), v))
    o = to_low(join_heads(outs[0], outs[1]))
    o_ref[...] = o
    lse_ref[0] = jnp.concatenate(lses, axis=0)
    part_ref[...] += dot_t(o, whole_weight(wo))


def self_call(q, k, v, segq, segk, wo, model):
    span, width = q.shape
    keys = k.shape[0]
    pair = lambda p: (0, p)
    fix = lambda p: (0, 0)
    return call(
        self_kernel,
        (width // PAIR,),
        [
            ((span, PAIR), pair),
            ((keys, PAIR), pair),
            ((keys, PAIR), pair),
            ((1, span), fix),
            ((keys, 1), fix),
            (PAIR, each_block),
        ],
        [
            ((span, PAIR), pair, (span, width), bf16),
            ((1, 2, span), lambda p: (p, 0, 0), (width // PAIR, 2, span), f32),
            ((span, model), fix, (span, model), f32),
        ],
        (q, k, v, segq, segk, wo),
        scratch=[pltpu.VMEM((keys, span), f32)],
    )


def block_bias(len_ref, block):
    key = lax.broadcasted_iota(jnp.int32, (KEYS, PAIR), 0)
    limit = jnp.where(key < NEIGH_LEN, len_ref[block, 0], len_ref[block, 1])
    return jnp.where(key % NEIGH_LEN < limit, 0.0, masked_fill)


def tile_bias(len_ref, tile, tiles):
    if tile:
        return block_bias(len_ref, tile)
    first = lax.broadcasted_iota(jnp.int32, (KEYS, PAIR), 1) % BLOCK == 0
    lead = jnp.where(first, masked_fill, block_bias(len_ref, 0))
    last = jnp.where(first, block_bias(len_ref, tiles), masked_fill)
    return jnp.concatenate([lead, last], axis=0)


def stack_heads(z):
    return jnp.concatenate(split_heads(z), axis=0)


def merge_heads(z):
    return join_heads(z[:BLOCK], z[BLOCK:])


def tile_keys(ref, tile, tiles):
    own = ref[tile * KEYS : (tile + 1) * KEYS, :]
    if tile:
        return own
    return jnp.concatenate([own, ref[tiles * KEYS : (tiles + 1) * KEYS, :]], axis=0)


def cross_kernel(
    len_ref, x_ref, pa_ref, pb_ref, g_ref, wq, k_ref, v_ref, keep_ref, wo,
    h_ref, n_ref, q_ref, o_ref, lse_ref, part_ref, acc_ref,
):
    span = x_ref.shape[0]
    tiles = span // BLOCK

    @pl.when(pl.program_id(0) == 0)
    def _():
        h = x_ref[...].astype(f32) + (pa_ref[...] + pb_ref[...])
        h_ref[...] = h
        n_ref[...] = to_low(h * rms_factor(h) * g_ref[...])
        part_ref[...] = jnp.zeros_like(part_ref)

    turned = pltpu.roll(to_low(dot(n_ref[...], whole_weight(wq))).astype(f32), 1, 0)
    q = to_low(turned * score_scale)
    q_ref[...] = q
    for tile in range(tiles):
        rows = slice(tile * BLOCK, (tile + 1) * BLOCK)
        k, v = tile_keys(k_ref, tile, tiles), tile_keys(v_ref, tile, tiles)
        sc = dot_t(k, stack_heads(q[rows])) + tile_bias(len_ref, tile, tiles)
        top = jnp.max(sc, axis=0, keepdims=True)
        e = jnp.exp(sc - top)
        total = jnp.sum(e, axis=0, keepdims=True)
        lse_ref[0, tile : tile + 1, :] = top + jnp.log(total)
        acc_ref[rows, :] = merge_heads(t_dot(to_low(e * (1.0 / total)), v))
    o = to_low(pltpu.roll(acc_ref[...] * keep_ref[...], span - 1, 0))
    o_ref[...] = o
    part_ref[...] += dot_t(o, whole_weight(wo))


def cross_call(lens, x, pa, pb, gain, wq, wo, kv2, keep):
    span, model = x.shape
    keys, width = kv2.shape[0], kv2.shape[1] // 2
    pairs = width // PAIR
    pair = lambda p, *_: (0, p)
    fix = lambda p, *_: (0, 0)
    return call(
        cross_kernel,
        (pairs,),
        [
            ((span, model), fix),
            ((span, model), fix),
            ((span, model), fix),
            ((1, model), fix),
            (PAIR, each_block),
            ((keys, PAIR), pair),
            ((keys, PAIR), lambda p, *_: (0, pairs + p)),
            ((span, 1), fix),
            (PAIR, each_block),
        ],
        [
            ((span, model), fix, (span, model), f32),
            ((span, model), fix, (span, model), bf16),
            ((span, PAIR), pair, (span, width), bf16),
            ((span, PAIR), pair, (span, width), bf16),
            ((1, span // BLOCK, PAIR), lambda p, *_: (p, 0, 0), (pairs, span // BLOCK, PAIR), f32),
            ((span, model), fix, (span, model), f32),
        ],
        (lens, x, pa, pb, gain, wq, kv2, kv2, keep, wo),
        scratch=[pltpu.VMEM((span, PAIR), f32)],
        prefetch=1,
    )


def gelu_and_slope(u):
    t = jnp.tanh(gelu_c * (u + gelu_k * (u * u * u)))
    slope = 0.5 * (1.0 + t) + 0.5 * u * (1.0 - t * t) * (gelu_c * (1.0 + 3.0 * gelu_k * (u * u)))
    return to_low(0.5 * u * (1.0 + t)), slope


def norm_kernel(h1_ref, pa_ref, pb_ref, g_ref, turn_ref, h_ref, n_ref):
    h = h1_ref[...] + (pa_ref[...] + pb_ref[...])
    h_ref[...] = h
    n_ref[...] = to_low(dot_t(to_low(h * rms_factor(h) * g_ref[...]), turn_ref[...]))


def norm_call(h1, pa, pb, gain, turn):
    span, model = h1.shape
    row = lambda i: (i, 0)
    fix = lambda i: (0, 0)
    rows = span
    return call(
        norm_kernel,
        (1,),
        [((rows, model), row)] * 3 + [((1, model), fix), ((model, model), fix)],
        [
            ((rows, model), row, (span, model), f32),
            ((rows, model), row, (span, model), bf16),
        ],
        (h1, pa, pb, gain, turn),
    )


def feed_kernel(n_ref, cot_ref, up_ref, down_ref, act_ref, du_ref, ya_ref, yb_ref, da_ref, db_ref):
    up, down = up_ref[...], down_ref[...]
    act, slope = gelu_and_slope(dot(n_ref[...], up))
    du = to_low(dot(cot_ref[...], down) * slope)
    act_ref[...] = act
    du_ref[...] = du
    y, dn = dot_t(act, down), dot_t(du, up)
    step = pl.program_id(0)
    half = pl.num_programs(0) // 2

    @pl.when(step < half)
    def _():
        ya_ref[...] = to_low(y)
        da_ref[...] = dn

    @pl.when(step >= half)
    def _():
        yb_ref[...] = to_low(y)
        db_ref[...] = dn


def feed_call(n, cot, w_feed):
    rows, model = n.shape
    hidden = w_feed.shape[1] // 2
    half = rows // TOKENS // 2
    row = lambda i: (i, 0)
    lead = lambda i: (jnp.minimum(i, half - 1), 0)
    tail = lambda i: (jnp.maximum(i - half, 0), 0)
    block = (TOKENS, model)
    part = (rows // 2, model)
    return call(
        feed_kernel,
        (rows // TOKENS,),
        [
            (block, row),
            (block, row),
            ((model, hidden), lambda i: (0, 0)),
            ((model, hidden), lambda i: (0, 1)),
        ],
        [
            ((TOKENS, hidden), row, (rows, hidden), bf16),
            ((TOKENS, hidden), row, (rows, hidden), bf16),
            (block, lead, part, bf16),
            (block, tail, part, bf16),
            (block, lead, part, f32),
            (block, tail, part, f32),
        ],
        (n, cot, w_feed, w_feed),
    )


def cross_back_kernel(
    len_ref, core_ref, base_ref, h_ref, da_ref, db_ref, turn_ref, g_ref, wo, q_ref, k_ref, v_ref, lse_ref,
    keep_ref, wq,
    grad_ref, low_ref, gain_ref, dq_ref, dk_ref, dv_ref, dn_ref, acc_ref,
):
    span = h_ref.shape[0]
    tiles = span // BLOCK

    @pl.when(pl.program_id(0) == 0)
    def _():
        first, other = da_ref[...], db_ref[...]
        given = jnp.where(
            core_ref[0] == 0,
            jnp.concatenate([first, other], axis=0),
            jnp.concatenate([other, first], axis=0),
        )
        high = to_low(given)
        low = to_low(given - high.astype(f32))
        turn = turn_ref[...]
        back, gains = rms_back(h_ref[...], g_ref[...], dot(high, turn) + dot(low, turn))
        grad = base_ref[...].astype(f32) + back
        grad_ref[...] = grad
        low_ref[...] = to_low(grad)
        gain_ref[...] = jnp.sum(gains, axis=0, keepdims=True)
        dn_ref[...] = jnp.zeros_like(dn_ref)

    do = to_low(dot(low_ref[...], whole_weight(wo))).astype(f32)
    do = to_low(pltpu.roll(do, 1, 0) * keep_ref[...])
    q = q_ref[...]
    for tile in range(tiles):
        rows = slice(tile * BLOCK, (tile + 1) * BLOCK)
        k, v = tile_keys(k_ref, tile, tiles), tile_keys(v_ref, tile, tiles)
        qs, dos = stack_heads(q[rows]), stack_heads(do[rows])
        p = jnp.exp(dot_t(k, qs) + tile_bias(len_ref, tile, tiles) - lse_ref[0, tile : tile + 1, :])
        dp = dot_t(v, dos)
        ds = to_low(p * (dp - jnp.sum(p * dp, axis=0, keepdims=True)))
        acc_ref[rows, :] = merge_heads(t_dot(ds, k))
        dk = to_low(dot(ds, qs))
        dv = to_low(dot(to_low(p), dos))
        own = slice(tile * KEYS, (tile + 1) * KEYS)
        dk_ref[own, :] = dk[:KEYS]
        dv_ref[own, :] = dv[:KEYS]
        if not tile:
            last = slice(tiles * KEYS, (tiles + 1) * KEYS)
            dk_ref[last, :] = dk[KEYS:]
            dv_ref[last, :] = dv[KEYS:]
    dq = to_low(pltpu.roll(acc_ref[...] * score_scale, span - 1, 0))
    dq_ref[...] = dq
    dn_ref[...] += dot_t(dq, whole_weight(wq))


def cross_back_call(lens, core, base, h, da, db, turn, gain, wq, wo, q, kv2, lse, keep):
    span, model = h.shape
    keys, width = kv2.shape[0], kv2.shape[1] // 2
    pairs = width // PAIR
    pair = lambda p, *_: (0, p)
    fix = lambda p, *_: (0, 0)
    return call(
        cross_back_kernel,
        (pairs,),
        [
            ((span, model), fix),
            ((span, model), fix),
            ((span // 2, model), fix),
            ((span // 2, model), fix),
            ((model, model), fix),
            ((1, model), fix),
            (PAIR, each_block),
            ((span, PAIR), pair),
            ((keys, PAIR), pair),
            ((keys, PAIR), lambda p, *_: (0, pairs + p)),
            ((1, span // BLOCK, PAIR), lambda p, *_: (p, 0, 0)),
            ((span, 1), fix),
            (PAIR, each_block),
        ],
        [
            ((span, model), fix, (span, model), f32),
            ((span, model), fix, (span, model), bf16),
            ((1, model), fix, (1, model), f32),
            ((span, PAIR), pair, (span, width), bf16),
            ((keys, PAIR), pair, (keys, width), bf16),
            ((keys, PAIR), pair, (keys, width), bf16),
            ((span, model), fix, (span, model), f32),
        ],
        (lens, core, base, h, da, db, turn, gain, wo, q, kv2, kv2, lse, keep, wq),
        scratch=[pltpu.VMEM((span, PAIR), f32)],
        prefetch=2,
    )


def self_back_kernel(
    base_ref, h_ref, da_ref, db_ref, g_ref, wo, q_ref, k_ref, v_ref, lse_ref, segq_ref,
    segk_ref, cos_ref, sin_ref,
    grad_ref, low_ref, gain_ref, dq_ref, dk_ref, dv_ref, bias_ref,
):
    span = h_ref.shape[0]
    keys = k_ref.shape[0]

    @pl.when(pl.program_id(0) == 0)
    def _():
        back, gains = rms_back(h_ref[...], g_ref[...], da_ref[...] + db_ref[...])
        grad = base_ref[...] + back
        grad_ref[...] = grad
        low_ref[...] = to_low(grad)
        gain_ref[...] = jnp.sum(gains, axis=0, keepdims=True)
        self_bias(segq_ref, segk_ref, bias_ref)

    do = to_low(dot(low_ref[...], whole_weight(wo)))
    k, v, bias = k_ref[...], v_ref[...], bias_ref[...]
    qs, dos = split_heads(q_ref[...] * score_scale), split_heads(do)
    dqs, dk, dv = [], 0.0, 0.0
    for h in range(2):
        p = jnp.exp(dot_t(k, qs[h]) + bias - lse_ref[0, h : h + 1, :])
        dp = dot_t(v, dos[h])
        ds = to_low(p * (dp - jnp.sum(p * dp, axis=0, keepdims=True)))
        dqs.append(t_dot(ds, k))
        dk = dk + dot(ds, qs[h])
        dv = dv + dot(to_low(p), dos[h])
    cos, sin = cos_ref[...], sin_ref[...]
    dq = join_heads(dqs[0], dqs[1]) * score_scale
    dq_ref[...] = to_low(rope(dq, cos[keys - span :], sin[keys - span :], -1.0))
    dk_ref[...] = to_low(rope(dk, cos, sin, -1.0))
    dv_ref[...] = to_low(dv)


def self_back_call(base, h, da, db, gain, wo, q, k, v, lse, segq, segk, cos, sin):
    span, model = h.shape
    keys, width = k.shape
    pair = lambda p: (0, p)
    fix = lambda p: (0, 0)
    return call(
        self_back_kernel,
        (width // PAIR,),
        [
            ((span, model), fix),
            ((span, model), fix),
            ((span, model), fix),
            ((span, model), fix),
            ((1, model), fix),
            (PAIR, each_block),
            ((span, PAIR), pair),
            ((keys, PAIR), pair),
            ((keys, PAIR), pair),
            ((1, 2, span), lambda p: (p, 0, 0)),
            ((1, span), fix),
            ((keys, 1), fix),
            ((keys, PAIR), fix),
            ((keys, PAIR), fix),
        ],
        [
            ((span, model), fix, (span, model), f32),
            ((span, model), fix, (span, model), bf16),
            ((1, model), fix, (1, model), f32),
            ((span, PAIR), pair, (span, width), bf16),
            ((keys, PAIR), pair, (keys, width), bf16),
            ((keys, PAIR), pair, (keys, width), bf16),
        ],
        (base, h, da, db, gain, wo, q, k, v, lse, segq, segk, cos, sin),
        scratch=[pltpu.VMEM((keys, span), f32)],
    )


def inner_kernel(x_ref, dq_ref, dk_ref, dv_ref, wq, wk, wv, dn_ref, gain_ref):
    step = pl.program_id(0)
    rows, span = x_ref.shape[0], dq_ref.shape[0]
    own = rows - span
    dn = dot_t(dk_ref[...], whole_weight(wk)) + dot_t(dv_ref[...], whole_weight(wv))
    dn_own = dot_t(dq_ref[...], whole_weight(wq))

    @pl.when(step == 0)
    def _():
        dn_ref[...] = dn
        dn_ref[own:, :] += dn_own

    @pl.when(step > 0)
    def _():
        dn_ref[...] += dn
        dn_ref[own:, :] += dn_own

    @pl.when(step == pl.num_programs(0) - 1)
    def _():
        x = x_ref[...].astype(f32)
        gain_ref[...] = jnp.sum(dn_ref[...] * x * rms_factor(x), axis=0, keepdims=True)


def inner_call(x_ext, dq, dk, dv, wq, wk, wv):
    rows, model = x_ext.shape
    span, width = dq.shape
    fix = lambda i: (0, 0)
    col = lambda i: (0, i)
    return call(
        inner_kernel,
        (width // CHUNK,),
        [
            ((rows, model), fix),
            ((span, CHUNK), col),
            ((rows, CHUNK), col),
            ((rows, CHUNK), col),
            (CHUNK, each_block),
            (CHUNK, each_block),
            (CHUNK, each_block),
        ],
        [
            ((rows, model), fix, (rows, model), f32),
            ((1, model), fix, (1, model), f32),
        ],
        (x_ext, dq, dk, dv, wq, wk, wv),
    )


def adam_call(factor, weights, grads, first, second, order):
    count, rows, width = weights.shape

    def adam_kernel(factor_ref, w_ref, g_ref, m_ref, v_ref, wo_ref, mo_ref, vo_ref):
        for j, at in enumerate(order):
            wo_ref[j], mo_ref[j], vo_ref[j] = adam_step(
                w_ref[j],
                g_ref[:, at * width : (at + 1) * width],
                m_ref[j],
                v_ref[j],
                factor_ref[0],
                learn_rate,
                weight_decay,
            )

    block = (weights.shape, lambda i, *_: (0, 0, 0))
    return call(
        adam_kernel,
        (1,),
        [block, (grads.shape, lambda i, *_: (0, 0)), block, block],
        [block + (weights.shape, f32)] * 3,
        (factor, weights, grads, first, second),
        prefetch=1,
    )


def half_sum_kernel(ka, ga, kb, gb, keep_a, keep_b, sent_a, sent_b):
    step = pl.program_id(0)
    sum_a = to_low(ka[...].astype(f32) + ga[...].astype(f32))
    sum_b = to_low(kb[...].astype(f32) + gb[...].astype(f32))

    @pl.when(step == 0)
    def _():
        sent_a[...] = sum_a
        sent_b[...] = sum_b

    @pl.when(step == 1)
    def _():
        keep_a[...] = sum_a
        keep_b[...] = sum_b


def half_sum_call(kept, got):
    rows, (wide_a, wide_b) = kept[0].shape[0] // 2, (k.shape[1] for k in kept)
    turn = lambda i: (1 - i, 0)
    fix = lambda i: (0, 0)
    a, b = (rows, wide_a), (rows, wide_b)
    return call(
        half_sum_kernel,
        (2,),
        [(a, turn), (a, turn), (b, turn), (b, turn)],
        [(a, fix, a, bf16), (b, fix, b, bf16), (a, fix, a, bf16), (b, fix, b, bf16)],
        (kept[0], got[0], kept[1], got[1]),
    )


def rows_kernel(a_ref, w, o_ref):
    o_ref[...] = to_low(dot(a_ref[...], whole_weight(w)))


def rows_call(a, w, width):
    rows, model = a.shape
    block = CHUNK if width % CHUNK == 0 else width // 7 if width % 7 == 0 else width
    return call(
        rows_kernel,
        (width // block,),
        [((rows, model), lambda i: (0, 0)), (block, each_block)],
        [((rows, block), lambda i: (0, i), (rows, width), bf16)],
        (a, w),
    )[0]


def turn_call(a, turn):
    rows, model = a.shape
    return call(
        turn_kernel,
        (rows // KEYS,),
        [((KEYS, model), lambda i: (i, 0)), ((model, model), lambda i: (0, 0))],
        [((KEYS, model), lambda i: (i, 0), (rows, model), bf16)],
        (a, turn),
    )[0]


def turn_kernel(a_ref, t_ref, o_ref):
    o_ref[...] = to_low(dot(a_ref[...], t_ref[...]))


def per_device(
    tokens,
    neighbours,
    neighbour_lengths,
    segment_ids,
    out_grad,
    self_weights,
    cross_weights,
    feed_weights,
    norm_gains,
    self_first,
    cross_first,
    feed_first,
    gains_first,
    self_second,
    cross_second,
    feed_second,
    gains_second,
):
    row_count, span, model = tokens.shape
    width = self_weights.shape[2]
    hidden = feed_weights.shape[2]
    shard_rows = self_weights.shape[1]
    pairs = width // PAIR
    blocks = span // BLOCK
    halo = min(-(-(DOC_MAX - 1) // span), lax.axis_size("seq") - 1)
    s_index = lax.axis_index("seq")
    core = lax.axis_index("mp")

    def columns(*parts):
        return jnp.concatenate([to_low(p) for p in parts], axis=1)

    gain_cols = jnp.zeros((shard_rows, PAIR), f32).at[:, :3].set(norm_gains.T)
    block_q = columns(self_weights[0], self_weights[1], self_weights[2], gain_cols)
    small = small_mesh()
    x_own, cot = tokens.reshape(span, model), out_grad.reshape(span, model)
    flat_own = neighbours.reshape(-1, model)
    half, pad = span // 2, KEYS // 2
    seg_here = segment_ids.reshape(1, span) + 1
    lengths = neighbour_lengths.reshape(blocks, NEIGHBOURS)
    ints = jnp.concatenate([seg_here[0], lengths[-1]]).astype(bf16)
    ints = jnp.zeros((8, model), bf16).at[0, : span + NEIGHBOURS].set(ints)
    mine = lax.dynamic_slice_in_dim(x_own, core * half, half, 0)
    edge = lax.dynamic_slice_in_dim(flat_own, flat_own.shape[0] - KEYS + core * pad, pad, 0)
    frequency = rope_base ** (-(jnp.arange(PAIR) % (HEAD_DIM // 2)).astype(f32) / (HEAD_DIM // 2))
    places = (s_index - halo) * span + jnp.arange((halo + 1) * span)
    angles = places.astype(f32)[:, None] * frequency[None, :]

    plane = lax.axis_size("seq")
    groups = hidden // PAIR
    wide = -(-groups // plane) * PAIR
    spans = [(groups + plane - 1 - k) // plane * PAIR for k in range(plane)]
    firsts = [sum(spans[:k]) for k in range(plane)]

    def share_of(matrix, k):
        return jnp.pad(
            matrix[:, firsts[k] : firsts[k] + spans[k]], ((0, 0), (0, wide - spans[k]))
        )

    near = shifted(jnp.concatenate([mine, edge, ints], axis=0), "seq", 1)
    far = [shifted(jnp.concatenate([mine, ints], axis=0), "seq", k) for k in range(2, halo + 1)]
    low_f = to_low(feed_weights)
    block_f = jnp.concatenate(
        [
            jnp.concatenate([share_of(low_f[0], k), share_of(low_f[1], k)], axis=1)
            for k in range(plane)
        ],
        axis=0,
    )
    block_c = columns(
        cross_weights[1], cross_weights[2], self_weights[3], cross_weights[0], cross_weights[3]
    )
    if small:
        col_q = exchanged(wide_for_dp(block_q), "dp")
        spots = [s_index ^ k for k in range(plane)]
        shares = block_f.reshape(plane, shard_rows, 2 * wide)
        shares = [take(shares, spot, 0) for spot in spots]
        shares = shares[:1] + [swapped(shares[k], "seq", k) for k in range(1, plane)]
        col_q, near, block_c, angles, s_index, *rest = meet(
            col_q, near, block_c, angles, s_index, *shares, *far
        )
        shares, far = rest[:plane], rest[plane:]
        xy_q = from_seq(col_q)
    cos, sin = jnp.cos(angles), jnp.sin(angles)
    if small:
        turn = own_order(model, s_index)
        col_c = lax.all_gather(block_c, "dp", axis=0, tiled=True)
        cot_turned = turn_call(cot, turn)
    else:
        turn = jnp.eye(model, dtype=bf16)
        cot_turned = cot
    got = jnp.concatenate([near[: half + pad]] + [f[:half] for f in far], axis=0)
    other = swapped(got, "mp", 1)
    low_half = jnp.where(core == 0, got, other)
    high_half = jnp.where(core == 0, other, got)

    def whole(start, size):
        return [low_half[start : start + size], high_half[start : start + size]]

    pieces = []
    for k in range(halo, 1, -1):
        pieces += whole(half + pad + (k - 2) * half, half)
    x_ext = jnp.concatenate(pieces + whole(0, half) + [x_own], axis=0)
    flat_ext = jnp.concatenate(whole(half, pad) + [flat_own], axis=0)
    ints_prev = [near[half + pad]] + [f[half] for f in far]
    ints_prev = [p[None, : span + NEIGHBOURS].astype(jnp.int32) for p in ints_prev]
    seg_keys = jnp.concatenate([p[:, :span] for p in ints_prev[::-1]] + [seg_here], axis=1)
    seg_keys = seg_keys.reshape(-1, 1)
    lens = jnp.concatenate([ints_prev[0][:, span:], lengths], axis=0)
    before = jnp.concatenate([ints_prev[0][0, span - 1 : span], seg_here[0, : span - 1]])
    heads_of = jnp.repeat(before[::BLOCK], BLOCK)
    spot = jnp.arange(span)
    starts = jnp.where(s_index == 0, BLOCK, 0)
    keep = jnp.logical_or(spot == 0, jnp.logical_and(before == heads_of, spot >= starts))
    keep = keep.astype(f32).reshape(span, 1)

    if small:
        w_feed = jnp.broadcast_to(shares[0], (plane, shard_rows, 2 * wide))
        for spot, piece in zip(spots[1:], shares[1:]):
            w_feed = put(w_feed, piece[None], (spot, 0, 0))
        w_feed = w_feed.reshape(plane * shard_rows, 2 * wide)
        x_ext = turn_call(x_ext, turn)
        w_feed = lax.all_gather(w_feed, "dp", axis=0, tiled=True)
        col_c, turn, cot_turned, cos, sin, x_ext, flat_ext, cot, *xy_q = meet(
            col_c, turn, cot_turned, cos, sin, x_ext, flat_ext, cot, *xy_q
        )
        lead = 3 * width
        lead_c = from_seq(col_c[:, :lead])
        flat_ext = turn_call(flat_ext, turn)
        q_pieces = [col_q] + xy_q
        s_q, s_k, s_v = (weight(q_pieces, j * width) for j in range(3))
        gain_rows = jnp.concatenate(
            [p[:, 3 * width : 3 * width + PAIR] for p in q_pieces], axis=0
        )
    else:
        full_q, full_c = (
            lax.all_gather(b, ("dp", "seq"), axis=0, tiled=True) for b in (block_q, block_c)
        )
        w_feed = lax.all_to_all(block_f, "seq", 0, 0, tiled=True)
        w_feed = lax.all_gather(w_feed, "dp", axis=0, tiled=True)
        s_q, s_k, s_v = ([(full_q, j * width)] for j in range(3))
        gain_rows = full_q[:, 3 * width :]
        c_kv, s_o, c_q, c_o = ([(full_c, j * width)] for j in (0, 2, 3, 4))
    gains = gain_rows[:, :3].T.astype(f32)
    x = x_ext[halo * span :]
    n1, q, k, v = qkv_call(x_ext, gains[:1], s_q, s_k, s_v, cos, sin, span, width)
    if small:
        rest_c = col_c[:, lead:]
        q, flat_ext, seg_keys, lens, keep, cot, rest_c, *lead_c = meet(
            q, flat_ext, seg_keys, lens, keep, cot, rest_c, *lead_c
        )
        tail_c = from_seq(rest_c)
        c_kv, s_o = (weight([col_c] + lead_c, j * width) for j in (0, 2))
    def over_plane(rows):
        own = lax.dynamic_slice_in_dim(rows, core * half, half, 0)
        return [own] + [swapped(own, "seq", k) for k in range(1, plane)]

    def with_other(pieces):
        got = jnp.concatenate(pieces, axis=0)
        return jnp.concatenate([got, swapped(got, "mp", 1)], axis=0)

    def back_to_owner(own, other):
        total = own.astype(f32) + swapped(other, "mp", 1).astype(f32)
        sent = to_low(total)
        return [total[:half]] + [
            swapped(sent[k * half : (k + 1) * half], "seq", k) for k in range(1, plane)
        ]

    def f_assembled(got):
        got = got.reshape(plane, shard_rows, 2 * wide)
        return jnp.concatenate(
            [got[k, :, at : at + spans[k]] for at in (0, wide) for k in range(plane)], axis=1
        ).astype(f32)

    cot_rows = over_plane(cot)
    attn, lse, part = self_call(q, k, v, seg_here, seg_keys, s_o, model)
    kv2 = rows_call(flat_ext, c_kv, 2 * width)
    if small:
        part, kv2, *rest = meet(part, kv2, *tail_c, *cot_rows)
        tail_c, cot_rows = rest[:3], rest[3:]
        c_q, c_o = (weight([rest_c] + tail_c, j * width) for j in (0, 1))
    cot_rows = with_other(cot_rows)
    other = swapped(part, "mp", 1)
    if small:
        other, cot_rows = meet(other, cot_rows)
    h1, n2, q2, cross, lse2, part2 = cross_call(
        lens, x, part, other, gains[1:2], c_q, c_o, kv2, keep
    )
    other = swapped(part2, "mp", 1)
    h2, n3 = norm_call(h1, part2, other, gains[2:3], turn)

    n_rows = with_other(over_plane(n3))
    act, du, y_own, y_other, dn_own, dn_other = feed_call(n_rows, cot_rows, w_feed)
    dn3 = plane_sum(back_to_owner(dn_own, dn_other))
    dn3_other = swapped(dn3, "mp", 1)
    g2, low2, dgain3, dq2, dk2, dv2, dn2 = cross_back_call(
        lens, core.reshape(1), cot_turned, h2, dn3, dn3_other, turn, gains[2:3], c_q, c_o,
        q2, kv2, lse2, keep,
    )
    other = swapped(dn2, "mp", 1)
    cross_sent, cross_kept = halves(
        [(n2, dq2), (low2, cross)], [(flat_ext, dk2), (flat_ext, dv2)]
    )
    if small:
        *cross_sent, other, du, act = meet(*cross_sent, other, du, act)
        cross_got = reduce_first(cross_sent)
    g1, low1, dgain2, dq, dk, dv = self_back_call(
        g2, h1, dn2, other, gains[1:2], s_o, q, k, v, lse, seg_here, seg_keys, cos, sin
    )
    if small:
        *cross_got, low1, dq, dk, dv = meet(*cross_got, low1, dq, dk, dv)
        cross_kept, cross_got = reduce_second(cross_kept, cross_got)
    dn1, dgain1 = inner_call(x_ext, dq, dk, dv, s_q, s_k, s_v)
    dgain1 = core_sum(dgain1)
    dgains = jnp.concatenate(
        [dgain1, dgain2, dgain3, jnp.zeros((PAIR - 3, model), f32)], axis=0
    )
    self_sent, self_kept = halves(
        [(n1[halo * span :], dq), (low1, attn)],
        [(n1, dk), (n1, dv), (to_low(dgains), jnp.eye(PAIR, dtype=bf16))],
    )
    if small:
        sent_a, sent_b, got_a, got_b = meet(*self_sent, *cross_got)
        du, act, _ = meet(du, act, token_of(sent_a))
        self_got = reduce_first((sent_a, sent_b))
        cross_part = lax.psum_scatter(
            last_sum(cross_kept, (got_a, got_b)), "dp", scatter_dimension=0, tiled=True
        ).astype(f32)
        feed_grads = jnp.concatenate(
            [to_low(t_dot(n_rows, du)), to_low(t_dot(cot_rows, act))], axis=1
        )
        feed_low = lax.psum_scatter(feed_grads, "dp", scatter_dimension=0, tiled=True)
        *self_got, _ = meet(*self_got, token_of(feed_grads))
        self_kept, self_got = reduce_second(self_kept, self_got)
        got_a, got_b, dn1, y_own, y_other = meet(*self_got, dn1, y_own, y_other)
        self_got = exchanged(last_sum(self_kept, (got_a, got_b)), "dp")
    y_sums = back_to_owner(y_own, y_other)
    own = dn1[halo * span :]
    if halo:
        view = dn1[: halo * span].reshape(halo, 2, half, model)
        summed = to_low(take(view, core, 1) + swapped(take(view, 1 - core, 1), "mp", 1))
        if small:
            summed = to_low(dot_t(summed.reshape(-1, model), turn)).reshape(halo, half, model)
    back_parts = [shifted(summed[halo - k], "seq", -k) for k in range(1, halo + 1)]
    if small:
        squares = jnp.sum(cross_part * cross_part) + jnp.sum(jnp.square(feed_low.astype(f32)))
        self_part = reduce_last(self_got)
    else:
        feed_grads = jnp.concatenate(
            [to_low(t_dot(n_rows, du)), to_low(t_dot(cot_rows, act))], axis=1
        )
        feed_low = lax.psum_scatter(feed_grads, "dp", scatter_dimension=0, tiled=True)
        feed_part = f_assembled(exchanged(feed_low, "seq"))
        cross_part, self_part = reduce_plain(cross_kept), reduce_plain(self_kept)
        squares = jnp.sum(feed_part * feed_part) + jnp.sum(cross_part * cross_part)
    gains_part = self_part[:, 4 * width : 4 * width + 3].T
    first_model = (core == 0).astype(f32)
    local_squares = (
        jnp.sum(jnp.square(self_part[:, : 4 * width]))
        + squares
        + first_model * jnp.sum(gains_part * gains_part)
    )
    local_squares = local_squares.reshape(1, 1)
    if small:
        shares = [take(feed_low.reshape(plane, shard_rows, 2 * wide), spot, 0) for spot in spots]
        local_squares, *rest = meet(local_squares, *y_sums, *back_parts, *shares)
        y_sums, back_parts, shares = rest[:plane], rest[plane:-plane], rest[-plane:]
        shares = shares[:1] + [swapped(shares[k], "seq", k) for k in range(1, plane)]
        feed_got = jnp.zeros((plane, shard_rows, 2 * wide), bf16)
        for spot, piece in zip(spots, shares):
            feed_got = put(feed_got, piece[None], (spot, 0, 0))
        feed_part = f_assembled(feed_got)
    grad_norm = jnp.sqrt(sum_everywhere(local_squares).reshape(()))
    factor = jnp.minimum(1.0, clip_limit / (grad_norm + 1e-06))
    scalar = factor.reshape(1)
    mixed_order, plain = (0, 2, 3, 1), (0, 1)
    y_half = plane_sum(y_sums)
    y_other = swapped(y_half, "mp", 1)
    y_all = jnp.concatenate(
        [jnp.where(core == 0, y_half, y_other), jnp.where(core == 0, y_other, y_half)], axis=0
    )
    if halo:
        back = sum(p.astype(f32) for p in back_parts)
        if small:
            back = dot(to_low(back), turn)
        own = own + put(jnp.zeros_like(own), back, (core * half, 0))
    back, _ = rms_back(x.astype(f32), gains[:1], core_sum(own))
    in_grad = g1 + back

    def in_model_order(rows):
        high = to_low(lax.reduce_precision(rows, 8, 7))
        rest = rows - high.astype(f32)
        mid = to_low(lax.reduce_precision(rest, 8, 7))
        low = to_low(rest - mid.astype(f32))
        return dot_t(high, turn) + (dot_t(mid, turn) + dot_t(low, turn))

    if small:
        in_grad = in_model_order(in_grad)
        result = to_low(in_model_order(h2) + y_all)
    else:
        result = to_low(h2 + y_all)
    in_grad = in_grad.reshape(row_count, span, model)
    out = result.reshape(row_count, span, model)
    self_new, self_first_new, self_second_new = adam_call(
        scalar, self_weights, self_part, self_first, self_second, mixed_order
    )
    cross_new, cross_first_new, cross_second_new = adam_call(
        scalar, cross_weights, cross_part, cross_first, cross_second, mixed_order
    )
    feed_new, feed_first_new, feed_second_new = adam_call(
        scalar, feed_weights, feed_part, feed_first, feed_second, plain
    )
    gains_new, gains_first_new, gains_second_new = adam_step(
        norm_gains, gains_part, gains_first, gains_second, factor, gain_rate, 0.0
    )
    return (
        out,
        in_grad,
        grad_norm,
        self_new,
        cross_new,
        feed_new,
        gains_new,
        self_first_new,
        cross_first_new,
        feed_first_new,
        gains_first_new,
        self_second_new,
        cross_second_new,
        feed_second_new,
        gains_second_new,
    )


def solution(mesh):
    tok = P("dp", "seq", None)
    mat = P(None, ("dp", "seq"), "mp")
    vec = P(None, ("dp", "seq"))
    in_specs = (
        tok,
        P("dp", "seq", None, None, None),
        tok,
        P("dp", "seq"),
        tok,
    ) + (mat, mat, mat, vec) * 3
    out_specs = (tok, tok, P()) + (mat, mat, mat, vec) * 3
    return jax.shard_map(
        per_device, mesh=mesh, in_specs=in_specs, out_specs=out_specs, check_vma=False
    )
```

```python
import jax
import jax.numpy as jnp
from jax import lax
from jax.experimental import pallas as pl
from jax.experimental.pallas import tpu as pltpu
from jax.sharding import PartitionSpec as P

HEAD_DIM = 64
PAIR = 128
BLOCK = 64
NEIGHBOURS = 2
NEIGH_LEN = 128
KEYS = NEIGHBOURS * NEIGH_LEN
STEP = 10
DOC_MAX = 512
CHUNK = 256
TOKENS = 512

norm_eps = 1e-05
rope_base = 10000.0
beta_one = 0.9
beta_two = 0.95
adam_eps = 1e-08
weight_decay = 0.1
learn_rate = 0.1
gain_rate = 0.5
clip_limit = 1.0
masked_fill = -1e30
score_scale = HEAD_DIM ** (-0.5)
gelu_c = 0.7978845608028654
gelu_k = 0.044715

f32 = jnp.float32
bf16 = jnp.bfloat16


def to_low(array_in):
    return array_in.astype(bf16)


def shifted(value, axis, by):
    count = lax.axis_size(axis)
    return lax.ppermute(value, axis, [(i, i + by) for i in range(count) if 0 <= i + by < count])


def rotated(value, axis, by):
    count = lax.axis_size(axis)
    return lax.ppermute(value, axis, [(i, (i + by) % count) for i in range(count)])


def swapped(value, axis, by):
    count = lax.axis_size(axis)
    return lax.ppermute(value, axis, [(i, i ^ by) for i in range(count)])


def butterfly(value, axes):
    for axis in axes:
        step = 1
        while step < lax.axis_size(axis):
            value = value + swapped(value, axis, step)
            step *= 2
    return value


def sum_everywhere(value):
    axes = ("dp", "seq", "mp")
    if not small_mesh():
        return butterfly(value, axes)
    count = lax.axis_size("dp") * lax.axis_size("seq") * lax.axis_size("mp")
    spread = jnp.broadcast_to(value, (count, 8, PAIR))
    return jnp.sum(lax.all_to_all(spread, axes, 0, 0, tiled=True)[:, :1, :1], axis=0)


def core_sum(partial_out):
    return partial_out + swapped(partial_out, "mp", 1)


def small_mesh():
    return lax.axis_size("dp") == 4 and lax.axis_size("seq") == 4


def put(buffer, piece, starts):
    return lax.dynamic_update_slice(buffer, piece, starts)


def meet(*values):
    return lax.optimization_barrier(values)


ORDER = (0, 2, 1, 3)


def own_order(model, s):
    rows = model // 16
    spot = jnp.arange(model)
    near, z, inner = spot // (4 * rows), spot // rows % 4, spot % rows
    flip = (near % 2) * 2 + near // 2
    source = (z * 4 + (s ^ flip)) * rows + inner
    return (spot[:, None] == source[None, :]).astype(bf16)


def plane_sum(pieces):
    return (pieces[0] + pieces[1].astype(f32)) + (pieces[2].astype(f32) + pieces[3].astype(f32))


def take(array_in, index, axis):
    return lax.dynamic_index_in_dim(array_in, index, axis, keepdims=False)


def wide_for_dp(block):
    rows, cols = block.shape
    return jnp.broadcast_to(block[None], (4, rows, cols)).reshape(4 * rows, cols)


def exchanged(array_in, axis):
    return lax.all_to_all(array_in, axis, 0, 0, tiled=True)


def from_seq(column):
    return [swapped(column, "seq", k) for k in ORDER[1:]]


def weight(pieces, start):
    return [(p, start) for p in pieces]


def reduce_first(sent):
    return swapped(sent[0], "seq", 1), swapped(sent[1], "seq", 2)


def reduce_second(kept, got):
    keep_a, keep_b, sent_a, sent_b = half_sum_call(kept, got)
    return (keep_a, keep_b), (swapped(sent_a, "seq", 2), swapped(sent_b, "seq", 1))


def reduce_last(got):
    rows, cols = got.shape
    return jnp.sum(got.reshape(4, rows // 4, cols).astype(f32), axis=0)


def reduce_plain(grads):
    return lax.psum_scatter(
        jnp.concatenate(grads, axis=1), ("dp", "seq"), scatter_dimension=0, tiled=True
    ).astype(f32)


def halves(left, right):
    if not small_mesh():
        return None, [jnp.concatenate([to_low(t_dot(a, b)) for a, b in left + right], axis=1)]

    def products(pairs, pick):
        parts = [to_low(t_dot(pick(a), b)) for a, b in pairs]
        return parts[0] if len(parts) == 1 else jnp.concatenate(parts, axis=1)

    def second(a, first):
        quarter = a.shape[1] // 4
        return jnp.concatenate(
            [
                a[:, first * quarter : (first + 1) * quarter],
                a[:, (first + 2) * quarter : (first + 3) * quarter],
            ],
            axis=1,
        )

    mid = left[0][0].shape[1] // 2
    sent = (products(left, lambda a: a[:, mid:]), products(right, lambda a: second(a, 1)))
    kept = (products(left, lambda a: a[:, :mid]), products(right, lambda a: second(a, 0)))
    return sent, kept


def adam_step(weight, gradient, first_old, second_old, factor, step_rate, decay_coef):
    clipped = gradient * factor
    first_new = beta_one * first_old + (1.0 - beta_one) * clipped
    second_new = beta_two * second_old + (1.0 - beta_two) * clipped * clipped
    first_hat = first_new / (1.0 - beta_one**STEP)
    second_hat = second_new / (1.0 - beta_two**STEP)
    weight_new = weight - step_rate * (
        first_hat / (jnp.sqrt(second_hat) + adam_eps) + decay_coef * weight
    )
    return (weight_new, first_new, second_new)


def call(kernel, grid, ins, outs, args, scratch=(), prefetch=0):
    specs, flat, counts = [], list(args[:prefetch]), [1] * prefetch
    for (shape, index), arg in zip(ins, args[prefetch:]):
        if not isinstance(arg, list):
            specs.append(pl.BlockSpec(shape, index))
            flat.append(arg)
            counts.append(1)
            continue
        for array_in, start in arg:
            place = lambda *ids, at=start // shape, f=index: (0, f(ids[0]) + at)
            specs.append(pl.BlockSpec((array_in.shape[0], shape), place))
            flat.append(array_in)
        counts.append(-len(arg))

    def body(*refs):
        refs, grouped = list(refs), []
        for count in counts:
            grouped.append(refs.pop(0) if count > 0 else [refs.pop(0) for _ in range(-count)])
        kernel(*grouped, *refs)

    return pl.pallas_call(
        body,
        out_shape=[jax.ShapeDtypeStruct(o[2], o[3]) for o in outs],
        grid_spec=pltpu.PrefetchScalarGridSpec(
            num_scalar_prefetch=prefetch,
            grid=grid,
            in_specs=specs,
            out_specs=[pl.BlockSpec(o[0], o[1]) for o in outs],
            scratch_shapes=list(scratch),
        ),
        compiler_params=pltpu.CompilerParams(
            dimension_semantics=("arbitrary",) * len(grid), vmem_limit_bytes=56 << 20
        ),
        name=kernel.__name__,
    )(*flat)


def whole_weight(refs):
    pieces = [r[...] for r in refs]
    return pieces[0] if len(pieces) == 1 else jnp.concatenate(pieces, axis=0)


first_block = lambda i: 0
each_block = lambda i: i


def dot(a, b):
    return jnp.dot(a, b, preferred_element_type=f32)


def dot_t(a, b):
    return lax.dot_general(a, b, (((1,), (1,)), ((), ())), preferred_element_type=f32)


def t_dot(a, b):
    return lax.dot_general(a, b, (((0,), (0,)), ((), ())), preferred_element_type=f32)


def rms_factor(z):
    return lax.rsqrt(jnp.mean(z * z, axis=-1, keepdims=True) + norm_eps)


def rms_back(z, gain, grad):
    factor = rms_factor(z)
    scaled = grad * gain
    inner = jnp.mean(scaled * z, axis=-1, keepdims=True)
    return factor * scaled - z * (factor * factor * factor * inner), grad * z * factor


def lane_in_head(shape):
    return lax.broadcasted_iota(jnp.int32, shape, 1)


def rope(z, cos, sin, sign):
    lane = lane_in_head(z.shape)
    lead = lane % HEAD_DIM < HEAD_DIM // 2
    partner = jnp.where(lead, -pltpu.roll(z, PAIR - 32, 1), pltpu.roll(z, 32, 1))
    return z * cos + partner * (sin * sign)


def split_heads(z):
    first = lane_in_head(z.shape) < HEAD_DIM
    zero = jnp.zeros_like(z)
    return jnp.where(first, z, zero), jnp.where(first, zero, z)


def join_heads(a, b):
    return jnp.where(lane_in_head(a.shape) < HEAD_DIM, a, b)


def qkv_kernel(x_ref, g_ref, wq, wk, wv, cos_ref, sin_ref, n_ref, q_ref, k_ref, v_ref):
    rows, span = n_ref.shape[0], q_ref.shape[0]

    @pl.when(pl.program_id(0) == 0)
    def _():
        x = x_ref[...].astype(f32)
        n_ref[...] = to_low(x * rms_factor(x) * g_ref[...])

    normed, cos, sin = n_ref[...], cos_ref[...], sin_ref[...]

    def turned(raw, cos, sin):
        return jnp.concatenate(
            [
                to_low(rope(raw[:, c : c + PAIR], cos, sin, 1.0))
                for c in range(0, raw.shape[1], PAIR)
            ],
            axis=1,
        )

    k_ref[...] = turned(dot(normed, whole_weight(wk)), cos, sin)
    v_ref[...] = to_low(dot(normed, whole_weight(wv)))
    own = rows - span
    q_ref[...] = turned(dot(normed[own:], whole_weight(wq)), cos[own:], sin[own:])


def qkv_call(x_ext, gain, wq, wk, wv, cos, sin, span, width):
    rows, model = x_ext.shape
    fix = lambda i: (0, 0)
    col = lambda i: (0, i)
    return call(
        qkv_kernel,
        (width // CHUNK,),
        [
            ((rows, model), fix),
            ((1, model), fix),
            (CHUNK, each_block),
            (CHUNK, each_block),
            (CHUNK, each_block),
            ((rows, PAIR), fix),
            ((rows, PAIR), fix),
        ],
        [
            ((rows, model), fix, (rows, model), bf16),
            ((span, CHUNK), col, (span, width), bf16),
            ((rows, CHUNK), col, (rows, width), bf16),
            ((rows, CHUNK), col, (rows, width), bf16),
        ],
        (x_ext, gain, wq, wk, wv, cos, sin),
    )


def self_bias(segq_ref, segk_ref, bias_ref):
    keys, span = bias_ref.shape
    key_pos = lax.broadcasted_iota(jnp.int32, (keys, span), 0) - (keys - span)
    query_pos = lax.broadcasted_iota(jnp.int32, (keys, span), 1)
    ok = jnp.logical_and(key_pos <= query_pos, segk_ref[...] == segq_ref[...])
    bias_ref[...] = jnp.where(ok, 0.0, masked_fill)


def self_kernel(q_ref, k_ref, v_ref, segq_ref, segk_ref, wo, o_ref, lse_ref, part_ref, bias_ref):
    @pl.when(pl.program_id(0) == 0)
    def _():
        self_bias(segq_ref, segk_ref, bias_ref)
        part_ref[...] = jnp.zeros_like(part_ref)

    k, v, bias = k_ref[...], v_ref[...], bias_ref[...]
    outs, lses = [], []
    for qh in split_heads(q_ref[...] * score_scale):
        s = dot_t(k, qh) + bias
        top = jnp.max(s, axis=0, keepdims=True)
        e = jnp.exp(s - top)
        total = jnp.sum(e, axis=0, keepdims=True)
        lses.append(top + jnp.log(total))
        outs.append(t_dot(to_low(e * (1.0 / total)), v))
    o = to_low(join_heads(outs[0], outs[1]))
    o_ref[...] = o
    lse_ref[0] = jnp.concatenate(lses, axis=0)
    part_ref[...] += dot_t(o, whole_weight(wo))


def self_call(q, k, v, segq, segk, wo, model):
    span, width = q.shape
    keys = k.shape[0]
    pair = lambda p: (0, p)
    fix = lambda p: (0, 0)
    return call(
        self_kernel,
        (width // PAIR,),
        [
            ((span, PAIR), pair),
            ((keys, PAIR), pair),
            ((keys, PAIR), pair),
            ((1, span), fix),
            ((keys, 1), fix),
            (PAIR, each_block),
        ],
        [
            ((span, PAIR), pair, (span, width), bf16),
            ((1, 2, span), lambda p: (p, 0, 0), (width // PAIR, 2, span), f32),
            ((span, model), fix, (span, model), f32),
        ],
        (q, k, v, segq, segk, wo),
        scratch=[pltpu.VMEM((keys, span), f32)],
    )


def block_bias(len_ref, block):
    key = lax.broadcasted_iota(jnp.int32, (KEYS, PAIR), 0)
    limit = jnp.where(key < NEIGH_LEN, len_ref[block, 0], len_ref[block, 1])
    return jnp.where(key % NEIGH_LEN < limit, 0.0, masked_fill)


def tile_bias(len_ref, tile, tiles):
    if tile:
        return block_bias(len_ref, tile)
    first = lax.broadcasted_iota(jnp.int32, (KEYS, PAIR), 1) % BLOCK == 0
    lead = jnp.where(first, masked_fill, block_bias(len_ref, 0))
    last = jnp.where(first, block_bias(len_ref, tiles), masked_fill)
    return jnp.concatenate([lead, last], axis=0)


def stack_heads(z):
    return jnp.concatenate(split_heads(z), axis=0)


def merge_heads(z):
    return join_heads(z[:BLOCK], z[BLOCK:])


def tile_keys(ref, tile, tiles):
    own = ref[tile * KEYS : (tile + 1) * KEYS, :]
    if tile:
        return own
    return jnp.concatenate([own, ref[tiles * KEYS : (tiles + 1) * KEYS, :]], axis=0)


def cross_kernel(
    len_ref, x_ref, pa_ref, pb_ref, g_ref, wq, k_ref, v_ref, keep_ref, wo,
    h_ref, n_ref, q_ref, o_ref, lse_ref, part_ref, acc_ref,
):
    span = x_ref.shape[0]
    tiles = span // BLOCK

    @pl.when(pl.program_id(0) == 0)
    def _():
        h = x_ref[...].astype(f32) + (pa_ref[...] + pb_ref[...])
        h_ref[...] = h
        n_ref[...] = to_low(h * rms_factor(h) * g_ref[...])
        part_ref[...] = jnp.zeros_like(part_ref)

    turned = pltpu.roll(to_low(dot(n_ref[...], whole_weight(wq))).astype(f32), 1, 0)
    q = to_low(turned * score_scale)
    q_ref[...] = q
    for tile in range(tiles):
        rows = slice(tile * BLOCK, (tile + 1) * BLOCK)
        k, v = tile_keys(k_ref, tile, tiles), tile_keys(v_ref, tile, tiles)
        sc = dot_t(k, stack_heads(q[rows])) + tile_bias(len_ref, tile, tiles)
        top = jnp.max(sc, axis=0, keepdims=True)
        e = jnp.exp(sc - top)
        total = jnp.sum(e, axis=0, keepdims=True)
        lse_ref[0, tile : tile + 1, :] = top + jnp.log(total)
        acc_ref[rows, :] = merge_heads(t_dot(to_low(e * (1.0 / total)), v))
    o = to_low(pltpu.roll(acc_ref[...] * keep_ref[...], span - 1, 0))
    o_ref[...] = o
    part_ref[...] += dot_t(o, whole_weight(wo))


def cross_call(lens, x, pa, pb, gain, wq, wo, kv2, keep):
    span, model = x.shape
    keys, width = kv2.shape[0], kv2.shape[1] // 2
    pairs = width // PAIR
    pair = lambda p, *_: (0, p)
    fix = lambda p, *_: (0, 0)
    return call(
        cross_kernel,
        (pairs,),
        [
            ((span, model), fix),
            ((span, model), fix),
            ((span, model), fix),
            ((1, model), fix),
            (PAIR, each_block),
            ((keys, PAIR), pair),
            ((keys, PAIR), lambda p, *_: (0, pairs + p)),
            ((span, 1), fix),
            (PAIR, each_block),
        ],
        [
            ((span, model), fix, (span, model), f32),
            ((span, model), fix, (span, model), bf16),
            ((span, PAIR), pair, (span, width), bf16),
            ((span, PAIR), pair, (span, width), bf16),
            ((1, span // BLOCK, PAIR), lambda p, *_: (p, 0, 0), (pairs, span // BLOCK, PAIR), f32),
            ((span, model), fix, (span, model), f32),
        ],
        (lens, x, pa, pb, gain, wq, kv2, kv2, keep, wo),
        scratch=[pltpu.VMEM((span, PAIR), f32)],
        prefetch=1,
    )


def gelu_and_slope(u):
    t = jnp.tanh(gelu_c * (u + gelu_k * (u * u * u)))
    slope = 0.5 * (1.0 + t) + 0.5 * u * (1.0 - t * t) * (gelu_c * (1.0 + 3.0 * gelu_k * (u * u)))
    return to_low(0.5 * u * (1.0 + t)), slope


def norm_kernel(h1_ref, pa_ref, pb_ref, g_ref, turn_ref, h_ref, n_ref):
    h = h1_ref[...] + (pa_ref[...] + pb_ref[...])
    h_ref[...] = h
    n_ref[...] = to_low(dot_t(to_low(h * rms_factor(h) * g_ref[...]), turn_ref[...]))


def norm_call(h1, pa, pb, gain, turn):
    span, model = h1.shape
    row = lambda i: (i, 0)
    fix = lambda i: (0, 0)
    rows = span
    return call(
        norm_kernel,
        (1,),
        [((rows, model), row)] * 3 + [((1, model), fix), ((model, model), fix)],
        [
            ((rows, model), row, (span, model), f32),
            ((rows, model), row, (span, model), bf16),
        ],
        (h1, pa, pb, gain, turn),
    )


def feed_kernel(n_ref, cot_ref, up_ref, down_ref, act_ref, du_ref, ya_ref, yb_ref, da_ref, db_ref):
    up, down = up_ref[...], down_ref[...]
    act, slope = gelu_and_slope(dot(n_ref[...], up))
    du = to_low(dot(cot_ref[...], down) * slope)
    act_ref[...] = act
    du_ref[...] = du
    y, dn = dot_t(act, down), dot_t(du, up)
    step = pl.program_id(0)
    half = pl.num_programs(0) // 2

    @pl.when(step < half)
    def _():
        ya_ref[...] = to_low(y)
        da_ref[...] = dn

    @pl.when(step >= half)
    def _():
        yb_ref[...] = to_low(y)
        db_ref[...] = dn


def feed_call(n, cot, w_feed):
    rows, model = n.shape
    hidden = w_feed.shape[1] // 2
    half = rows // TOKENS // 2
    row = lambda i: (i, 0)
    lead = lambda i: (jnp.minimum(i, half - 1), 0)
    tail = lambda i: (jnp.maximum(i - half, 0), 0)
    block = (TOKENS, model)
    part = (rows // 2, model)
    return call(
        feed_kernel,
        (rows // TOKENS,),
        [
            (block, row),
            (block, row),
            ((model, hidden), lambda i: (0, 0)),
            ((model, hidden), lambda i: (0, 1)),
        ],
        [
            ((TOKENS, hidden), row, (rows, hidden), bf16),
            ((TOKENS, hidden), row, (rows, hidden), bf16),
            (block, lead, part, bf16),
            (block, tail, part, bf16),
            (block, lead, part, f32),
            (block, tail, part, f32),
        ],
        (n, cot, w_feed, w_feed),
    )


def cross_back_kernel(
    len_ref, core_ref, base_ref, h_ref, da_ref, db_ref, turn_ref, g_ref, wo, q_ref, k_ref, v_ref, lse_ref,
    keep_ref, wq,
    grad_ref, low_ref, gain_ref, dq_ref, dk_ref, dv_ref, dn_ref, acc_ref,
):
    span = h_ref.shape[0]
    tiles = span // BLOCK

    @pl.when(pl.program_id(0) == 0)
    def _():
        first, other = da_ref[...], db_ref[...]
        given = jnp.where(
            core_ref[0] == 0,
            jnp.concatenate([first, other], axis=0),
            jnp.concatenate([other, first], axis=0),
        )
        high = to_low(given)
        low = to_low(given - high.astype(f32))
        turn = turn_ref[...]
        back, gains = rms_back(h_ref[...], g_ref[...], dot(high, turn) + dot(low, turn))
        grad = base_ref[...].astype(f32) + back
        grad_ref[...] = grad
        low_ref[...] = to_low(grad)
        gain_ref[...] = jnp.sum(gains, axis=0, keepdims=True)
        dn_ref[...] = jnp.zeros_like(dn_ref)

    do = to_low(dot(low_ref[...], whole_weight(wo))).astype(f32)
    do = to_low(pltpu.roll(do, 1, 0) * keep_ref[...])
    q = q_ref[...]
    for tile in range(tiles):
        rows = slice(tile * BLOCK, (tile + 1) * BLOCK)
        k, v = tile_keys(k_ref, tile, tiles), tile_keys(v_ref, tile, tiles)
        qs, dos = stack_heads(q[rows]), stack_heads(do[rows])
        p = jnp.exp(dot_t(k, qs) + tile_bias(len_ref, tile, tiles) - lse_ref[0, tile : tile + 1, :])
        dp = dot_t(v, dos)
        ds = to_low(p * (dp - jnp.sum(p * dp, axis=0, keepdims=True)))
        acc_ref[rows, :] = merge_heads(t_dot(ds, k))
        dk = to_low(dot(ds, qs))
        dv = to_low(dot(to_low(p), dos))
        own = slice(tile * KEYS, (tile + 1) * KEYS)
        dk_ref[own, :] = dk[:KEYS]
        dv_ref[own, :] = dv[:KEYS]
        if not tile:
            last = slice(tiles * KEYS, (tiles + 1) * KEYS)
            dk_ref[last, :] = dk[KEYS:]
            dv_ref[last, :] = dv[KEYS:]
    dq = to_low(pltpu.roll(acc_ref[...] * score_scale, span - 1, 0))
    dq_ref[...] = dq
    dn_ref[...] += dot_t(dq, whole_weight(wq))


def cross_back_call(lens, core, base, h, da, db, turn, gain, wq, wo, q, kv2, lse, keep):
    span, model = h.shape
    keys, width = kv2.shape[0], kv2.shape[1] // 2
    pairs = width // PAIR
    pair = lambda p, *_: (0, p)
    fix = lambda p, *_: (0, 0)
    return call(
        cross_back_kernel,
        (pairs,),
        [
            ((span, model), fix),
            ((span, model), fix),
            ((span // 2, model), fix),
            ((span // 2, model), fix),
            ((model, model), fix),
            ((1, model), fix),
            (PAIR, each_block),
            ((span, PAIR), pair),
            ((keys, PAIR), pair),
            ((keys, PAIR), lambda p, *_: (0, pairs + p)),
            ((1, span // BLOCK, PAIR), lambda p, *_: (p, 0, 0)),
            ((span, 1), fix),
            (PAIR, each_block),
        ],
        [
            ((span, model), fix, (span, model), f32),
            ((span, model), fix, (span, model), bf16),
            ((1, model), fix, (1, model), f32),
            ((span, PAIR), pair, (span, width), bf16),
            ((keys, PAIR), pair, (keys, width), bf16),
            ((keys, PAIR), pair, (keys, width), bf16),
            ((span, model), fix, (span, model), f32),
        ],
        (lens, core, base, h, da, db, turn, gain, wo, q, kv2, kv2, lse, keep, wq),
        scratch=[pltpu.VMEM((span, PAIR), f32)],
        prefetch=2,
    )


def self_back_kernel(
    base_ref, h_ref, da_ref, db_ref, g_ref, wo, q_ref, k_ref, v_ref, lse_ref, segq_ref,
    segk_ref, cos_ref, sin_ref,
    grad_ref, low_ref, gain_ref, dq_ref, dk_ref, dv_ref, bias_ref,
):
    span = h_ref.shape[0]
    keys = k_ref.shape[0]

    @pl.when(pl.program_id(0) == 0)
    def _():
        back, gains = rms_back(h_ref[...], g_ref[...], da_ref[...] + db_ref[...])
        grad = base_ref[...] + back
        grad_ref[...] = grad
        low_ref[...] = to_low(grad)
        gain_ref[...] = jnp.sum(gains, axis=0, keepdims=True)
        self_bias(segq_ref, segk_ref, bias_ref)

    do = to_low(dot(low_ref[...], whole_weight(wo)))
    k, v, bias = k_ref[...], v_ref[...], bias_ref[...]
    qs, dos = split_heads(q_ref[...] * score_scale), split_heads(do)
    dqs, dk, dv = [], 0.0, 0.0
    for h in range(2):
        p = jnp.exp(dot_t(k, qs[h]) + bias - lse_ref[0, h : h + 1, :])
        dp = dot_t(v, dos[h])
        ds = to_low(p * (dp - jnp.sum(p * dp, axis=0, keepdims=True)))
        dqs.append(t_dot(ds, k))
        dk = dk + dot(ds, qs[h])
        dv = dv + dot(to_low(p), dos[h])
    cos, sin = cos_ref[...], sin_ref[...]
    dq = join_heads(dqs[0], dqs[1]) * score_scale
    dq_ref[...] = to_low(rope(dq, cos[keys - span :], sin[keys - span :], -1.0))
    dk_ref[...] = to_low(rope(dk, cos, sin, -1.0))
    dv_ref[...] = to_low(dv)


def self_back_call(base, h, da, db, gain, wo, q, k, v, lse, segq, segk, cos, sin):
    span, model = h.shape
    keys, width = k.shape
    pair = lambda p: (0, p)
    fix = lambda p: (0, 0)
    return call(
        self_back_kernel,
        (width // PAIR,),
        [
            ((span, model), fix),
            ((span, model), fix),
            ((span, model), fix),
            ((span, model), fix),
            ((1, model), fix),
            (PAIR, each_block),
            ((span, PAIR), pair),
            ((keys, PAIR), pair),
            ((keys, PAIR), pair),
            ((1, 2, span), lambda p: (p, 0, 0)),
            ((1, span), fix),
            ((keys, 1), fix),
            ((keys, PAIR), fix),
            ((keys, PAIR), fix),
        ],
        [
            ((span, model), fix, (span, model), f32),
            ((span, model), fix, (span, model), bf16),
            ((1, model), fix, (1, model), f32),
            ((span, PAIR), pair, (span, width), bf16),
            ((keys, PAIR), pair, (keys, width), bf16),
            ((keys, PAIR), pair, (keys, width), bf16),
        ],
        (base, h, da, db, gain, wo, q, k, v, lse, segq, segk, cos, sin),
        scratch=[pltpu.VMEM((keys, span), f32)],
    )


def inner_kernel(x_ref, dq_ref, dk_ref, dv_ref, wq, wk, wv, dn_ref, gain_ref):
    step = pl.program_id(0)
    rows, span = x_ref.shape[0], dq_ref.shape[0]
    own = rows - span
    dn = dot_t(dk_ref[...], whole_weight(wk)) + dot_t(dv_ref[...], whole_weight(wv))
    dn_own = dot_t(dq_ref[...], whole_weight(wq))

    @pl.when(step == 0)
    def _():
        dn_ref[...] = dn
        dn_ref[own:, :] += dn_own

    @pl.when(step > 0)
    def _():
        dn_ref[...] += dn
        dn_ref[own:, :] += dn_own

    @pl.when(step == pl.num_programs(0) - 1)
    def _():
        x = x_ref[...].astype(f32)
        gain_ref[...] = jnp.sum(dn_ref[...] * x * rms_factor(x), axis=0, keepdims=True)


def inner_call(x_ext, dq, dk, dv, wq, wk, wv):
    rows, model = x_ext.shape
    span, width = dq.shape
    fix = lambda i: (0, 0)
    col = lambda i: (0, i)
    return call(
        inner_kernel,
        (width // CHUNK,),
        [
            ((rows, model), fix),
            ((span, CHUNK), col),
            ((rows, CHUNK), col),
            ((rows, CHUNK), col),
            (CHUNK, each_block),
            (CHUNK, each_block),
            (CHUNK, each_block),
        ],
        [
            ((rows, model), fix, (rows, model), f32),
            ((1, model), fix, (1, model), f32),
        ],
        (x_ext, dq, dk, dv, wq, wk, wv),
    )


def adam_call(factor, groups):
    orders = [g[4] for g in groups]
    counts = len(groups)

    def adam_kernel(factor_ref, *refs):
        ins, outs = refs[: 4 * counts], refs[4 * counts :]
        for n, order in enumerate(orders):
            w_ref, g_ref, m_ref, v_ref = ins[4 * n : 4 * n + 4]
            wo_ref, mo_ref, vo_ref = outs[3 * n : 3 * n + 3]
            width = w_ref.shape[2]
            for j, at in enumerate(order):
                wo_ref[j], mo_ref[j], vo_ref[j] = adam_step(
                    w_ref[j],
                    g_ref[:, at * width : (at + 1) * width],
                    m_ref[j],
                    v_ref[j],
                    factor_ref[0],
                    learn_rate,
                    weight_decay,
                )

    def whole(a):
        return (a.shape, lambda i, *_, n=a.ndim: (0,) * n)

    arrays = [a for g in groups for a in g[:4]]
    results = [whole(g[0]) + (g[0].shape, f32) for g in groups for _ in range(3)]
    return call(
        adam_kernel, (1,), [whole(a) for a in arrays], results, (factor, *arrays), prefetch=1
    )


def last_sum_kernel(ka, ga, kb, gb, o_ref, mark_ref):
    mark_ref[...] = jnp.zeros_like(mark_ref)
    wide = ka.shape[1]
    o_ref[:, :wide] = to_low(ka[...].astype(f32) + ga[...].astype(f32))
    o_ref[:, wide:] = to_low(kb[...].astype(f32) + gb[...].astype(f32))


def last_sum_call(kept, got):
    rows, wide_a = kept[0].shape
    wide_b = kept[1].shape[1]
    fix = lambda i: (0, 0)
    a, b, o = (rows, wide_a), (rows, wide_b), (rows, wide_a + wide_b)
    return call(
        last_sum_kernel,
        (1,),
        [(a, fix), (a, fix), (b, fix), (b, fix)],
        [(o, fix, o, bf16), ((8, PAIR), fix, (8, PAIR), f32)],
        (kept[0], got[0], kept[1], got[1]),
    )


def total_kernel(got_ref, mark_ref, o_ref, squares_ref):
    rows = o_ref.shape[0]
    total = got_ref[:rows].astype(f32)
    for k in range(1, 4):
        total = total + got_ref[k * rows : (k + 1) * rows].astype(f32)
    o_ref[...] = total
    squares_ref[...] = jnp.sum(jnp.sum(total * total, axis=0, keepdims=True), axis=1, keepdims=True)


def total_call(got, mark):
    rows, cols = got.shape
    fix = lambda i: (0, 0)
    out = (rows // 4, cols)
    return call(
        total_kernel, (1,), [((rows, cols), fix), ((8, PAIR), fix)],
        [(out, fix, out, f32), ((1, 1), fix, (1, 1), f32)], (got, mark),
    )


def half_sum_kernel(ka, ga, kb, gb, keep_a, keep_b, sent_a, sent_b):
    step = pl.program_id(0)
    sum_a = to_low(ka[...].astype(f32) + ga[...].astype(f32))
    sum_b = to_low(kb[...].astype(f32) + gb[...].astype(f32))

    @pl.when(step == 0)
    def _():
        sent_a[...] = sum_a
        sent_b[...] = sum_b

    @pl.when(step == 1)
    def _():
        keep_a[...] = sum_a
        keep_b[...] = sum_b


def half_sum_call(kept, got):
    rows, (wide_a, wide_b) = kept[0].shape[0] // 2, (k.shape[1] for k in kept)
    turn = lambda i: (1 - i, 0)
    fix = lambda i: (0, 0)
    a, b = (rows, wide_a), (rows, wide_b)
    return call(
        half_sum_kernel,
        (2,),
        [(a, turn), (a, turn), (b, turn), (b, turn)],
        [(a, fix, a, bf16), (b, fix, b, bf16), (a, fix, a, bf16), (b, fix, b, bf16)],
        (kept[0], got[0], kept[1], got[1]),
    )


def pack_call(place, own, cross, feed, gain_cols, firsts, spans, wide):
    _, rows, width = own.shape
    plane = len(spans)

    def pack_kernel(place_ref, own_ref, cross_ref, feed_ref, gain_ref, q_ref, c_ref, f_ref):
        for j in range(3):
            q_ref[:, j * width : (j + 1) * width] = to_low(own_ref[j])
        q_ref[:, 3 * width :] = to_low(gain_ref[...])
        for j, part in enumerate((cross_ref[1], cross_ref[2], own_ref[3], cross_ref[0], cross_ref[3])):
            c_ref[:, j * width : (j + 1) * width] = to_low(part)
        for k in range(plane):
            pieces = []
            for m in range(2):
                pieces.append(to_low(feed_ref[m, :, firsts[k] : firsts[k] + spans[k]]))
                if spans[k] < wide:
                    pieces.append(jnp.zeros((rows, wide - spans[k]), bf16))
            f_ref[place_ref[k]] = jnp.concatenate(pieces, axis=1)

    whole = lambda a: (a.shape, lambda i, *_: (0,) * a.ndim)
    outs = [(rows, 3 * width + PAIR), (rows, 5 * width), (plane, rows, 2 * wide)]
    return call(
        pack_kernel,
        (1,),
        [whole(own), whole(cross), whole(feed), whole(gain_cols)],
        [(o, lambda i, *_, n=len(o): (0,) * n, o, bf16) for o in outs],
        (place, own, cross, feed, gain_cols),
        prefetch=1,
    )


def rows_kernel(a_ref, w, o_ref):
    o_ref[...] = to_low(dot(a_ref[...], whole_weight(w)))


def rows_call(a, w, width):
    rows, model = a.shape
    block = CHUNK if width % CHUNK == 0 else width // 7 if width % 7 == 0 else width
    return call(
        rows_kernel,
        (width // block,),
        [((rows, model), lambda i: (0, 0)), (block, each_block)],
        [((rows, block), lambda i: (0, i), (rows, width), bf16)],
        (a, w),
    )[0]


def turn_call(a, turn):
    rows, model = a.shape
    return call(
        turn_kernel,
        (rows // KEYS,),
        [((KEYS, model), lambda i: (i, 0)), ((model, model), lambda i: (0, 0))],
        [((KEYS, model), lambda i: (i, 0), (rows, model), bf16)],
        (a, turn),
    )[0]


def turn_kernel(a_ref, t_ref, o_ref):
    o_ref[...] = to_low(dot(a_ref[...], t_ref[...]))


def per_device(
    tokens,
    neighbours,
    neighbour_lengths,
    segment_ids,
    out_grad,
    self_weights,
    cross_weights,
    feed_weights,
    norm_gains,
    self_first,
    cross_first,
    feed_first,
    gains_first,
    self_second,
    cross_second,
    feed_second,
    gains_second,
):
    row_count, span, model = tokens.shape
    width = self_weights.shape[2]
    hidden = feed_weights.shape[2]
    shard_rows = self_weights.shape[1]
    pairs = width // PAIR
    blocks = span // BLOCK
    halo = min(-(-(DOC_MAX - 1) // span), lax.axis_size("seq") - 1)
    s_index = lax.axis_index("seq")
    core = lax.axis_index("mp")

    def columns(*parts):
        return jnp.concatenate([to_low(p) for p in parts], axis=1)

    gain_cols = jnp.zeros((shard_rows, PAIR), f32).at[:, :3].set(norm_gains.T)
    small = small_mesh()
    x_own, cot = tokens.reshape(span, model), out_grad.reshape(span, model)
    flat_own = neighbours.reshape(-1, model)
    half, pad = span // 2, KEYS // 2
    seg_here = segment_ids.reshape(1, span) + 1
    lengths = neighbour_lengths.reshape(blocks, NEIGHBOURS)
    ints = jnp.concatenate([seg_here[0], lengths[-1]]).astype(bf16)
    ints = jnp.zeros((8, model), bf16).at[0, : span + NEIGHBOURS].set(ints)
    mine = lax.dynamic_slice_in_dim(x_own, core * half, half, 0)
    edge = lax.dynamic_slice_in_dim(flat_own, flat_own.shape[0] - KEYS + core * pad, pad, 0)
    frequency = rope_base ** (-(jnp.arange(PAIR) % (HEAD_DIM // 2)).astype(f32) / (HEAD_DIM // 2))
    places = (s_index - halo) * span + jnp.arange((halo + 1) * span)
    angles = places.astype(f32)[:, None] * frequency[None, :]

    plane = lax.axis_size("seq")
    groups = hidden // PAIR
    wide = -(-groups // plane) * PAIR
    spans = [(groups + plane - 1 - k) // plane * PAIR for k in range(plane)]
    firsts = [sum(spans[:k]) for k in range(plane)]

    small = small_mesh()
    places_of = [s_index ^ k if small else k for k in range(plane)]
    block_q, block_c, block_f = pack_call(
        jnp.stack([jnp.asarray(p, jnp.int32) for p in places_of]),
        self_weights, cross_weights, feed_weights, gain_cols, firsts, spans, wide,
    )
    near = shifted(jnp.concatenate([mine, edge, ints], axis=0), "seq", 1)
    far = [shifted(jnp.concatenate([mine, ints], axis=0), "seq", k) for k in range(2, halo + 1)]
    if small:
        col_q = exchanged(wide_for_dp(block_q), "dp")
        spots = [s_index ^ k for k in range(plane)]
        col_q, near, block_c, block_f, angles, s_index, *far = meet(
            col_q, near, block_c, block_f, angles, s_index, *far
        )
        shares = [block_f[k] for k in range(plane)]
        xy_q = from_seq(col_q)
        shares = shares[:1] + [swapped(shares[k], "seq", k) for k in range(1, plane)]
    cos, sin = jnp.cos(angles), jnp.sin(angles)
    if small:
        turn = own_order(model, s_index)
        col_c = lax.all_gather(block_c, "dp", axis=0, tiled=True)
        cot_turned = turn_call(cot, turn)
    else:
        turn = jnp.eye(model, dtype=bf16)
        cot_turned = cot
    got = jnp.concatenate([near[: half + pad]] + [f[:half] for f in far], axis=0)
    other = swapped(got, "mp", 1)
    low_half = jnp.where(core == 0, got, other)
    high_half = jnp.where(core == 0, other, got)

    def whole(start, size):
        return [low_half[start : start + size], high_half[start : start + size]]

    pieces = []
    for k in range(halo, 1, -1):
        pieces += whole(half + pad + (k - 2) * half, half)
    x_ext = jnp.concatenate(pieces + whole(0, half) + [x_own], axis=0)
    flat_ext = jnp.concatenate(whole(half, pad) + [flat_own], axis=0)
    ints_prev = [near[half + pad]] + [f[half] for f in far]
    ints_prev = [p[None, : span + NEIGHBOURS].astype(jnp.int32) for p in ints_prev]
    seg_keys = jnp.concatenate([p[:, :span] for p in ints_prev[::-1]] + [seg_here], axis=1)
    seg_keys = seg_keys.reshape(-1, 1)
    lens = jnp.concatenate([ints_prev[0][:, span:], lengths], axis=0)
    before = jnp.concatenate([ints_prev[0][0, span - 1 : span], seg_here[0, : span - 1]])
    heads_of = jnp.repeat(before[::BLOCK], BLOCK)
    spot = jnp.arange(span)
    starts = jnp.where(s_index == 0, BLOCK, 0)
    keep = jnp.logical_or(spot == 0, jnp.logical_and(before == heads_of, spot >= starts))
    keep = keep.astype(f32).reshape(span, 1)

    if small:
        x_ext = turn_call(x_ext, turn)
        col_c, turn, cot_turned, cos, sin, x_ext, flat_ext, cot, *rest = meet(
            col_c, turn, cot_turned, cos, sin, x_ext, flat_ext, cot, *xy_q, *shares
        )
        xy_q, shares = rest[:3], rest[3:]
        w_feed = jnp.broadcast_to(shares[0], (plane, shard_rows, 2 * wide))
        for spot, piece in zip(spots[1:], shares[1:]):
            w_feed = put(w_feed, piece[None], (spot, 0, 0))
        w_feed = w_feed.reshape(plane * shard_rows, 2 * wide)
        w_feed = lax.all_gather(w_feed, "dp", axis=0, tiled=True)
        lead = 3 * width
        lead_c = from_seq(col_c[:, :lead])
        flat_ext = turn_call(flat_ext, turn)
        q_pieces = [col_q] + xy_q
        s_q, s_k, s_v = (weight(q_pieces, j * width) for j in range(3))
        gain_rows = jnp.concatenate(
            [p[:, 3 * width : 3 * width + PAIR] for p in q_pieces], axis=0
        )
    else:
        full_q, full_c = (
            lax.all_gather(b, ("dp", "seq"), axis=0, tiled=True) for b in (block_q, block_c)
        )
        w_feed = exchanged(block_f.reshape(plane * shard_rows, 2 * wide), "seq")
        w_feed = lax.all_gather(w_feed, "dp", axis=0, tiled=True)
        s_q, s_k, s_v = ([(full_q, j * width)] for j in range(3))
        gain_rows = full_q[:, 3 * width :]
        c_kv, s_o, c_q, c_o = ([(full_c, j * width)] for j in (0, 2, 3, 4))
    gains = gain_rows[:, :3].T.astype(f32)
    x = x_ext[halo * span :]
    n1, q, k, v = qkv_call(x_ext, gains[:1], s_q, s_k, s_v, cos, sin, span, width)
    if small:
        rest_c = col_c[:, lead:]
        q, flat_ext, seg_keys, lens, keep, cot, rest_c, *lead_c = meet(
            q, flat_ext, seg_keys, lens, keep, cot, rest_c, *lead_c
        )
        tail_c = from_seq(rest_c)
        c_kv, s_o = (weight([col_c] + lead_c, j * width) for j in (0, 2))
    def over_plane(rows):
        own = lax.dynamic_slice_in_dim(rows, core * half, half, 0)
        return [own] + [swapped(own, "seq", k) for k in range(1, plane)]

    def with_other(pieces):
        got = jnp.concatenate(pieces, axis=0)
        return jnp.concatenate([got, swapped(got, "mp", 1)], axis=0)

    def back_to_owner(own, other):
        total = own.astype(f32) + swapped(other, "mp", 1).astype(f32)
        sent = to_low(total)
        return [total[:half]] + [
            swapped(sent[k * half : (k + 1) * half], "seq", k) for k in range(1, plane)
        ]

    def f_assembled(got):
        got = got.reshape(plane, shard_rows, 2 * wide)
        return jnp.concatenate(
            [got[k, :, at : at + spans[k]] for at in (0, wide) for k in range(plane)], axis=1
        ).astype(f32)

    attn, lse, part = self_call(q, k, v, seg_here, seg_keys, s_o, model)
    kv2 = rows_call(flat_ext, c_kv, 2 * width)
    if small:
        part, kv2, cot, *tail_c = meet(part, kv2, cot, *tail_c)
        c_q, c_o = (weight([rest_c] + tail_c, j * width) for j in (0, 1))
    cot_rows = over_plane(cot)
    other = swapped(part, "mp", 1)
    h1, n2, q2, cross, lse2, part2 = cross_call(
        lens, x, part, other, gains[1:2], c_q, c_o, kv2, keep
    )
    if small:
        part2, *cot_rows = meet(part2, *cot_rows)
    cot_rows = with_other(cot_rows)
    other = swapped(part2, "mp", 1)
    h2, n3 = norm_call(h1, part2, other, gains[2:3], turn)

    n_rows = with_other(over_plane(n3))
    act, du, y_own, y_other, dn_own, dn_other = feed_call(n_rows, cot_rows, w_feed)
    dn3 = plane_sum(back_to_owner(dn_own, dn_other))
    dn3_other = swapped(dn3, "mp", 1)
    g2, low2, dgain3, dq2, dk2, dv2, dn2 = cross_back_call(
        lens, core.reshape(1), cot_turned, h2, dn3, dn3_other, turn, gains[2:3], c_q, c_o,
        q2, kv2, lse2, keep,
    )
    other = swapped(dn2, "mp", 1)
    cross_sent, cross_kept = halves(
        [(n2, dq2), (low2, cross)], [(flat_ext, dk2), (flat_ext, dv2)]
    )
    if small:
        *cross_sent, other, du, act = meet(*cross_sent, other, du, act)
        cross_got = reduce_first(cross_sent)
    g1, low1, dgain2, dq, dk, dv = self_back_call(
        g2, h1, dn2, other, gains[1:2], s_o, q, k, v, lse, seg_here, seg_keys, cos, sin
    )
    if small:
        *cross_got, low1, dq, dk, dv = meet(*cross_got, low1, dq, dk, dv)
        cross_kept, cross_got = reduce_second(cross_kept, cross_got)
    dn1, dgain1 = inner_call(x_ext, dq, dk, dv, s_q, s_k, s_v)
    if small:
        dn1, dgain1, dq, dk, dv, low1, *cross_got = meet(
            dn1, dgain1, dq, dk, dv, low1, *cross_got
        )
    dgains = jnp.concatenate([dgain1, 0.5 * dgain2, 0.5 * dgain3], axis=0)
    if small:
        dgains = jnp.dot(dgains, turn.T.astype(f32), precision=lax.Precision.HIGHEST)
        slots = jnp.pad(
            dgains.reshape(3, -1, shard_rows).transpose(1, 0, 2),
            ((0, 0), (0, 5), (0, PAIR - shard_rows)),
        )
        slots = jnp.repeat(slots, lax.axis_size("mp"), axis=0)
    self_sent, self_kept = halves(
        [(n1[halo * span :], dq), (low1, attn)],
        [(n1, dk), (n1, dv)],
    )
    if small:
        sent_a, sent_b, slots, du, act = meet(*self_sent, slots, du, act)
        self_got = reduce_first((sent_a, sent_b))
        slots = lax.all_to_all(slots, ("dp", "seq", "mp"), 0, 0, tiled=True)
        gains_part = jnp.sum(slots, axis=0)[:3, :shard_rows]
        cross_part = lax.psum_scatter(
            last_sum_call(cross_kept, cross_got)[0], "dp", scatter_dimension=0, tiled=True
        ).astype(f32)
        feed_grads = jnp.concatenate(
            [to_low(t_dot(n_rows, du)), to_low(t_dot(cot_rows, act))], axis=1
        )
        feed_low = lax.psum_scatter(feed_grads, "dp", scatter_dimension=0, tiled=True)
        *self_got, gains_part = meet(*self_got, gains_part)
        self_kept, self_got = reduce_second(self_kept, self_got)
        self_col, mark = last_sum_call(self_kept, meet(*self_got))
        dn1, y_own, y_other, mark = meet(dn1, y_own, y_other, mark)
        self_got = exchanged(self_col, "dp")
    y_sums = back_to_owner(y_own, y_other)
    own = dn1[halo * span :]
    if halo:
        view = dn1[: halo * span].reshape(halo, 2, half, model)
        summed = to_low(take(view, core, 1) + swapped(take(view, 1 - core, 1), "mp", 1))
        if small:
            summed = to_low(dot_t(summed.reshape(-1, model), turn)).reshape(halo, half, model)
    back_parts = [shifted(summed[halo - k], "seq", -k) for k in range(1, halo + 1)]
    if small:
        squares = jnp.sum(cross_part * cross_part) + jnp.sum(jnp.square(feed_low.astype(f32)))
        self_got, squares = meet(self_got, squares)
        self_part, self_squares = total_call(self_got, mark)
    else:
        feed_grads = jnp.concatenate(
            [to_low(t_dot(n_rows, du)), to_low(t_dot(cot_rows, act))], axis=1
        )
        feed_low = lax.psum_scatter(feed_grads, "dp", scatter_dimension=0, tiled=True)
        feed_part = f_assembled(exchanged(feed_low, "seq"))
        cross_part, self_part = reduce_plain(cross_kept), reduce_plain(self_kept)
        squares = jnp.sum(feed_part * feed_part) + jnp.sum(cross_part * cross_part)
        self_squares = jnp.sum(jnp.square(self_part)).reshape(1, 1)
    if not small:
        gain_sums = butterfly(dgains, ("mp", "seq", "dp"))
        shard = lax.axis_index("dp") * lax.axis_size("seq") + s_index
        gains_part = lax.dynamic_slice_in_dim(gain_sums, shard * shard_rows, shard_rows, axis=1)
    first_model = (core == 0).astype(f32)
    local_squares = (
        self_squares
        + squares
        + first_model * jnp.sum(gains_part * gains_part)
    )
    if small:
        shares = [take(feed_low.reshape(plane, shard_rows, 2 * wide), spot, 0) for spot in spots]
        local_squares, *rest = meet(local_squares, *y_sums, *back_parts, *shares)
        y_sums, back_parts, shares = rest[:plane], rest[plane:-plane], rest[-plane:]
        shares = shares[:1] + [swapped(shares[k], "seq", k) for k in range(1, plane)]
        feed_got = jnp.zeros((plane, shard_rows, 2 * wide), bf16)
        for spot, piece in zip(spots, shares):
            feed_got = put(feed_got, piece[None], (spot, 0, 0))
        feed_part = f_assembled(feed_got)
    grad_norm = jnp.sqrt(sum_everywhere(local_squares).reshape(()))
    factor = jnp.minimum(1.0, clip_limit / (grad_norm + 1e-06))
    scalar = factor.reshape(1)
    mixed_order, plain = (0, 2, 3, 1), (0, 1)
    y_half = plane_sum(y_sums)
    y_other = swapped(y_half, "mp", 1)
    y_all = jnp.concatenate(
        [jnp.where(core == 0, y_half, y_other), jnp.where(core == 0, y_other, y_half)], axis=0
    )
    if halo:
        back = sum(p.astype(f32) for p in back_parts)
        if small:
            back = dot(to_low(back), turn)
        own = own + put(jnp.zeros_like(own), back, (core * half, 0))
    back, _ = rms_back(x.astype(f32), gains[:1], core_sum(own))
    in_grad = g1 + back

    def in_model_order(rows):
        high = to_low(lax.reduce_precision(rows, 8, 7))
        rest = rows - high.astype(f32)
        mid = to_low(lax.reduce_precision(rest, 8, 7))
        low = to_low(rest - mid.astype(f32))
        return dot_t(high, turn) + (dot_t(mid, turn) + dot_t(low, turn))

    if small:
        in_grad = in_model_order(in_grad)
        result = to_low(in_model_order(h2) + y_all)
    else:
        result = to_low(h2 + y_all)
    in_grad = in_grad.reshape(row_count, span, model)
    out = result.reshape(row_count, span, model)
    (
        self_new, self_first_new, self_second_new,
        cross_new, cross_first_new, cross_second_new,
        feed_new, feed_first_new, feed_second_new,
    ) = adam_call(
        scalar,
        [
            (self_weights, self_part, self_first, self_second, mixed_order),
            (cross_weights, cross_part, cross_first, cross_second, mixed_order),
            (feed_weights, feed_part, feed_first, feed_second, plain),
        ],
    )
    gains_new, gains_first_new, gains_second_new = adam_step(
        norm_gains, gains_part, gains_first, gains_second, factor, gain_rate, 0.0
    )
    return (
        out,
        in_grad,
        grad_norm,
        self_new,
        cross_new,
        feed_new,
        gains_new,
        self_first_new,
        cross_first_new,
        feed_first_new,
        gains_first_new,
        self_second_new,
        cross_second_new,
        feed_second_new,
        gains_second_new,
    )


def solution(mesh):
    tok = P("dp", "seq", None)
    mat = P(None, ("dp", "seq"), "mp")
    vec = P(None, ("dp", "seq"))
    in_specs = (
        tok,
        P("dp", "seq", None, None, None),
        tok,
        P("dp", "seq"),
        tok,
    ) + (mat, mat, mat, vec) * 3
    out_specs = (tok, tok, P()) + (mat, mat, mat, vec) * 3
    return jax.shard_map(
        per_device, mesh=mesh, in_specs=in_specs, out_specs=out_specs, check_vma=False
    )
```

```python
import jax
import jax.numpy as jnp
from jax import lax
from jax.experimental import pallas as pl
from jax.experimental.pallas import tpu as pltpu
from jax.sharding import PartitionSpec as P

HEAD_DIM = 64
PAIR = 128
BLOCK = 64
NEIGHBOURS = 2
NEIGH_LEN = 128
KEYS = NEIGHBOURS * NEIGH_LEN
STEP = 10
DOC_MAX = 512
CHUNK = 256
TOKENS = 512

norm_eps = 1e-05
rope_base = 10000.0
beta_one = 0.9
beta_two = 0.95
adam_eps = 1e-08
weight_decay = 0.1
learn_rate = 0.1
gain_rate = 0.5
clip_limit = 1.0
masked_fill = -1e30
score_scale = HEAD_DIM ** (-0.5)
gelu_c = 0.7978845608028654
gelu_k = 0.044715

f32 = jnp.float32
bf16 = jnp.bfloat16


def to_low(array_in):
    return array_in.astype(bf16)


def shifted(value, axis, by):
    count = lax.axis_size(axis)
    return lax.ppermute(value, axis, [(i, i + by) for i in range(count) if 0 <= i + by < count])


def rotated(value, axis, by):
    count = lax.axis_size(axis)
    return lax.ppermute(value, axis, [(i, (i + by) % count) for i in range(count)])


def swapped(value, axis, by):
    count = lax.axis_size(axis)
    return lax.ppermute(value, axis, [(i, i ^ by) for i in range(count)])


def butterfly(value, axes):
    for axis in axes:
        step = 1
        while step < lax.axis_size(axis):
            value = value + swapped(value, axis, step)
            step *= 2
    return value


def sum_everywhere(value):
    axes = ("dp", "seq", "mp")
    if not small_mesh():
        return butterfly(value, axes)
    count = lax.axis_size("dp") * lax.axis_size("seq") * lax.axis_size("mp")
    spread = jnp.broadcast_to(value, (count, 8, PAIR))
    return jnp.sum(lax.all_to_all(spread, axes, 0, 0, tiled=True)[:, :1, :1], axis=0)


def core_sum(partial_out):
    return partial_out + swapped(partial_out, "mp", 1)


def small_mesh():
    return lax.axis_size("dp") == 4 and lax.axis_size("seq") == 4


def put(buffer, piece, starts):
    return lax.dynamic_update_slice(buffer, piece, starts)


def meet(*values):
    return lax.optimization_barrier(values)


ORDER = (0, 2, 1, 3)


def own_order(model, s):
    rows = model // 16
    spot = jnp.arange(model)
    near, z, inner = spot // (4 * rows), spot // rows % 4, spot % rows
    flip = (near % 2) * 2 + near // 2
    source = (z * 4 + (s ^ flip)) * rows + inner
    return (spot[:, None] == source[None, :]).astype(bf16)


def plane_sum(pieces):
    return (pieces[0] + pieces[1].astype(f32)) + (pieces[2].astype(f32) + pieces[3].astype(f32))


def take(array_in, index, axis):
    return lax.dynamic_index_in_dim(array_in, index, axis, keepdims=False)


def wide_for_dp(block):
    rows, cols = block.shape
    return jnp.broadcast_to(block[None], (4, rows, cols)).reshape(4 * rows, cols)


def exchanged(array_in, axis):
    return lax.all_to_all(array_in, axis, 0, 0, tiled=True)


def from_seq(column):
    return [swapped(column, "seq", k) for k in ORDER[1:]]


def weight(pieces, start):
    return [(p, start) for p in pieces]


def reduce_first(sent):
    return swapped(sent[0], "seq", 1), swapped(sent[1], "seq", 2)


def reduce_second(kept, got):
    keep_a, keep_b, sent_a, sent_b = half_sum_call(kept, got)
    return (keep_a, keep_b), (swapped(sent_a, "seq", 2), swapped(sent_b, "seq", 1))


def reduce_last(got):
    rows, cols = got.shape
    return jnp.sum(got.reshape(4, rows // 4, cols).astype(f32), axis=0)


def reduce_plain(grads):
    return lax.psum_scatter(
        jnp.concatenate(grads, axis=1), ("dp", "seq"), scatter_dimension=0, tiled=True
    ).astype(f32)


def halves(left, right):
    if not small_mesh():
        return None, [jnp.concatenate([to_low(t_dot(a, b)) for a, b in left + right], axis=1)]

    def products(pairs, pick):
        parts = [to_low(t_dot(pick(a), b)) for a, b in pairs]
        return parts[0] if len(parts) == 1 else jnp.concatenate(parts, axis=1)

    def second(a, first):
        quarter = a.shape[1] // 4
        return jnp.concatenate(
            [
                a[:, first * quarter : (first + 1) * quarter],
                a[:, (first + 2) * quarter : (first + 3) * quarter],
            ],
            axis=1,
        )

    mid = left[0][0].shape[1] // 2
    sent = (products(left, lambda a: a[:, mid:]), products(right, lambda a: second(a, 1)))
    kept = (products(left, lambda a: a[:, :mid]), products(right, lambda a: second(a, 0)))
    return sent, kept


def adam_step(weight, gradient, first_old, second_old, factor, step_rate, decay_coef):
    clipped = gradient * factor
    first_new = beta_one * first_old + (1.0 - beta_one) * clipped
    second_new = beta_two * second_old + (1.0 - beta_two) * clipped * clipped
    first_hat = first_new / (1.0 - beta_one**STEP)
    second_hat = second_new / (1.0 - beta_two**STEP)
    weight_new = weight - step_rate * (
        first_hat / (jnp.sqrt(second_hat) + adam_eps) + decay_coef * weight
    )
    return (weight_new, first_new, second_new)


def call(kernel, grid, ins, outs, args, scratch=(), prefetch=0):
    specs, flat, counts = [], list(args[:prefetch]), [1] * prefetch
    for (shape, index), arg in zip(ins, args[prefetch:]):
        if not isinstance(arg, list):
            specs.append(pl.BlockSpec(shape, index))
            flat.append(arg)
            counts.append(1)
            continue
        for array_in, start in arg:
            place = lambda *ids, at=start // shape, f=index: (0, f(ids[0]) + at)
            specs.append(pl.BlockSpec((array_in.shape[0], shape), place))
            flat.append(array_in)
        counts.append(-len(arg))

    def body(*refs):
        refs, grouped = list(refs), []
        for count in counts:
            grouped.append(refs.pop(0) if count > 0 else [refs.pop(0) for _ in range(-count)])
        kernel(*grouped, *refs)

    return pl.pallas_call(
        body,
        out_shape=[jax.ShapeDtypeStruct(o[2], o[3]) for o in outs],
        grid_spec=pltpu.PrefetchScalarGridSpec(
            num_scalar_prefetch=prefetch,
            grid=grid,
            in_specs=specs,
            out_specs=[pl.BlockSpec(o[0], o[1]) for o in outs],
            scratch_shapes=list(scratch),
        ),
        compiler_params=pltpu.CompilerParams(
            dimension_semantics=("arbitrary",) * len(grid), vmem_limit_bytes=56 << 20
        ),
        name=kernel.__name__,
    )(*flat)


def whole_weight(refs):
    pieces = [r[...] for r in refs]
    return pieces[0] if len(pieces) == 1 else jnp.concatenate(pieces, axis=0)


first_block = lambda i: 0
each_block = lambda i: i


def dot(a, b):
    return jnp.dot(a, b, preferred_element_type=f32)


def dot_t(a, b):
    return lax.dot_general(a, b, (((1,), (1,)), ((), ())), preferred_element_type=f32)


def t_dot(a, b):
    return lax.dot_general(a, b, (((0,), (0,)), ((), ())), preferred_element_type=f32)


def rms_factor(z):
    return lax.rsqrt(jnp.mean(z * z, axis=-1, keepdims=True) + norm_eps)


def rms_back(z, gain, grad):
    factor = rms_factor(z)
    scaled = grad * gain
    inner = jnp.mean(scaled * z, axis=-1, keepdims=True)
    return factor * scaled - z * (factor * factor * factor * inner), grad * z * factor


def lane_in_head(shape):
    return lax.broadcasted_iota(jnp.int32, shape, 1)


def rope(z, cos, sin, sign):
    lane = lane_in_head(z.shape)
    lead = lane % HEAD_DIM < HEAD_DIM // 2
    partner = jnp.where(lead, -pltpu.roll(z, PAIR - 32, 1), pltpu.roll(z, 32, 1))
    return z * cos + partner * (sin * sign)


def split_heads(z):
    first = lane_in_head(z.shape) < HEAD_DIM
    zero = jnp.zeros_like(z)
    return jnp.where(first, z, zero), jnp.where(first, zero, z)


def join_heads(a, b):
    return jnp.where(lane_in_head(a.shape) < HEAD_DIM, a, b)


def qkv_kernel(x_ref, g_ref, wq, wk, wv, cos_ref, sin_ref, n_ref, q_ref, k_ref, v_ref):
    rows, span = n_ref.shape[0], q_ref.shape[0]

    @pl.when(pl.program_id(0) == 0)
    def _():
        x = x_ref[...].astype(f32)
        n_ref[...] = to_low(x * rms_factor(x) * g_ref[...])

    normed, cos, sin = n_ref[...], cos_ref[...], sin_ref[...]

    def turned(raw, cos, sin):
        return jnp.concatenate(
            [
                to_low(rope(raw[:, c : c + PAIR], cos, sin, 1.0))
                for c in range(0, raw.shape[1], PAIR)
            ],
            axis=1,
        )

    k_ref[...] = turned(dot(normed, whole_weight(wk)), cos, sin)
    v_ref[...] = to_low(dot(normed, whole_weight(wv)))
    own = rows - span
    q_ref[...] = turned(dot(normed[own:], whole_weight(wq)), cos[own:], sin[own:])


def qkv_call(x_ext, gain, wq, wk, wv, cos, sin, span, width):
    rows, model = x_ext.shape
    fix = lambda i: (0, 0)
    col = lambda i: (0, i)
    return call(
        qkv_kernel,
        (width // CHUNK,),
        [
            ((rows, model), fix),
            ((1, model), fix),
            (CHUNK, each_block),
            (CHUNK, each_block),
            (CHUNK, each_block),
            ((rows, PAIR), fix),
            ((rows, PAIR), fix),
        ],
        [
            ((rows, model), fix, (rows, model), bf16),
            ((span, CHUNK), col, (span, width), bf16),
            ((rows, CHUNK), col, (rows, width), bf16),
            ((rows, CHUNK), col, (rows, width), bf16),
        ],
        (x_ext, gain, wq, wk, wv, cos, sin),
    )


def self_bias(segq_ref, segk_ref, bias_ref):
    keys, span = bias_ref.shape
    key_pos = lax.broadcasted_iota(jnp.int32, (keys, span), 0) - (keys - span)
    query_pos = lax.broadcasted_iota(jnp.int32, (keys, span), 1)
    ok = jnp.logical_and(key_pos <= query_pos, segk_ref[...] == segq_ref[...])
    bias_ref[...] = jnp.where(ok, 0.0, masked_fill)


def self_kernel(q_ref, k_ref, v_ref, segq_ref, segk_ref, wo, o_ref, lse_ref, part_ref, bias_ref):
    @pl.when(pl.program_id(0) == 0)
    def _():
        self_bias(segq_ref, segk_ref, bias_ref)
        part_ref[...] = jnp.zeros_like(part_ref)

    k, v, bias = k_ref[...], v_ref[...], bias_ref[...]
    outs, lses = [], []
    for qh in split_heads(q_ref[...] * score_scale):
        s = dot_t(k, qh) + bias
        top = jnp.max(s, axis=0, keepdims=True)
        e = jnp.exp(s - top)
        total = jnp.sum(e, axis=0, keepdims=True)
        lses.append(top + jnp.log(total))
        outs.append(t_dot(to_low(e * (1.0 / total)), v))
    o = to_low(join_heads(outs[0], outs[1]))
    o_ref[...] = o
    lse_ref[0] = jnp.concatenate(lses, axis=0)
    part_ref[...] += dot_t(o, whole_weight(wo))


def self_call(q, k, v, segq, segk, wo, model):
    span, width = q.shape
    keys = k.shape[0]
    pair = lambda p: (0, p)
    fix = lambda p: (0, 0)
    return call(
        self_kernel,
        (width // PAIR,),
        [
            ((span, PAIR), pair),
            ((keys, PAIR), pair),
            ((keys, PAIR), pair),
            ((1, span), fix),
            ((keys, 1), fix),
            (PAIR, each_block),
        ],
        [
            ((span, PAIR), pair, (span, width), bf16),
            ((1, 2, span), lambda p: (p, 0, 0), (width // PAIR, 2, span), f32),
            ((span, model), fix, (span, model), f32),
        ],
        (q, k, v, segq, segk, wo),
        scratch=[pltpu.VMEM((keys, span), f32)],
    )


def block_bias(len_ref, block):
    key = lax.broadcasted_iota(jnp.int32, (KEYS, PAIR), 0)
    limit = jnp.where(key < NEIGH_LEN, len_ref[block, 0], len_ref[block, 1])
    return jnp.where(key % NEIGH_LEN < limit, 0.0, masked_fill)


def tile_bias(len_ref, tile, tiles):
    if tile:
        return block_bias(len_ref, tile)
    first = lax.broadcasted_iota(jnp.int32, (KEYS, PAIR), 1) % BLOCK == 0
    lead = jnp.where(first, masked_fill, block_bias(len_ref, 0))
    last = jnp.where(first, block_bias(len_ref, tiles), masked_fill)
    return jnp.concatenate([lead, last], axis=0)


def stack_heads(z):
    return jnp.concatenate(split_heads(z), axis=0)


def merge_heads(z):
    return join_heads(z[:BLOCK], z[BLOCK:])


def tile_keys(ref, tile, tiles):
    own = ref[tile * KEYS : (tile + 1) * KEYS, :]
    if tile:
        return own
    return jnp.concatenate([own, ref[tiles * KEYS : (tiles + 1) * KEYS, :]], axis=0)


def cross_kernel(
    len_ref, x_ref, pa_ref, pb_ref, g_ref, wq, k_ref, v_ref, keep_ref, wo,
    h_ref, n_ref, q_ref, o_ref, lse_ref, part_ref, acc_ref,
):
    span = x_ref.shape[0]
    tiles = span // BLOCK

    @pl.when(pl.program_id(0) == 0)
    def _():
        h = x_ref[...].astype(f32) + (pa_ref[...] + pb_ref[...])
        h_ref[...] = h
        n_ref[...] = to_low(h * rms_factor(h) * g_ref[...])
        part_ref[...] = jnp.zeros_like(part_ref)

    turned = pltpu.roll(to_low(dot(n_ref[...], whole_weight(wq))).astype(f32), 1, 0)
    q = to_low(turned * score_scale)
    q_ref[...] = q
    for tile in range(tiles):
        rows = slice(tile * BLOCK, (tile + 1) * BLOCK)
        k, v = tile_keys(k_ref, tile, tiles), tile_keys(v_ref, tile, tiles)
        sc = dot_t(k, stack_heads(q[rows])) + tile_bias(len_ref, tile, tiles)
        top = jnp.max(sc, axis=0, keepdims=True)
        e = jnp.exp(sc - top)
        total = jnp.sum(e, axis=0, keepdims=True)
        lse_ref[0, tile : tile + 1, :] = top + jnp.log(total)
        acc_ref[rows, :] = merge_heads(t_dot(to_low(e * (1.0 / total)), v))
    o = to_low(pltpu.roll(acc_ref[...] * keep_ref[...], span - 1, 0))
    o_ref[...] = o
    part_ref[...] += dot_t(o, whole_weight(wo))


def cross_call(lens, x, pa, pb, gain, wq, wo, kv2, keep):
    span, model = x.shape
    keys, width = kv2.shape[0], kv2.shape[1] // 2
    pairs = width // PAIR
    pair = lambda p, *_: (0, p)
    fix = lambda p, *_: (0, 0)
    return call(
        cross_kernel,
        (pairs,),
        [
            ((span, model), fix),
            ((span, model), fix),
            ((span, model), fix),
            ((1, model), fix),
            (PAIR, each_block),
            ((keys, PAIR), pair),
            ((keys, PAIR), lambda p, *_: (0, pairs + p)),
            ((span, 1), fix),
            (PAIR, each_block),
        ],
        [
            ((span, model), fix, (span, model), f32),
            ((span, model), fix, (span, model), bf16),
            ((span, PAIR), pair, (span, width), bf16),
            ((span, PAIR), pair, (span, width), bf16),
            ((1, span // BLOCK, PAIR), lambda p, *_: (p, 0, 0), (pairs, span // BLOCK, PAIR), f32),
            ((span, model), fix, (span, model), f32),
        ],
        (lens, x, pa, pb, gain, wq, kv2, kv2, keep, wo),
        scratch=[pltpu.VMEM((span, PAIR), f32)],
        prefetch=1,
    )


def gelu_and_slope(u):
    t = jnp.tanh(gelu_c * (u + gelu_k * (u * u * u)))
    slope = 0.5 * (1.0 + t) + 0.5 * u * (1.0 - t * t) * (gelu_c * (1.0 + 3.0 * gelu_k * (u * u)))
    return to_low(0.5 * u * (1.0 + t)), slope


def norm_kernel(core_ref, h1_ref, pa_ref, pb_ref, g_ref, turn_ref, h_ref, n_ref):
    h = h1_ref[...] + (pa_ref[...] + pb_ref[...])
    h_ref[...] = h
    normed = to_low(h * rms_factor(h) * g_ref[...])
    rows = n_ref.shape[0]
    mine = jnp.where(core_ref[0] == 0, normed[:rows], normed[rows:])
    n_ref[...] = to_low(dot_t(mine, turn_ref[...]))


def norm_call(core, h1, pa, pb, gain, turn):
    span, model = h1.shape
    fix = lambda i, *_: (0, 0)
    whole = ((span, model), fix)
    return call(
        norm_kernel,
        (1,),
        [whole, whole, whole, ((1, model), fix), ((model, model), fix)],
        [
            ((span, model), fix, (span, model), f32),
            ((span // 2, model), fix, (span // 2, model), bf16),
        ],
        (core, h1, pa, pb, gain, turn),
        prefetch=1,
    )


def feed_kernel(n_ref, cot_ref, up_ref, down_ref, act_ref, du_ref, ya_ref, yb_ref, da_ref, db_ref):
    up, down = up_ref[...], down_ref[...]
    act, slope = gelu_and_slope(dot(n_ref[...], up))
    du = to_low(dot(cot_ref[...], down) * slope)
    act_ref[...] = act
    du_ref[...] = du
    y, dn = dot_t(act, down), dot_t(du, up)
    step = pl.program_id(0)
    half = pl.num_programs(0) // 2

    @pl.when(step < half)
    def _():
        ya_ref[...] = to_low(y)
        da_ref[...] = dn

    @pl.when(step >= half)
    def _():
        yb_ref[...] = to_low(y)
        db_ref[...] = dn


def feed_call(n, cot, w_feed):
    rows, model = n.shape
    hidden = w_feed.shape[1] // 2
    half = rows // TOKENS // 2
    row = lambda i: (i, 0)
    lead = lambda i: (jnp.minimum(i, half - 1), 0)
    tail = lambda i: (jnp.maximum(i - half, 0), 0)
    block = (TOKENS, model)
    part = (rows // 2, model)
    return call(
        feed_kernel,
        (rows // TOKENS,),
        [
            (block, row),
            (block, row),
            ((model, hidden), lambda i: (0, 0)),
            ((model, hidden), lambda i: (0, 1)),
        ],
        [
            ((TOKENS, hidden), row, (rows, hidden), bf16),
            ((TOKENS, hidden), row, (rows, hidden), bf16),
            (block, lead, part, bf16),
            (block, tail, part, bf16),
            (block, lead, part, f32),
            (block, tail, part, f32),
        ],
        (n, cot, w_feed, w_feed),
    )


def cross_back_kernel(
    len_ref, core_ref, base_ref, h_ref, da_ref, db_ref, turn_ref, g_ref, wo, q_ref, k_ref, v_ref, lse_ref,
    keep_ref, wq,
    grad_ref, low_ref, gain_ref, dq_ref, dk_ref, dv_ref, dn_ref, acc_ref,
):
    span = h_ref.shape[0]
    tiles = span // BLOCK

    @pl.when(pl.program_id(0) == 0)
    def _():
        first, other = da_ref[...], db_ref[...]
        given = jnp.where(
            core_ref[0] == 0,
            jnp.concatenate([first, other], axis=0),
            jnp.concatenate([other, first], axis=0),
        )
        high = to_low(given)
        low = to_low(given - high.astype(f32))
        turn = turn_ref[...]
        back, gains = rms_back(h_ref[...], g_ref[...], dot(high, turn) + dot(low, turn))
        grad = base_ref[...].astype(f32) + back
        grad_ref[...] = grad
        low_ref[...] = to_low(grad)
        gain_ref[...] = jnp.sum(gains, axis=0, keepdims=True)
        dn_ref[...] = jnp.zeros_like(dn_ref)

    do = to_low(dot(low_ref[...], whole_weight(wo))).astype(f32)
    do = to_low(pltpu.roll(do, 1, 0) * keep_ref[...])
    q = q_ref[...]
    for tile in range(tiles):
        rows = slice(tile * BLOCK, (tile + 1) * BLOCK)
        k, v = tile_keys(k_ref, tile, tiles), tile_keys(v_ref, tile, tiles)
        qs, dos = stack_heads(q[rows]), stack_heads(do[rows])
        p = jnp.exp(dot_t(k, qs) + tile_bias(len_ref, tile, tiles) - lse_ref[0, tile : tile + 1, :])
        dp = dot_t(v, dos)
        ds = to_low(p * (dp - jnp.sum(p * dp, axis=0, keepdims=True)))
        acc_ref[rows, :] = merge_heads(t_dot(ds, k))
        dk = to_low(dot(ds, qs))
        dv = to_low(dot(to_low(p), dos))
        own = slice(tile * KEYS, (tile + 1) * KEYS)
        dk_ref[own, :] = dk[:KEYS]
        dv_ref[own, :] = dv[:KEYS]
        if not tile:
            last = slice(tiles * KEYS, (tiles + 1) * KEYS)
            dk_ref[last, :] = dk[KEYS:]
            dv_ref[last, :] = dv[KEYS:]
    dq = to_low(pltpu.roll(acc_ref[...] * score_scale, span - 1, 0))
    dq_ref[...] = dq
    dn_ref[...] += dot_t(dq, whole_weight(wq))


def cross_back_call(lens, core, base, h, da, db, turn, gain, wq, wo, q, kv2, lse, keep):
    span, model = h.shape
    keys, width = kv2.shape[0], kv2.shape[1] // 2
    pairs = width // PAIR
    pair = lambda p, *_: (0, p)
    fix = lambda p, *_: (0, 0)
    return call(
        cross_back_kernel,
        (pairs,),
        [
            ((span, model), fix),
            ((span, model), fix),
            ((span // 2, model), fix),
            ((span // 2, model), fix),
            ((model, model), fix),
            ((1, model), fix),
            (PAIR, each_block),
            ((span, PAIR), pair),
            ((keys, PAIR), pair),
            ((keys, PAIR), lambda p, *_: (0, pairs + p)),
            ((1, span // BLOCK, PAIR), lambda p, *_: (p, 0, 0)),
            ((span, 1), fix),
            (PAIR, each_block),
        ],
        [
            ((span, model), fix, (span, model), f32),
            ((span, model), fix, (span, model), bf16),
            ((1, model), fix, (1, model), f32),
            ((span, PAIR), pair, (span, width), bf16),
            ((keys, PAIR), pair, (keys, width), bf16),
            ((keys, PAIR), pair, (keys, width), bf16),
            ((span, model), fix, (span, model), f32),
        ],
        (lens, core, base, h, da, db, turn, gain, wo, q, kv2, kv2, lse, keep, wq),
        scratch=[pltpu.VMEM((span, PAIR), f32)],
        prefetch=2,
    )


def self_back_kernel(
    base_ref, h_ref, da_ref, db_ref, g_ref, wo, q_ref, k_ref, v_ref, lse_ref, segq_ref,
    segk_ref, cos_ref, sin_ref,
    grad_ref, low_ref, gain_ref, dq_ref, dk_ref, dv_ref, bias_ref,
):
    span = h_ref.shape[0]
    keys = k_ref.shape[0]

    @pl.when(pl.program_id(0) == 0)
    def _():
        back, gains = rms_back(h_ref[...], g_ref[...], da_ref[...] + db_ref[...])
        grad = base_ref[...] + back
        grad_ref[...] = grad
        low_ref[...] = to_low(grad)
        gain_ref[...] = jnp.sum(gains, axis=0, keepdims=True)
        self_bias(segq_ref, segk_ref, bias_ref)

    do = to_low(dot(low_ref[...], whole_weight(wo)))
    k, v, bias = k_ref[...], v_ref[...], bias_ref[...]
    qs, dos = split_heads(q_ref[...] * score_scale), split_heads(do)
    dqs, dk, dv = [], 0.0, 0.0
    for h in range(2):
        p = jnp.exp(dot_t(k, qs[h]) + bias - lse_ref[0, h : h + 1, :])
        dp = dot_t(v, dos[h])
        ds = to_low(p * (dp - jnp.sum(p * dp, axis=0, keepdims=True)))
        dqs.append(t_dot(ds, k))
        dk = dk + dot(ds, qs[h])
        dv = dv + dot(to_low(p), dos[h])
    cos, sin = cos_ref[...], sin_ref[...]
    dq = join_heads(dqs[0], dqs[1]) * score_scale
    dq_ref[...] = to_low(rope(dq, cos[keys - span :], sin[keys - span :], -1.0))
    dk_ref[...] = to_low(rope(dk, cos, sin, -1.0))
    dv_ref[...] = to_low(dv)


def self_back_call(base, h, da, db, gain, wo, q, k, v, lse, segq, segk, cos, sin):
    span, model = h.shape
    keys, width = k.shape
    pair = lambda p: (0, p)
    fix = lambda p: (0, 0)
    return call(
        self_back_kernel,
        (width // PAIR,),
        [
            ((span, model), fix),
            ((span, model), fix),
            ((span, model), fix),
            ((span, model), fix),
            ((1, model), fix),
            (PAIR, each_block),
            ((span, PAIR), pair),
            ((keys, PAIR), pair),
            ((keys, PAIR), pair),
            ((1, 2, span), lambda p: (p, 0, 0)),
            ((1, span), fix),
            ((keys, 1), fix),
            ((keys, PAIR), fix),
            ((keys, PAIR), fix),
        ],
        [
            ((span, model), fix, (span, model), f32),
            ((span, model), fix, (span, model), bf16),
            ((1, model), fix, (1, model), f32),
            ((span, PAIR), pair, (span, width), bf16),
            ((keys, PAIR), pair, (keys, width), bf16),
            ((keys, PAIR), pair, (keys, width), bf16),
        ],
        (base, h, da, db, gain, wo, q, k, v, lse, segq, segk, cos, sin),
        scratch=[pltpu.VMEM((keys, span), f32)],
    )


def inner_kernel(
    core_ref, x_ref, dq_ref, dk_ref, dv_ref, wq, wk, wv,
    own_ref, mine_ref, other_ref, gain_ref, dn_ref,
):
    step = pl.program_id(0)
    rows, span = x_ref.shape[0], dq_ref.shape[0]
    own, half = rows - span, span // 2
    dn = dot_t(dk_ref[...], whole_weight(wk)) + dot_t(dv_ref[...], whole_weight(wv))
    dn_own = dot_t(dq_ref[...], whole_weight(wq))

    @pl.when(step == 0)
    def _():
        dn_ref[...] = dn
        dn_ref[own:, :] += dn_own

    @pl.when(step > 0)
    def _():
        dn_ref[...] += dn
        dn_ref[own:, :] += dn_own

    @pl.when(step == pl.num_programs(0) - 1)
    def _():
        x = x_ref[...].astype(f32)
        gain_ref[...] = jnp.sum(dn_ref[...] * x * rms_factor(x), axis=0, keepdims=True)
        own_ref[...] = dn_ref[own:, :]
        core = core_ref[0]
        for k in range(own // span):
            spot = slice(k * half, (k + 1) * half)
            mine = pl.multiple_of(k * span + core * half, half)
            other = pl.multiple_of(k * span + (1 - core) * half, half)
            mine_ref[spot, :] = dn_ref[pl.ds(mine, half), :]
            other_ref[spot, :] = dn_ref[pl.ds(other, half), :]


def inner_call(core, x_ext, dq, dk, dv, wq, wk, wv):
    rows, model = x_ext.shape
    span, width = dq.shape
    fix = lambda i, *_: (0, 0)
    col = lambda i, *_: (0, i)
    part = ((rows - span) // 2, model)
    return call(
        inner_kernel,
        (width // CHUNK,),
        [
            ((rows, model), fix),
            ((span, CHUNK), col),
            ((rows, CHUNK), col),
            ((rows, CHUNK), col),
            (CHUNK, each_block),
            (CHUNK, each_block),
            (CHUNK, each_block),
        ],
        [
            ((span, model), fix, (span, model), f32),
            (part, fix, part, f32),
            (part, fix, part, f32),
            ((1, model), fix, (1, model), f32),
        ],
        (core, x_ext, dq, dk, dv, wq, wk, wv),
        scratch=[pltpu.VMEM((rows, model), f32)],
        prefetch=1,
    )


def adam_call(factor, groups):
    orders = [g[4] for g in groups]
    counts = len(groups)

    def adam_kernel(factor_ref, *refs):
        ins, outs = refs[: 4 * counts], refs[4 * counts :]
        for n, order in enumerate(orders):
            w_ref, g_ref, m_ref, v_ref = ins[4 * n : 4 * n + 4]
            wo_ref, mo_ref, vo_ref = outs[3 * n : 3 * n + 3]
            width = w_ref.shape[2]
            for j, at in enumerate(order):
                wo_ref[j], mo_ref[j], vo_ref[j] = adam_step(
                    w_ref[j],
                    g_ref[:, at * width : (at + 1) * width],
                    m_ref[j],
                    v_ref[j],
                    factor_ref[0],
                    learn_rate,
                    weight_decay,
                )

    def whole(a):
        return (a.shape, lambda i, *_, n=a.ndim: (0,) * n)

    arrays = [a for g in groups for a in g[:4]]
    results = [whole(g[0]) + (g[0].shape, f32) for g in groups for _ in range(3)]
    return call(
        adam_kernel, (1,), [whole(a) for a in arrays], results, (factor, *arrays), prefetch=1
    )


def last_sum_kernel(ka, ga, kb, gb, o_ref, mark_ref):
    mark_ref[...] = jnp.zeros_like(mark_ref)
    wide = ka.shape[1]
    o_ref[:, :wide] = to_low(ka[...].astype(f32) + ga[...].astype(f32))
    o_ref[:, wide:] = to_low(kb[...].astype(f32) + gb[...].astype(f32))


def last_sum_call(kept, got):
    rows, wide_a = kept[0].shape
    wide_b = kept[1].shape[1]
    fix = lambda i: (0, 0)
    a, b, o = (rows, wide_a), (rows, wide_b), (rows, wide_a + wide_b)
    return call(
        last_sum_kernel,
        (1,),
        [(a, fix), (a, fix), (b, fix), (b, fix)],
        [(o, fix, o, bf16), ((8, PAIR), fix, (8, PAIR), f32)],
        (kept[0], got[0], kept[1], got[1]),
    )


def total_kernel(got_ref, mark_ref, o_ref, squares_ref):
    rows = o_ref.shape[0]
    total = got_ref[:rows].astype(f32)
    for k in range(1, 4):
        total = total + got_ref[k * rows : (k + 1) * rows].astype(f32)
    o_ref[...] = total
    squares_ref[...] = jnp.sum(jnp.sum(total * total, axis=0, keepdims=True), axis=1, keepdims=True)


def total_call(got, mark):
    rows, cols = got.shape
    fix = lambda i: (0, 0)
    out = (rows // 4, cols)
    return call(
        total_kernel, (1,), [((rows, cols), fix), ((8, PAIR), fix)],
        [(out, fix, out, f32), ((1, 1), fix, (1, 1), f32)], (got, mark),
    )


def half_sum_kernel(ka, ga, kb, gb, keep_a, keep_b, sent_a, sent_b):
    step = pl.program_id(0)
    sum_a = to_low(ka[...].astype(f32) + ga[...].astype(f32))
    sum_b = to_low(kb[...].astype(f32) + gb[...].astype(f32))

    @pl.when(step == 0)
    def _():
        sent_a[...] = sum_a
        sent_b[...] = sum_b

    @pl.when(step == 1)
    def _():
        keep_a[...] = sum_a
        keep_b[...] = sum_b


def half_sum_call(kept, got):
    rows, (wide_a, wide_b) = kept[0].shape[0] // 2, (k.shape[1] for k in kept)
    turn = lambda i: (1 - i, 0)
    fix = lambda i: (0, 0)
    a, b = (rows, wide_a), (rows, wide_b)
    return call(
        half_sum_kernel,
        (2,),
        [(a, turn), (a, turn), (b, turn), (b, turn)],
        [(a, fix, a, bf16), (b, fix, b, bf16), (a, fix, a, bf16), (b, fix, b, bf16)],
        (kept[0], got[0], kept[1], got[1]),
    )


def pack_call(place, own, cross, feed, gain_cols, firsts, spans, wide):
    _, rows, width = own.shape
    plane = len(spans)

    def pack_kernel(place_ref, own_ref, cross_ref, feed_ref, gain_ref, q_ref, c_ref, f_ref):
        for j in range(3):
            q_ref[:, j * width : (j + 1) * width] = to_low(own_ref[j])
        q_ref[:, 3 * width :] = to_low(gain_ref[...])
        for j, part in enumerate((cross_ref[1], cross_ref[2], own_ref[3], cross_ref[0], cross_ref[3])):
            c_ref[:, j * width : (j + 1) * width] = to_low(part)
        for k in range(plane):
            pieces = []
            for m in range(2):
                pieces.append(to_low(feed_ref[m, :, firsts[k] : firsts[k] + spans[k]]))
                if spans[k] < wide:
                    pieces.append(jnp.zeros((rows, wide - spans[k]), bf16))
            f_ref[place_ref[k]] = jnp.concatenate(pieces, axis=1)

    whole = lambda a: (a.shape, lambda i, *_: (0,) * a.ndim)
    outs = [(rows, 3 * width + PAIR), (rows, 5 * width), (plane, rows, 2 * wide)]
    return call(
        pack_kernel,
        (1,),
        [whole(own), whole(cross), whole(feed), whole(gain_cols)],
        [(o, lambda i, *_, n=len(o): (0,) * n, o, bf16) for o in outs],
        (place, own, cross, feed, gain_cols),
        prefetch=1,
    )


def rows_kernel(a_ref, w, o_ref):
    o_ref[...] = to_low(dot(a_ref[...], whole_weight(w)))


def rows_call(a, w, width):
    rows, model = a.shape
    block = CHUNK if width % CHUNK == 0 else width // 7 if width % 7 == 0 else width
    return call(
        rows_kernel,
        (width // block,),
        [((rows, model), lambda i: (0, 0)), (block, each_block)],
        [((rows, block), lambda i: (0, i), (rows, width), bf16)],
        (a, w),
    )[0]


def turn_call(a, turn):
    rows, model = a.shape
    return call(
        turn_kernel,
        (rows // KEYS,),
        [((KEYS, model), lambda i: (i, 0)), ((model, model), lambda i: (0, 0))],
        [((KEYS, model), lambda i: (i, 0), (rows, model), bf16)],
        (a, turn),
    )[0]


def turn_kernel(a_ref, t_ref, o_ref):
    o_ref[...] = to_low(dot(a_ref[...], t_ref[...]))


def per_device(
    tokens,
    neighbours,
    neighbour_lengths,
    segment_ids,
    out_grad,
    self_weights,
    cross_weights,
    feed_weights,
    norm_gains,
    self_first,
    cross_first,
    feed_first,
    gains_first,
    self_second,
    cross_second,
    feed_second,
    gains_second,
):
    row_count, span, model = tokens.shape
    width = self_weights.shape[2]
    hidden = feed_weights.shape[2]
    shard_rows = self_weights.shape[1]
    pairs = width // PAIR
    blocks = span // BLOCK
    halo = min(-(-(DOC_MAX - 1) // span), lax.axis_size("seq") - 1)
    s_index = lax.axis_index("seq")
    core = lax.axis_index("mp")

    def columns(*parts):
        return jnp.concatenate([to_low(p) for p in parts], axis=1)

    gain_cols = jnp.zeros((shard_rows, PAIR), f32).at[:, :3].set(norm_gains.T)
    small = small_mesh()
    x_own, cot = tokens.reshape(span, model), out_grad.reshape(span, model)
    flat_own = neighbours.reshape(-1, model)
    half, pad = span // 2, KEYS // 2
    seg_here = segment_ids.reshape(1, span) + 1
    lengths = neighbour_lengths.reshape(blocks, NEIGHBOURS)
    ints = jnp.concatenate([seg_here[0], lengths[-1]]).astype(bf16)
    ints = jnp.zeros((8, model), bf16).at[0, : span + NEIGHBOURS].set(ints)
    mine = lax.dynamic_slice_in_dim(x_own, core * half, half, 0)
    edge = lax.dynamic_slice_in_dim(flat_own, flat_own.shape[0] - KEYS + core * pad, pad, 0)
    frequency = rope_base ** (-(jnp.arange(PAIR) % (HEAD_DIM // 2)).astype(f32) / (HEAD_DIM // 2))
    places = (s_index - halo) * span + jnp.arange((halo + 1) * span)
    angles = places.astype(f32)[:, None] * frequency[None, :]

    plane = lax.axis_size("seq")
    groups = hidden // PAIR
    wide = -(-groups // plane) * PAIR
    spans = [(groups + plane - 1 - k) // plane * PAIR for k in range(plane)]
    firsts = [sum(spans[:k]) for k in range(plane)]

    small = small_mesh()
    places_of = [s_index ^ k if small else k for k in range(plane)]
    block_q, block_c, block_f = pack_call(
        jnp.stack([jnp.asarray(p, jnp.int32) for p in places_of]),
        self_weights, cross_weights, feed_weights, gain_cols, firsts, spans, wide,
    )
    near = shifted(jnp.concatenate([mine, edge, ints], axis=0), "seq", 1)
    far = [shifted(jnp.concatenate([mine, ints], axis=0), "seq", k) for k in range(2, halo + 1)]
    if small:
        col_q = exchanged(wide_for_dp(block_q), "dp")
        spots = [s_index ^ k for k in range(plane)]
        cos, sin, turn = jnp.cos(angles), jnp.sin(angles), own_order(model, s_index)
        shares = [block_f[k] for k in range(plane)]
        shares = shares[:1] + [swapped(shares[k], "seq", k) for k in range(1, plane)]
        col_q, near, block_c, cos, sin, turn, *rest = meet(
            col_q, near, block_c, cos, sin, turn, *shares, *far
        )
        shares, far = rest[:plane], rest[plane:]
        xy_q = from_seq(col_q)
    if small:
        col_c = lax.all_gather(block_c, "dp", axis=0, tiled=True)
        cot_turned = turn_call(cot, turn)
    else:
        cos, sin = jnp.cos(angles), jnp.sin(angles)
        turn = jnp.eye(model, dtype=bf16)
        cot_turned = cot
    got = jnp.concatenate([near[: half + pad]] + [f[:half] for f in far], axis=0)
    other = swapped(got, "mp", 1)
    low_half = jnp.where(core == 0, got, other)
    high_half = jnp.where(core == 0, other, got)

    def whole(start, size):
        return [low_half[start : start + size], high_half[start : start + size]]

    pieces = []
    for k in range(halo, 1, -1):
        pieces += whole(half + pad + (k - 2) * half, half)
    x_ext = jnp.concatenate(pieces + whole(0, half) + [x_own], axis=0)
    flat_ext = jnp.concatenate(whole(half, pad) + [flat_own], axis=0)
    ints_prev = [near[half + pad]] + [f[half] for f in far]
    ints_prev = [p[None, : span + NEIGHBOURS].astype(jnp.int32) for p in ints_prev]
    seg_keys = jnp.concatenate([p[:, :span] for p in ints_prev[::-1]] + [seg_here], axis=1)
    seg_keys = seg_keys.reshape(-1, 1)
    lens = jnp.concatenate([ints_prev[0][:, span:], lengths], axis=0)
    before = jnp.concatenate([ints_prev[0][0, span - 1 : span], seg_here[0, : span - 1]])
    heads_of = jnp.repeat(before[::BLOCK], BLOCK)
    spot = jnp.arange(span)
    starts = jnp.where(s_index == 0, BLOCK, 0)
    keep = jnp.logical_or(spot == 0, jnp.logical_and(before == heads_of, spot >= starts))
    keep = keep.astype(f32).reshape(span, 1)

    if small:
        x_ext = turn_call(x_ext, turn)
        col_c, turn, cot_turned, cos, sin, x_ext, flat_ext, cot, *rest = meet(
            col_c, turn, cot_turned, cos, sin, x_ext, flat_ext, cot, *xy_q, *shares
        )
        xy_q, shares = rest[:3], rest[3:]
        w_feed = jnp.broadcast_to(shares[0], (plane, shard_rows, 2 * wide))
        for spot, piece in zip(spots[1:], shares[1:]):
            w_feed = put(w_feed, piece[None], (spot, 0, 0))
        w_feed = w_feed.reshape(plane * shard_rows, 2 * wide)
        lead = 3 * width
        lead_c = from_seq(col_c[:, :lead])
        flat_ext = turn_call(flat_ext, turn)
        q_pieces = [col_q] + xy_q
        s_q, s_k, s_v = (weight(q_pieces, j * width) for j in range(3))
        gain_rows = jnp.concatenate(
            [p[:, 3 * width : 3 * width + PAIR] for p in q_pieces], axis=0
        )
    else:
        full_q, full_c = (
            lax.all_gather(b, ("dp", "seq"), axis=0, tiled=True) for b in (block_q, block_c)
        )
        w_feed = exchanged(block_f.reshape(plane * shard_rows, 2 * wide), "seq")
        w_feed = lax.all_gather(w_feed, "dp", axis=0, tiled=True)
        s_q, s_k, s_v = ([(full_q, j * width)] for j in range(3))
        gain_rows = full_q[:, 3 * width :]
        c_kv, s_o, c_q, c_o = ([(full_c, j * width)] for j in (0, 2, 3, 4))
    gains = gain_rows[:, :3].T.astype(f32)
    x = x_ext[halo * span :]
    n1, q, k, v = qkv_call(x_ext, gains[:1], s_q, s_k, s_v, cos, sin, span, width)
    if small:
        rest_c = col_c[:, lead:]
        q, flat_ext, seg_keys, lens, keep, cot, rest_c, w_feed, *lead_c = meet(
            q, flat_ext, seg_keys, lens, keep, cot, rest_c, w_feed, *lead_c
        )
        w_feed = lax.all_gather(w_feed, "dp", axis=0, tiled=True)
        tail_c = from_seq(rest_c)
        c_kv, s_o = (weight([col_c] + lead_c, j * width) for j in (0, 2))
    def over_plane(own):
        return [own] + [swapped(own, "seq", k) for k in range(1, plane)]

    def with_other(pieces):
        got = jnp.concatenate(pieces, axis=0)
        return jnp.concatenate([got, swapped(got, "mp", 1)], axis=0)

    def back_to_owner(own, other):
        total = own.astype(f32) + swapped(other, "mp", 1).astype(f32)
        sent = to_low(total)
        return [total[:half]] + [
            swapped(sent[k * half : (k + 1) * half], "seq", k) for k in range(1, plane)
        ]

    def f_assembled(got):
        got = got.reshape(plane, shard_rows, 2 * wide)
        return jnp.concatenate(
            [got[k, :, at : at + spans[k]] for at in (0, wide) for k in range(plane)], axis=1
        ).astype(f32)

    attn, lse, part = self_call(q, k, v, seg_here, seg_keys, s_o, model)
    kv2 = rows_call(flat_ext, c_kv, 2 * width)
    if small:
        part, kv2, cot, *tail_c = meet(part, kv2, cot, *tail_c)
        c_q, c_o = (weight([rest_c] + tail_c, j * width) for j in (0, 1))
    cot_rows = over_plane(lax.dynamic_slice_in_dim(cot, core * half, half, 0))
    other = swapped(part, "mp", 1)
    h1, n2, q2, cross, lse2, part2 = cross_call(
        lens, x, part, other, gains[1:2], c_q, c_o, kv2, keep
    )
    if small:
        part2, *cot_rows = meet(part2, *cot_rows)
    cot_rows = with_other(cot_rows)
    other = swapped(part2, "mp", 1)
    h2, n3 = norm_call(core.reshape(1), h1, part2, other, gains[2:3], turn)

    n_rows = with_other(over_plane(n3))
    act, du, y_own, y_other, dn_own, dn_other = feed_call(n_rows, cot_rows, w_feed)
    dn3 = plane_sum(back_to_owner(dn_own, dn_other))
    dn3_other = swapped(dn3, "mp", 1)
    g2, low2, dgain3, dq2, dk2, dv2, dn2 = cross_back_call(
        lens, core.reshape(1), cot_turned, h2, dn3, dn3_other, turn, gains[2:3], c_q, c_o,
        q2, kv2, lse2, keep,
    )
    other = swapped(dn2, "mp", 1)
    def in_model_order(rows):
        high = to_low(lax.reduce_precision(rows, 8, 7))
        rest = to_low(rows - high.astype(f32))
        both = dot_t(jnp.concatenate([high, rest], axis=0), turn)
        return both[:span] + both[span:]

    cross_sent, cross_kept = halves(
        [(n2, dq2), (low2, cross)], [(flat_ext, dk2), (flat_ext, dv2)]
    )
    if small:
        *cross_sent, other, du, act = meet(*cross_sent, other, du, act)
        cross_got = reduce_first(cross_sent)
    g1, low1, dgain2, dq, dk, dv = self_back_call(
        g2, h1, dn2, other, gains[1:2], s_o, q, k, v, lse, seg_here, seg_keys, cos, sin
    )
    if small:
        *cross_got, low1, dq, dk, dv = meet(*cross_got, low1, dq, dk, dv)
        cross_kept, cross_got = reduce_second(cross_kept, cross_got)
    own, dn_mine, dn_given, dgain1 = inner_call(
        core.reshape(1), x_ext, dq, dk, dv, s_q, s_k, s_v
    )
    if small:
        dn_mine, dn_given, dgain1, dq, dk, dv, low1, *cross_got = meet(
            dn_mine, dn_given, dgain1, dq, dk, dv, low1, *cross_got
        )
    dgains = jnp.concatenate([dgain1, 0.5 * dgain2, 0.5 * dgain3], axis=0)
    if small:
        dgains = jnp.dot(dgains, turn.T.astype(f32), precision=lax.Precision.HIGHEST)
        slots = jnp.pad(
            dgains.reshape(3, -1, shard_rows).transpose(1, 0, 2),
            ((0, 0), (0, 5), (0, PAIR - shard_rows)),
        )
        slots = jnp.repeat(slots, lax.axis_size("mp"), axis=0)
    self_sent, self_kept = halves(
        [(n1[halo * span :], dq), (low1, attn)],
        [(n1, dk), (n1, dv)],
    )
    if small:
        sent_a, sent_b, slots, du, act = meet(*self_sent, slots, du, act)
        self_got = reduce_first((sent_a, sent_b))
        slots = lax.all_to_all(slots, ("dp", "seq", "mp"), 0, 0, tiled=True)
        gains_part = jnp.sum(slots, axis=0)[:3, :shard_rows]
        cross_part = lax.psum_scatter(
            last_sum_call(cross_kept, cross_got)[0], "dp", scatter_dimension=0, tiled=True
        ).astype(f32)
        feed_grads = jnp.concatenate(
            [to_low(t_dot(n_rows, du)), to_low(t_dot(cot_rows, act))], axis=1
        )
        feed_low = lax.psum_scatter(feed_grads, "dp", scatter_dimension=0, tiled=True)
        *self_got, gains_part = meet(*self_got, gains_part)
        self_kept, self_got = reduce_second(self_kept, self_got)
        *self_got, h2_model = meet(*self_got, in_model_order(h2))
        self_col, mark = last_sum_call(self_kept, self_got)
        dn_mine, dn_given, y_own, y_other, mark = meet(dn_mine, dn_given, y_own, y_other, mark)
        self_got = exchanged(self_col, "dp")
    y_sums = back_to_owner(y_own, y_other)
    summed = to_low(dn_mine + swapped(dn_given, "mp", 1))
    if small:
        summed = to_low(dot_t(summed, turn))
    summed = summed.reshape(halo, half, model)
    back_parts = [shifted(summed[halo - k], "seq", -k) for k in range(1, halo + 1)]
    if small:
        squares = jnp.sum(cross_part * cross_part) + jnp.sum(jnp.square(feed_low.astype(f32)))
        self_got, squares = meet(self_got, squares)
        self_part, self_squares = total_call(self_got, mark)
    else:
        feed_grads = jnp.concatenate(
            [to_low(t_dot(n_rows, du)), to_low(t_dot(cot_rows, act))], axis=1
        )
        feed_low = lax.psum_scatter(feed_grads, "dp", scatter_dimension=0, tiled=True)
        feed_part = f_assembled(exchanged(feed_low, "seq"))
        cross_part, self_part = reduce_plain(cross_kept), reduce_plain(self_kept)
        squares = jnp.sum(feed_part * feed_part) + jnp.sum(cross_part * cross_part)
        self_squares = jnp.sum(jnp.square(self_part)).reshape(1, 1)
    if not small:
        gain_sums = butterfly(dgains, ("mp", "seq", "dp"))
        shard = lax.axis_index("dp") * lax.axis_size("seq") + s_index
        gains_part = lax.dynamic_slice_in_dim(gain_sums, shard * shard_rows, shard_rows, axis=1)
    first_model = (core == 0).astype(f32)
    local_squares = (
        self_squares
        + squares
        + first_model * jnp.sum(gains_part * gains_part)
    )
    if small:
        shares = [take(feed_low.reshape(plane, shard_rows, 2 * wide), spot, 0) for spot in spots]
        local_squares, *rest = meet(local_squares, *y_sums, *back_parts, *shares)
        y_sums, back_parts, shares = rest[:plane], rest[plane:-plane], rest[-plane:]
        shares = shares[:1] + [swapped(shares[k], "seq", k) for k in range(1, plane)]
        feed_got = jnp.zeros((plane, shard_rows, 2 * wide), bf16)
        for spot, piece in zip(spots, shares):
            feed_got = put(feed_got, piece[None], (spot, 0, 0))
        feed_part = f_assembled(feed_got)
    grad_norm = jnp.sqrt(sum_everywhere(local_squares).reshape(()))
    factor = jnp.minimum(1.0, clip_limit / (grad_norm + 1e-06))
    scalar = factor.reshape(1)
    mixed_order, plain = (0, 2, 3, 1), (0, 1)
    y_half = plane_sum(y_sums)
    y_other = swapped(y_half, "mp", 1)
    y_all = jnp.concatenate(
        [jnp.where(core == 0, y_half, y_other), jnp.where(core == 0, y_other, y_half)], axis=0
    )
    if halo:
        back = sum(p.astype(f32) for p in back_parts)
        if small:
            back = dot(to_low(back), turn)
        own = own + put(jnp.zeros_like(own), back, (core * half, 0))
    back, _ = rms_back(x.astype(f32), gains[:1], core_sum(own))
    in_grad = g1 + back

    if small:
        in_grad = in_model_order(in_grad)
        result = to_low(h2_model + y_all)
    else:
        result = to_low(h2 + y_all)
    in_grad = in_grad.reshape(row_count, span, model)
    out = result.reshape(row_count, span, model)
    (
        self_new, self_first_new, self_second_new,
        cross_new, cross_first_new, cross_second_new,
        feed_new, feed_first_new, feed_second_new,
    ) = adam_call(
        scalar,
        [
            (self_weights, self_part, self_first, self_second, mixed_order),
            (cross_weights, cross_part, cross_first, cross_second, mixed_order),
            (feed_weights, feed_part, feed_first, feed_second, plain),
        ],
    )
    gains_new, gains_first_new, gains_second_new = adam_step(
        norm_gains, gains_part, gains_first, gains_second, factor, gain_rate, 0.0
    )
    return (
        out,
        in_grad,
        grad_norm,
        self_new,
        cross_new,
        feed_new,
        gains_new,
        self_first_new,
        cross_first_new,
        feed_first_new,
        gains_first_new,
        self_second_new,
        cross_second_new,
        feed_second_new,
        gains_second_new,
    )


def solution(mesh):
    tok = P("dp", "seq", None)
    mat = P(None, ("dp", "seq"), "mp")
    vec = P(None, ("dp", "seq"))
    in_specs = (
        tok,
        P("dp", "seq", None, None, None),
        tok,
        P("dp", "seq"),
        tok,
    ) + (mat, mat, mat, vec) * 3
    out_specs = (tok, tok, P()) + (mat, mat, mat, vec) * 3
    return jax.shard_map(
        per_device, mesh=mesh, in_specs=in_specs, out_specs=out_specs, check_vma=False
    )
```

```python
import jax
import jax.numpy as jnp
from jax import lax
from jax.experimental import pallas as pl
from jax.experimental.pallas import tpu as pltpu
from jax.sharding import PartitionSpec as P

HEAD_DIM = 64
PAIR = 128
BLOCK = 64
NEIGHBOURS = 2
NEIGH_LEN = 128
KEYS = NEIGHBOURS * NEIGH_LEN
STEP = 10
DOC_MAX = 512
CHUNK = 256
TOKENS = 512

norm_eps = 1e-05
rope_base = 10000.0
beta_one = 0.9
beta_two = 0.95
adam_eps = 1e-08
weight_decay = 0.1
learn_rate = 0.1
gain_rate = 0.5
clip_limit = 1.0
masked_fill = -1e30
score_scale = HEAD_DIM ** (-0.5)
gelu_c = 0.7978845608028654
gelu_k = 0.044715

f32 = jnp.float32
bf16 = jnp.bfloat16


def to_low(array_in):
    return array_in.astype(bf16)


def shifted(value, axis, by):
    count = lax.axis_size(axis)
    return lax.ppermute(value, axis, [(i, i + by) for i in range(count) if 0 <= i + by < count])


def rotated(value, axis, by):
    count = lax.axis_size(axis)
    return lax.ppermute(value, axis, [(i, (i + by) % count) for i in range(count)])


def swapped(value, axis, by):
    count = lax.axis_size(axis)
    return lax.ppermute(value, axis, [(i, i ^ by) for i in range(count)])


def butterfly(value, axes):
    for axis in axes:
        step = 1
        while step < lax.axis_size(axis):
            value = value + swapped(value, axis, step)
            step *= 2
    return value


def sum_everywhere(value):
    axes = ("dp", "seq", "mp")
    if not small_mesh():
        return butterfly(value, axes)
    count = lax.axis_size("dp") * lax.axis_size("seq") * lax.axis_size("mp")
    spread = jnp.broadcast_to(value, (count, 8, PAIR))
    return jnp.sum(lax.all_to_all(spread, axes, 0, 0, tiled=True)[:, :1, :1], axis=0)


def core_sum(partial_out):
    return partial_out + swapped(partial_out, "mp", 1)


def small_mesh():
    return lax.axis_size("dp") == 4 and lax.axis_size("seq") == 4


def put(buffer, piece, starts):
    return lax.dynamic_update_slice(buffer, piece, starts)


def meet(*values):
    return lax.optimization_barrier(values)


ORDER = (0, 2, 1, 3)


def own_order(model, s):
    rows = model // 16
    spot = jnp.arange(model)
    near, z, inner = spot // (4 * rows), spot // rows % 4, spot % rows
    flip = (near % 2) * 2 + near // 2
    source = (z * 4 + (s ^ flip)) * rows + inner
    return (spot[:, None] == source[None, :]).astype(bf16)


def plane_sum(pieces):
    return (pieces[0] + pieces[1].astype(f32)) + (pieces[2].astype(f32) + pieces[3].astype(f32))


def take(array_in, index, axis):
    return lax.dynamic_index_in_dim(array_in, index, axis, keepdims=False)


def wide_for_dp(block):
    rows, cols = block.shape
    return jnp.broadcast_to(block[None], (4, rows, cols)).reshape(4 * rows, cols)


def exchanged(array_in, axis):
    return lax.all_to_all(array_in, axis, 0, 0, tiled=True)


def from_seq(column):
    return [swapped(column, "seq", k) for k in ORDER[1:]]


def weight(pieces, start):
    return [(p, start) for p in pieces]


def reduce_first(sent):
    return swapped(sent[0], "seq", 1), swapped(sent[1], "seq", 2)


def reduce_second(kept, got):
    sent_a, sent_b = half_sum_call(kept, got)
    return (*kept, *got), (swapped(sent_a, "seq", 2), swapped(sent_b, "seq", 1))


def reduce_last(got):
    rows, cols = got.shape
    return jnp.sum(got.reshape(4, rows // 4, cols).astype(f32), axis=0)


def reduce_plain(grads):
    return lax.psum_scatter(
        jnp.concatenate(grads, axis=1), ("dp", "seq"), scatter_dimension=0, tiled=True
    ).astype(f32)


def halves(left, right):
    if not small_mesh():
        return None, [jnp.concatenate([to_low(t_dot(a, b)) for a, b in left + right], axis=1)]

    def products(pairs, pick):
        parts = [to_low(t_dot(pick(a), b)) for a, b in pairs]
        return parts[0] if len(parts) == 1 else jnp.concatenate(parts, axis=1)

    def second(a, first):
        quarter = a.shape[1] // 4
        return jnp.concatenate(
            [
                a[:, first * quarter : (first + 1) * quarter],
                a[:, (first + 2) * quarter : (first + 3) * quarter],
            ],
            axis=1,
        )

    mid = left[0][0].shape[1] // 2
    sent = (products(left, lambda a: a[:, mid:]), products(right, lambda a: second(a, 1)))
    kept = (products(left, lambda a: a[:, :mid]), products(right, lambda a: second(a, 0)))
    return sent, kept


def adam_step(weight, gradient, first_old, second_old, factor, step_rate, decay_coef):
    clipped = gradient * factor
    first_new = beta_one * first_old + (1.0 - beta_one) * clipped
    second_new = beta_two * second_old + (1.0 - beta_two) * clipped * clipped
    first_hat = first_new / (1.0 - beta_one**STEP)
    second_hat = second_new / (1.0 - beta_two**STEP)
    weight_new = weight - step_rate * (
        first_hat / (jnp.sqrt(second_hat) + adam_eps) + decay_coef * weight
    )
    return (weight_new, first_new, second_new)


def call(kernel, grid, ins, outs, args, scratch=(), prefetch=0):
    specs, flat, counts = [], list(args[:prefetch]), [1] * prefetch
    for (shape, index), arg in zip(ins, args[prefetch:]):
        if not isinstance(arg, list):
            specs.append(pl.BlockSpec(shape, index))
            flat.append(arg)
            counts.append(1)
            continue
        for array_in, start in arg:
            place = lambda *ids, at=start // shape, f=index: (0, f(ids[0]) + at)
            specs.append(pl.BlockSpec((array_in.shape[0], shape), place))
            flat.append(array_in)
        counts.append(-len(arg))

    def body(*refs):
        refs, grouped = list(refs), []
        for count in counts:
            grouped.append(refs.pop(0) if count > 0 else [refs.pop(0) for _ in range(-count)])
        kernel(*grouped, *refs)

    return pl.pallas_call(
        body,
        out_shape=[jax.ShapeDtypeStruct(o[2], o[3]) for o in outs],
        grid_spec=pltpu.PrefetchScalarGridSpec(
            num_scalar_prefetch=prefetch,
            grid=grid,
            in_specs=specs,
            out_specs=[pl.BlockSpec(o[0], o[1]) for o in outs],
            scratch_shapes=list(scratch),
        ),
        compiler_params=pltpu.CompilerParams(
            dimension_semantics=("arbitrary",) * len(grid), vmem_limit_bytes=56 << 20
        ),
        name=kernel.__name__,
    )(*flat)


def whole_weight(refs):
    pieces = [r[...] for r in refs]
    return pieces[0] if len(pieces) == 1 else jnp.concatenate(pieces, axis=0)


first_block = lambda i: 0
each_block = lambda i: i


def dot(a, b):
    return jnp.dot(a, b, preferred_element_type=f32)


def dot_t(a, b):
    return lax.dot_general(a, b, (((1,), (1,)), ((), ())), preferred_element_type=f32)


def t_dot(a, b):
    return lax.dot_general(a, b, (((0,), (0,)), ((), ())), preferred_element_type=f32)


def rms_factor(z):
    return lax.rsqrt(jnp.mean(z * z, axis=-1, keepdims=True) + norm_eps)


def rms_back(z, gain, grad):
    factor = rms_factor(z)
    scaled = grad * gain
    inner = jnp.mean(scaled * z, axis=-1, keepdims=True)
    return factor * scaled - z * (factor * factor * factor * inner), grad * z * factor


def lane_in_head(shape):
    return lax.broadcasted_iota(jnp.int32, shape, 1)


def rope(z, cos, sin, sign):
    lane = lane_in_head(z.shape)
    lead = lane % HEAD_DIM < HEAD_DIM // 2
    partner = jnp.where(lead, -pltpu.roll(z, PAIR - 32, 1), pltpu.roll(z, 32, 1))
    return z * cos + partner * (sin * sign)


def split_heads(z):
    first = lane_in_head(z.shape) < HEAD_DIM
    zero = jnp.zeros_like(z)
    return jnp.where(first, z, zero), jnp.where(first, zero, z)


def join_heads(a, b):
    return jnp.where(lane_in_head(a.shape) < HEAD_DIM, a, b)


def qkv_kernel(x_ref, g_ref, wq, wk, wv, cos_ref, sin_ref, n_ref, q_ref, k_ref, v_ref):
    rows, span = n_ref.shape[0], q_ref.shape[0]

    @pl.when(pl.program_id(0) == 0)
    def _():
        x = x_ref[...].astype(f32)
        n_ref[...] = to_low(x * rms_factor(x) * g_ref[...])

    normed, cos, sin = n_ref[...], cos_ref[...], sin_ref[...]

    def turned(raw, cos, sin):
        return jnp.concatenate(
            [
                to_low(rope(raw[:, c : c + PAIR], cos, sin, 1.0))
                for c in range(0, raw.shape[1], PAIR)
            ],
            axis=1,
        )

    k_ref[...] = turned(dot(normed, whole_weight(wk)), cos, sin)
    v_ref[...] = to_low(dot(normed, whole_weight(wv)))
    own = rows - span
    q_ref[...] = turned(dot(normed[own:], whole_weight(wq)), cos[own:], sin[own:])


def qkv_call(x_ext, gain, wq, wk, wv, cos, sin, span, width):
    rows, model = x_ext.shape
    fix = lambda i: (0, 0)
    col = lambda i: (0, i)
    return call(
        qkv_kernel,
        (width // CHUNK,),
        [
            ((rows, model), fix),
            ((1, model), fix),
            (CHUNK, each_block),
            (CHUNK, each_block),
            (CHUNK, each_block),
            ((rows, PAIR), fix),
            ((rows, PAIR), fix),
        ],
        [
            ((rows, model), fix, (rows, model), bf16),
            ((span, CHUNK), col, (span, width), bf16),
            ((rows, CHUNK), col, (rows, width), bf16),
            ((rows, CHUNK), col, (rows, width), bf16),
        ],
        (x_ext, gain, wq, wk, wv, cos, sin),
    )


def self_bias(segq_ref, segk_ref, bias_ref):
    keys, span = bias_ref.shape
    key_pos = lax.broadcasted_iota(jnp.int32, (keys, span), 0) - (keys - span)
    query_pos = lax.broadcasted_iota(jnp.int32, (keys, span), 1)
    ok = jnp.logical_and(key_pos <= query_pos, segk_ref[...] == segq_ref[...])
    bias_ref[...] = jnp.where(ok, 0.0, masked_fill)


def self_kernel(q_ref, k_ref, v_ref, segq_ref, segk_ref, wo, o_ref, lse_ref, part_ref, bias_ref):
    @pl.when(pl.program_id(0) == 0)
    def _():
        self_bias(segq_ref, segk_ref, bias_ref)
        part_ref[...] = jnp.zeros_like(part_ref)

    k, v, bias = k_ref[...], v_ref[...], bias_ref[...]
    outs, lses = [], []
    for qh in split_heads(q_ref[...] * score_scale):
        s = dot_t(k, qh) + bias
        top = jnp.max(s, axis=0, keepdims=True)
        e = jnp.exp(s - top)
        total = jnp.sum(e, axis=0, keepdims=True)
        lses.append(top + jnp.log(total))
        outs.append(t_dot(to_low(e * (1.0 / total)), v))
    o = to_low(join_heads(outs[0], outs[1]))
    o_ref[...] = o
    lse_ref[0] = jnp.concatenate(lses, axis=0)
    part_ref[...] += dot_t(o, whole_weight(wo))


def self_call(q, k, v, segq, segk, wo, model):
    span, width = q.shape
    keys = k.shape[0]
    pair = lambda p: (0, p)
    fix = lambda p: (0, 0)
    return call(
        self_kernel,
        (width // PAIR,),
        [
            ((span, PAIR), pair),
            ((keys, PAIR), pair),
            ((keys, PAIR), pair),
            ((1, span), fix),
            ((keys, 1), fix),
            (PAIR, each_block),
        ],
        [
            ((span, PAIR), pair, (span, width), bf16),
            ((1, 2, span), lambda p: (p, 0, 0), (width // PAIR, 2, span), f32),
            ((span, model), fix, (span, model), f32),
        ],
        (q, k, v, segq, segk, wo),
        scratch=[pltpu.VMEM((keys, span), f32)],
    )


def block_bias(len_ref, block):
    key = lax.broadcasted_iota(jnp.int32, (KEYS, PAIR), 0)
    limit = jnp.where(key < NEIGH_LEN, len_ref[block, 0], len_ref[block, 1])
    return jnp.where(key % NEIGH_LEN < limit, 0.0, masked_fill)


def tile_bias(len_ref, tile, tiles):
    if tile:
        return block_bias(len_ref, tile)
    first = lax.broadcasted_iota(jnp.int32, (KEYS, PAIR), 1) % BLOCK == 0
    lead = jnp.where(first, masked_fill, block_bias(len_ref, 0))
    last = jnp.where(first, block_bias(len_ref, tiles), masked_fill)
    return jnp.concatenate([lead, last], axis=0)


def stack_heads(z):
    return jnp.concatenate(split_heads(z), axis=0)


def merge_heads(z):
    return join_heads(z[:BLOCK], z[BLOCK:])


def tile_keys(ref, tile, tiles):
    own = ref[tile * KEYS : (tile + 1) * KEYS, :]
    if tile:
        return own
    return jnp.concatenate([own, ref[tiles * KEYS : (tiles + 1) * KEYS, :]], axis=0)


def cross_kernel(
    len_ref, x_ref, pa_ref, pb_ref, g_ref, wq, k_ref, v_ref, keep_ref, wo,
    h_ref, n_ref, q_ref, o_ref, lse_ref, part_ref, acc_ref,
):
    span = x_ref.shape[0]
    tiles = span // BLOCK

    @pl.when(pl.program_id(0) == 0)
    def _():
        h = x_ref[...].astype(f32) + (pa_ref[...] + pb_ref[...])
        h_ref[...] = h
        n_ref[...] = to_low(h * rms_factor(h) * g_ref[...])
        part_ref[...] = jnp.zeros_like(part_ref)

    turned = pltpu.roll(to_low(dot(n_ref[...], whole_weight(wq))).astype(f32), 1, 0)
    q = to_low(turned * score_scale)
    q_ref[...] = q
    for tile in range(tiles):
        rows = slice(tile * BLOCK, (tile + 1) * BLOCK)
        k, v = tile_keys(k_ref, tile, tiles), tile_keys(v_ref, tile, tiles)
        sc = dot_t(k, stack_heads(q[rows])) + tile_bias(len_ref, tile, tiles)
        top = jnp.max(sc, axis=0, keepdims=True)
        e = jnp.exp(sc - top)
        total = jnp.sum(e, axis=0, keepdims=True)
        lse_ref[0, tile : tile + 1, :] = top + jnp.log(total)
        acc_ref[rows, :] = merge_heads(t_dot(to_low(e * (1.0 / total)), v))
    o = to_low(pltpu.roll(acc_ref[...] * keep_ref[...], span - 1, 0))
    o_ref[...] = o
    part_ref[...] += dot_t(o, whole_weight(wo))


def cross_call(lens, x, pa, pb, gain, wq, wo, kv2, keep):
    span, model = x.shape
    keys, width = kv2.shape[0], kv2.shape[1] // 2
    pairs = width // PAIR
    pair = lambda p, *_: (0, p)
    fix = lambda p, *_: (0, 0)
    return call(
        cross_kernel,
        (pairs,),
        [
            ((span, model), fix),
            ((span, model), fix),
            ((span, model), fix),
            ((1, model), fix),
            (PAIR, each_block),
            ((keys, PAIR), pair),
            ((keys, PAIR), lambda p, *_: (0, pairs + p)),
            ((span, 1), fix),
            (PAIR, each_block),
        ],
        [
            ((span, model), fix, (span, model), f32),
            ((span, model), fix, (span, model), bf16),
            ((span, PAIR), pair, (span, width), bf16),
            ((span, PAIR), pair, (span, width), bf16),
            ((1, span // BLOCK, PAIR), lambda p, *_: (p, 0, 0), (pairs, span // BLOCK, PAIR), f32),
            ((span, model), fix, (span, model), f32),
        ],
        (lens, x, pa, pb, gain, wq, kv2, kv2, keep, wo),
        scratch=[pltpu.VMEM((span, PAIR), f32)],
        prefetch=1,
    )


def gelu_and_slope(u):
    t = jnp.tanh(gelu_c * (u + gelu_k * (u * u * u)))
    slope = 0.5 * (1.0 + t) + 0.5 * u * (1.0 - t * t) * (gelu_c * (1.0 + 3.0 * gelu_k * (u * u)))
    return to_low(0.5 * u * (1.0 + t)), slope


def norm_kernel(core_ref, h1_ref, pa_ref, pb_ref, g_ref, turn_ref, h_ref, n_ref):
    h = h1_ref[...] + (pa_ref[...] + pb_ref[...])
    h_ref[...] = h
    normed = to_low(h * rms_factor(h) * g_ref[...])
    rows = n_ref.shape[0]
    mine = jnp.where(core_ref[0] == 0, normed[:rows], normed[rows:])
    n_ref[...] = to_low(dot_t(mine, turn_ref[...]))


def norm_call(core, h1, pa, pb, gain, turn):
    span, model = h1.shape
    fix = lambda i, *_: (0, 0)
    whole = ((span, model), fix)
    return call(
        norm_kernel,
        (1,),
        [whole, whole, whole, ((1, model), fix), ((model, model), fix)],
        [
            ((span, model), fix, (span, model), f32),
            ((span // 2, model), fix, (span // 2, model), bf16),
        ],
        (core, h1, pa, pb, gain, turn),
        prefetch=1,
    )


def feed_kernel(n_ref, cot_ref, up_ref, down_ref, act_ref, du_ref, ya_ref, yb_ref, da_ref, db_ref):
    up, down = up_ref[...], down_ref[...]
    act, slope = gelu_and_slope(dot(n_ref[...], up))
    du = to_low(dot(cot_ref[...], down) * slope)
    act_ref[...] = act
    du_ref[...] = du
    y, dn = dot_t(act, down), dot_t(du, up)
    step = pl.program_id(0)
    half = pl.num_programs(0) // 2

    @pl.when(step < half)
    def _():
        ya_ref[...] = to_low(y)
        da_ref[...] = dn

    @pl.when(step >= half)
    def _():
        yb_ref[...] = to_low(y)
        db_ref[...] = dn


def feed_call(n, cot, w_feed):
    rows, model = n.shape
    hidden = w_feed.shape[1] // 2
    half = rows // TOKENS // 2
    row = lambda i: (i, 0)
    lead = lambda i: (jnp.minimum(i, half - 1), 0)
    tail = lambda i: (jnp.maximum(i - half, 0), 0)
    block = (TOKENS, model)
    part = (rows // 2, model)
    return call(
        feed_kernel,
        (rows // TOKENS,),
        [
            (block, row),
            (block, row),
            ((model, hidden), lambda i: (0, 0)),
            ((model, hidden), lambda i: (0, 1)),
        ],
        [
            ((TOKENS, hidden), row, (rows, hidden), bf16),
            ((TOKENS, hidden), row, (rows, hidden), bf16),
            (block, lead, part, bf16),
            (block, tail, part, bf16),
            (block, lead, part, f32),
            (block, tail, part, f32),
        ],
        (n, cot, w_feed, w_feed),
    )


def cross_back_kernel(
    len_ref, core_ref, base_ref, h_ref, da_ref, db_ref, turn_ref, g_ref, wo, q_ref, k_ref, v_ref, lse_ref,
    keep_ref, wq,
    grad_ref, low_ref, gain_ref, dq_ref, dk_ref, dv_ref, dn_ref, acc_ref,
):
    span = h_ref.shape[0]
    tiles = span // BLOCK

    @pl.when(pl.program_id(0) == 0)
    def _():
        first, other = da_ref[...], db_ref[...]
        given = jnp.where(
            core_ref[0] == 0,
            jnp.concatenate([first, other], axis=0),
            jnp.concatenate([other, first], axis=0),
        )
        high = to_low(given)
        low = to_low(given - high.astype(f32))
        turn = turn_ref[...]
        back, gains = rms_back(h_ref[...], g_ref[...], dot(high, turn) + dot(low, turn))
        grad = base_ref[...].astype(f32) + back
        grad_ref[...] = grad
        low_ref[...] = to_low(grad)
        gain_ref[...] = jnp.sum(gains, axis=0, keepdims=True)
        dn_ref[...] = jnp.zeros_like(dn_ref)

    do = to_low(dot(low_ref[...], whole_weight(wo))).astype(f32)
    do = to_low(pltpu.roll(do, 1, 0) * keep_ref[...])
    q = q_ref[...]
    for tile in range(tiles):
        rows = slice(tile * BLOCK, (tile + 1) * BLOCK)
        k, v = tile_keys(k_ref, tile, tiles), tile_keys(v_ref, tile, tiles)
        qs, dos = stack_heads(q[rows]), stack_heads(do[rows])
        p = jnp.exp(dot_t(k, qs) + tile_bias(len_ref, tile, tiles) - lse_ref[0, tile : tile + 1, :])
        dp = dot_t(v, dos)
        ds = to_low(p * (dp - jnp.sum(p * dp, axis=0, keepdims=True)))
        acc_ref[rows, :] = merge_heads(t_dot(ds, k))
        dk = to_low(dot(ds, qs))
        dv = to_low(dot(to_low(p), dos))
        own = slice(tile * KEYS, (tile + 1) * KEYS)
        dk_ref[own, :] = dk[:KEYS]
        dv_ref[own, :] = dv[:KEYS]
        if not tile:
            last = slice(tiles * KEYS, (tiles + 1) * KEYS)
            dk_ref[last, :] = dk[KEYS:]
            dv_ref[last, :] = dv[KEYS:]
    dq = to_low(pltpu.roll(acc_ref[...] * score_scale, span - 1, 0))
    dq_ref[...] = dq
    dn_ref[...] += dot_t(dq, whole_weight(wq))


def cross_back_call(lens, core, base, h, da, db, turn, gain, wq, wo, q, kv2, lse, keep):
    span, model = h.shape
    keys, width = kv2.shape[0], kv2.shape[1] // 2
    pairs = width // PAIR
    pair = lambda p, *_: (0, p)
    fix = lambda p, *_: (0, 0)
    return call(
        cross_back_kernel,
        (pairs,),
        [
            ((span, model), fix),
            ((span, model), fix),
            ((span // 2, model), fix),
            ((span // 2, model), fix),
            ((model, model), fix),
            ((1, model), fix),
            (PAIR, each_block),
            ((span, PAIR), pair),
            ((keys, PAIR), pair),
            ((keys, PAIR), lambda p, *_: (0, pairs + p)),
            ((1, span // BLOCK, PAIR), lambda p, *_: (p, 0, 0)),
            ((span, 1), fix),
            (PAIR, each_block),
        ],
        [
            ((span, model), fix, (span, model), f32),
            ((span, model), fix, (span, model), bf16),
            ((1, model), fix, (1, model), f32),
            ((span, PAIR), pair, (span, width), bf16),
            ((keys, PAIR), pair, (keys, width), bf16),
            ((keys, PAIR), pair, (keys, width), bf16),
            ((span, model), fix, (span, model), f32),
        ],
        (lens, core, base, h, da, db, turn, gain, wo, q, kv2, kv2, lse, keep, wq),
        scratch=[pltpu.VMEM((span, PAIR), f32)],
        prefetch=2,
    )


def self_back_kernel(
    base_ref, h_ref, da_ref, db_ref, g_ref, wo, q_ref, k_ref, v_ref, lse_ref, segq_ref,
    segk_ref, cos_ref, sin_ref,
    grad_ref, low_ref, gain_ref, dq_ref, dk_ref, dv_ref, bias_ref,
):
    span = h_ref.shape[0]
    keys = k_ref.shape[0]

    @pl.when(pl.program_id(0) == 0)
    def _():
        back, gains = rms_back(h_ref[...], g_ref[...], da_ref[...] + db_ref[...])
        grad = base_ref[...] + back
        grad_ref[...] = grad
        low_ref[...] = to_low(grad)
        gain_ref[...] = jnp.sum(gains, axis=0, keepdims=True)
        self_bias(segq_ref, segk_ref, bias_ref)

    do = to_low(dot(low_ref[...], whole_weight(wo)))
    k, v, bias = k_ref[...], v_ref[...], bias_ref[...]
    qs, dos = split_heads(q_ref[...] * score_scale), split_heads(do)
    dqs, dk, dv = [], 0.0, 0.0
    for h in range(2):
        p = jnp.exp(dot_t(k, qs[h]) + bias - lse_ref[0, h : h + 1, :])
        dp = dot_t(v, dos[h])
        ds = to_low(p * (dp - jnp.sum(p * dp, axis=0, keepdims=True)))
        dqs.append(t_dot(ds, k))
        dk = dk + dot(ds, qs[h])
        dv = dv + dot(to_low(p), dos[h])
    cos, sin = cos_ref[...], sin_ref[...]
    dq = join_heads(dqs[0], dqs[1]) * score_scale
    dq_ref[...] = to_low(rope(dq, cos[keys - span :], sin[keys - span :], -1.0))
    dk_ref[...] = to_low(rope(dk, cos, sin, -1.0))
    dv_ref[...] = to_low(dv)


def self_back_call(base, h, da, db, gain, wo, q, k, v, lse, segq, segk, cos, sin):
    span, model = h.shape
    keys, width = k.shape
    pair = lambda p: (0, p)
    fix = lambda p: (0, 0)
    return call(
        self_back_kernel,
        (width // PAIR,),
        [
            ((span, model), fix),
            ((span, model), fix),
            ((span, model), fix),
            ((span, model), fix),
            ((1, model), fix),
            (PAIR, each_block),
            ((span, PAIR), pair),
            ((keys, PAIR), pair),
            ((keys, PAIR), pair),
            ((1, 2, span), lambda p: (p, 0, 0)),
            ((1, span), fix),
            ((keys, 1), fix),
            ((keys, PAIR), fix),
            ((keys, PAIR), fix),
        ],
        [
            ((span, model), fix, (span, model), f32),
            ((span, model), fix, (span, model), bf16),
            ((1, model), fix, (1, model), f32),
            ((span, PAIR), pair, (span, width), bf16),
            ((keys, PAIR), pair, (keys, width), bf16),
            ((keys, PAIR), pair, (keys, width), bf16),
        ],
        (base, h, da, db, gain, wo, q, k, v, lse, segq, segk, cos, sin),
        scratch=[pltpu.VMEM((keys, span), f32)],
    )


def inner_kernel(
    core_ref, x_ref, dq_ref, dk_ref, dv_ref, wq, wk, wv,
    own_ref, mine_ref, other_ref, gain_ref, dn_ref,
):
    step = pl.program_id(0)
    rows, span = x_ref.shape[0], dq_ref.shape[0]
    own, half = rows - span, span // 2
    dn = dot_t(dk_ref[...], whole_weight(wk)) + dot_t(dv_ref[...], whole_weight(wv))
    dn_own = dot_t(dq_ref[...], whole_weight(wq))

    @pl.when(step == 0)
    def _():
        dn_ref[...] = dn
        dn_ref[own:, :] += dn_own

    @pl.when(step > 0)
    def _():
        dn_ref[...] += dn
        dn_ref[own:, :] += dn_own

    @pl.when(step == pl.num_programs(0) - 1)
    def _():
        x = x_ref[...].astype(f32)
        gain_ref[...] = jnp.sum(dn_ref[...] * x * rms_factor(x), axis=0, keepdims=True)
        own_ref[...] = dn_ref[own:, :]
        core = core_ref[0]
        for k in range(own // span):
            spot = slice(k * half, (k + 1) * half)
            mine = pl.multiple_of(k * span + core * half, half)
            other = pl.multiple_of(k * span + (1 - core) * half, half)
            mine_ref[spot, :] = dn_ref[pl.ds(mine, half), :]
            other_ref[spot, :] = dn_ref[pl.ds(other, half), :]


def inner_call(core, x_ext, dq, dk, dv, wq, wk, wv):
    rows, model = x_ext.shape
    span, width = dq.shape
    fix = lambda i, *_: (0, 0)
    col = lambda i, *_: (0, i)
    part = ((rows - span) // 2, model)
    return call(
        inner_kernel,
        (width // CHUNK,),
        [
            ((rows, model), fix),
            ((span, CHUNK), col),
            ((rows, CHUNK), col),
            ((rows, CHUNK), col),
            (CHUNK, each_block),
            (CHUNK, each_block),
            (CHUNK, each_block),
        ],
        [
            ((span, model), fix, (span, model), f32),
            (part, fix, part, f32),
            (part, fix, part, f32),
            ((1, model), fix, (1, model), f32),
        ],
        (core, x_ext, dq, dk, dv, wq, wk, wv),
        scratch=[pltpu.VMEM((rows, model), f32)],
        prefetch=1,
    )


def adam_call(factor, groups):
    orders = [g[4] for g in groups]
    counts = len(groups)

    def adam_kernel(factor_ref, *refs):
        ins, outs = refs[: 4 * counts], refs[4 * counts :]
        for n, order in enumerate(orders):
            w_ref, g_ref, m_ref, v_ref = ins[4 * n : 4 * n + 4]
            wo_ref, mo_ref, vo_ref = outs[3 * n : 3 * n + 3]
            width = w_ref.shape[2]
            for j, at in enumerate(order):
                wo_ref[j], mo_ref[j], vo_ref[j] = adam_step(
                    w_ref[j],
                    g_ref[:, at * width : (at + 1) * width],
                    m_ref[j],
                    v_ref[j],
                    factor_ref[0],
                    learn_rate,
                    weight_decay,
                )

    def whole(a):
        return (a.shape, lambda i, *_, n=a.ndim: (0,) * n)

    arrays = [a for g in groups for a in g[:4]]
    results = [whole(g[0]) + (g[0].shape, f32) for g in groups for _ in range(3)]
    return call(
        adam_kernel, (1,), [whole(a) for a in arrays], results, (factor, *arrays), prefetch=1
    )


def last_sum_kernel(ka, kb, ga, gb, ra, rb, o_ref, mark_ref):
    mark_ref[...] = jnp.zeros_like(mark_ref)
    wide = ka.shape[1]
    o_ref[:, :wide] = to_low((ka[...].astype(f32) + ga[...].astype(f32)) + ra[...].astype(f32))
    o_ref[:, wide:] = to_low((kb[...].astype(f32) + gb[...].astype(f32)) + rb[...].astype(f32))


def last_sum_call(held, got):
    (rows, wide_a), wide_b = got[0].shape, got[1].shape[1]
    fix = lambda i: (0, 0)
    a, b, o = (rows, wide_a), (rows, wide_b), (rows, wide_a + wide_b)
    return call(
        last_sum_kernel,
        (1,),
        [(a, fix), (b, fix)] * 3,
        [(o, fix, o, bf16), ((8, PAIR), fix, (8, PAIR), f32)],
        (*held, *got),
    )


def total_kernel(got_ref, mark_ref, o_ref, squares_ref):
    rows = o_ref.shape[0]
    total = got_ref[:rows].astype(f32)
    for k in range(1, 4):
        total = total + got_ref[k * rows : (k + 1) * rows].astype(f32)
    o_ref[...] = total
    squares_ref[...] = jnp.sum(jnp.sum(total * total, axis=0, keepdims=True), axis=1, keepdims=True)


def total_call(got, mark):
    rows, cols = got.shape
    fix = lambda i: (0, 0)
    out = (rows // 4, cols)
    return call(
        total_kernel, (1,), [((rows, cols), fix), ((8, PAIR), fix)],
        [(out, fix, out, f32), ((1, 1), fix, (1, 1), f32)], (got, mark),
    )


def half_sum_kernel(ka, ga, kb, gb, out_a, out_b):
    out_a[...] = to_low(ka[...].astype(f32) + ga[...].astype(f32))
    out_b[...] = to_low(kb[...].astype(f32) + gb[...].astype(f32))


def half_sum_call(kept, got):
    rows, (wide_a, wide_b) = kept[0].shape[0] // 2, (k.shape[1] for k in kept)
    half = lambda i: (1, 0)
    fix = lambda i: (0, 0)
    a, b = (rows, wide_a), (rows, wide_b)
    return call(
        half_sum_kernel,
        (1,),
        [(a, half), (a, half), (b, half), (b, half)],
        [(a, fix, a, bf16), (b, fix, b, bf16)],
        (kept[0], got[0], kept[1], got[1]),
    )


def pack_call(place, own, cross, feed, gain_cols, firsts, spans, wide):
    _, rows, width = own.shape
    plane = len(spans)

    def pack_kernel(place_ref, own_ref, cross_ref, feed_ref, gain_ref, q_ref, c_ref, f_ref):
        for j in range(3):
            q_ref[:, j * width : (j + 1) * width] = to_low(own_ref[j])
        q_ref[:, 3 * width :] = to_low(gain_ref[...])
        for j, part in enumerate((cross_ref[1], cross_ref[2], own_ref[3], cross_ref[0], cross_ref[3])):
            c_ref[:, j * width : (j + 1) * width] = to_low(part)
        for k in range(plane):
            pieces = []
            for m in range(2):
                pieces.append(to_low(feed_ref[m, :, firsts[k] : firsts[k] + spans[k]]))
                if spans[k] < wide:
                    pieces.append(jnp.zeros((rows, wide - spans[k]), bf16))
            f_ref[place_ref[k]] = jnp.concatenate(pieces, axis=1)

    whole = lambda a: (a.shape, lambda i, *_: (0,) * a.ndim)
    outs = [(rows, 3 * width + PAIR), (rows, 5 * width), (plane, rows, 2 * wide)]
    return call(
        pack_kernel,
        (1,),
        [whole(own), whole(cross), whole(feed), whole(gain_cols)],
        [(o, lambda i, *_, n=len(o): (0,) * n, o, bf16) for o in outs],
        (place, own, cross, feed, gain_cols),
        prefetch=1,
    )


def rows_kernel(a_ref, w, o_ref):
    o_ref[...] = to_low(dot(a_ref[...], whole_weight(w)))


def rows_call(a, w, width):
    rows, model = a.shape
    block = CHUNK if width % CHUNK == 0 else width // 7 if width % 7 == 0 else width
    return call(
        rows_kernel,
        (width // block,),
        [((rows, model), lambda i: (0, 0)), (block, each_block)],
        [((rows, block), lambda i: (0, i), (rows, width), bf16)],
        (a, w),
    )[0]


def turn_call(a, turn):
    rows, model = a.shape
    return call(
        turn_kernel,
        (rows // KEYS,),
        [((KEYS, model), lambda i: (i, 0)), ((model, model), lambda i: (0, 0))],
        [((KEYS, model), lambda i: (i, 0), (rows, model), bf16)],
        (a, turn),
    )[0]


def turn_kernel(a_ref, t_ref, o_ref):
    o_ref[...] = to_low(dot(a_ref[...], t_ref[...]))


def per_device(
    tokens,
    neighbours,
    neighbour_lengths,
    segment_ids,
    out_grad,
    self_weights,
    cross_weights,
    feed_weights,
    norm_gains,
    self_first,
    cross_first,
    feed_first,
    gains_first,
    self_second,
    cross_second,
    feed_second,
    gains_second,
):
    row_count, span, model = tokens.shape
    width = self_weights.shape[2]
    hidden = feed_weights.shape[2]
    shard_rows = self_weights.shape[1]
    pairs = width // PAIR
    blocks = span // BLOCK
    halo = min(-(-(DOC_MAX - 1) // span), lax.axis_size("seq") - 1)
    s_index = lax.axis_index("seq")
    core = lax.axis_index("mp")

    def columns(*parts):
        return jnp.concatenate([to_low(p) for p in parts], axis=1)

    gain_cols = jnp.zeros((shard_rows, PAIR), f32).at[:, :3].set(norm_gains.T)
    small = small_mesh()
    x_own, cot = tokens.reshape(span, model), out_grad.reshape(span, model)
    flat_own = neighbours.reshape(-1, model)
    half, pad = span // 2, KEYS // 2
    seg_here = segment_ids.reshape(1, span) + 1
    lengths = neighbour_lengths.reshape(blocks, NEIGHBOURS)
    ints = jnp.concatenate([seg_here[0], lengths[-1]]).astype(bf16)
    ints = jnp.zeros((8, model), bf16).at[0, : span + NEIGHBOURS].set(ints)
    mine = lax.dynamic_slice_in_dim(x_own, core * half, half, 0)
    edge = lax.dynamic_slice_in_dim(flat_own, flat_own.shape[0] - KEYS + core * pad, pad, 0)
    frequency = rope_base ** (-(jnp.arange(PAIR) % (HEAD_DIM // 2)).astype(f32) / (HEAD_DIM // 2))
    places = (s_index - halo) * span + jnp.arange((halo + 1) * span)
    angles = places.astype(f32)[:, None] * frequency[None, :]

    plane = lax.axis_size("seq")
    groups = hidden // PAIR
    wide = -(-groups // plane) * PAIR
    spans = [(groups + plane - 1 - k) // plane * PAIR for k in range(plane)]
    firsts = [sum(spans[:k]) for k in range(plane)]

    small = small_mesh()
    places_of = [s_index ^ k if small else k for k in range(plane)]
    block_q, block_c, block_f = pack_call(
        jnp.stack([jnp.asarray(p, jnp.int32) for p in places_of]),
        self_weights, cross_weights, feed_weights, gain_cols, firsts, spans, wide,
    )
    near = shifted(jnp.concatenate([mine, edge, ints], axis=0), "seq", 1)
    far = [shifted(jnp.concatenate([mine, ints], axis=0), "seq", k) for k in range(2, halo + 1)]
    if small:
        col_q = exchanged(wide_for_dp(block_q), "dp")
        spots = [s_index ^ k for k in range(plane)]
        cos, sin, turn = jnp.cos(angles), jnp.sin(angles), own_order(model, s_index)
        shares = [block_f[k] for k in range(plane)]
        shares = shares[:1] + [swapped(shares[k], "seq", k) for k in range(1, plane)]
        col_q, near, block_c, cos, sin, turn, *rest = meet(
            col_q, near, block_c, cos, sin, turn, *shares, *far
        )
        shares, far = rest[:plane], rest[plane:]
        xy_q = from_seq(col_q)
    if small:
        col_c = lax.all_gather(block_c, "dp", axis=0, tiled=True)
        cot_turned = turn_call(cot, turn)
    else:
        cos, sin = jnp.cos(angles), jnp.sin(angles)
        turn = jnp.eye(model, dtype=bf16)
        cot_turned = cot
    got = jnp.concatenate([near[: half + pad]] + [f[:half] for f in far], axis=0)
    other = swapped(got, "mp", 1)
    low_half = jnp.where(core == 0, got, other)
    high_half = jnp.where(core == 0, other, got)

    def whole(start, size):
        return [low_half[start : start + size], high_half[start : start + size]]

    pieces = []
    for k in range(halo, 1, -1):
        pieces += whole(half + pad + (k - 2) * half, half)
    x_ext = jnp.concatenate(pieces + whole(0, half) + [x_own], axis=0)
    flat_ext = jnp.concatenate(whole(half, pad) + [flat_own], axis=0)
    ints_prev = [near[half + pad]] + [f[half] for f in far]
    ints_prev = [p[None, : span + NEIGHBOURS].astype(jnp.int32) for p in ints_prev]
    seg_keys = jnp.concatenate([p[:, :span] for p in ints_prev[::-1]] + [seg_here], axis=1)
    seg_keys = seg_keys.reshape(-1, 1)
    lens = jnp.concatenate([ints_prev[0][:, span:], lengths], axis=0)
    before = jnp.concatenate([ints_prev[0][0, span - 1 : span], seg_here[0, : span - 1]])
    heads_of = jnp.repeat(before[::BLOCK], BLOCK)
    spot = jnp.arange(span)
    starts = jnp.where(s_index == 0, BLOCK, 0)
    keep = jnp.logical_or(spot == 0, jnp.logical_and(before == heads_of, spot >= starts))
    keep = keep.astype(f32).reshape(span, 1)

    if small:
        x_ext = turn_call(x_ext, turn)
        col_c, turn, cot_turned, cos, sin, x_ext, flat_ext, cot, *rest = meet(
            col_c, turn, cot_turned, cos, sin, x_ext, flat_ext, cot, *xy_q, *shares
        )
        xy_q, shares = rest[:3], rest[3:]
        w_feed = jnp.broadcast_to(shares[0], (plane, shard_rows, 2 * wide))
        for spot, piece in zip(spots[1:], shares[1:]):
            w_feed = put(w_feed, piece[None], (spot, 0, 0))
        w_feed = w_feed.reshape(plane * shard_rows, 2 * wide)
        lead = 3 * width
        lead_c = from_seq(col_c[:, :lead])
        flat_ext = turn_call(flat_ext, turn)
        q_pieces = [col_q] + xy_q
        s_q, s_k, s_v = (weight(q_pieces, j * width) for j in range(3))
        gain_rows = jnp.concatenate(
            [p[:, 3 * width : 3 * width + PAIR] for p in q_pieces], axis=0
        )
    else:
        full_q, full_c = (
            lax.all_gather(b, ("dp", "seq"), axis=0, tiled=True) for b in (block_q, block_c)
        )
        w_feed = exchanged(block_f.reshape(plane * shard_rows, 2 * wide), "seq")
        w_feed = lax.all_gather(w_feed, "dp", axis=0, tiled=True)
        s_q, s_k, s_v = ([(full_q, j * width)] for j in range(3))
        gain_rows = full_q[:, 3 * width :]
        c_kv, s_o, c_q, c_o = ([(full_c, j * width)] for j in (0, 2, 3, 4))
    gains = gain_rows[:, :3].T.astype(f32)
    x = x_ext[halo * span :]
    n1, q, k, v = qkv_call(x_ext, gains[:1], s_q, s_k, s_v, cos, sin, span, width)
    if small:
        rest_c = col_c[:, lead:]
        q, flat_ext, seg_keys, lens, keep, cot, rest_c, w_feed, *lead_c = meet(
            q, flat_ext, seg_keys, lens, keep, cot, rest_c, w_feed, *lead_c
        )
        w_feed = lax.all_gather(w_feed, "dp", axis=0, tiled=True)
        tail_c = from_seq(rest_c)
        c_kv, s_o = (weight([col_c] + lead_c, j * width) for j in (0, 2))
    def over_plane(own):
        return [own] + [swapped(own, "seq", k) for k in range(1, plane)]

    def with_other(pieces):
        got = jnp.concatenate(pieces, axis=0)
        return jnp.concatenate([got, swapped(got, "mp", 1)], axis=0)

    def back_to_owner(own, other):
        total = own.astype(f32) + swapped(other, "mp", 1).astype(f32)
        sent = to_low(total)
        return [total[:half]] + [
            swapped(sent[k * half : (k + 1) * half], "seq", k) for k in range(1, plane)
        ]

    def f_assembled(got):
        got = got.reshape(plane, shard_rows, 2 * wide)
        return jnp.concatenate(
            [got[k, :, at : at + spans[k]] for at in (0, wide) for k in range(plane)], axis=1
        ).astype(f32)

    attn, lse, part = self_call(q, k, v, seg_here, seg_keys, s_o, model)
    kv2 = rows_call(flat_ext, c_kv, 2 * width)
    if small:
        part, kv2, cot, *tail_c = meet(part, kv2, cot, *tail_c)
        c_q, c_o = (weight([rest_c] + tail_c, j * width) for j in (0, 1))
    cot_rows = over_plane(lax.dynamic_slice_in_dim(cot, core * half, half, 0))
    other = swapped(part, "mp", 1)
    h1, n2, q2, cross, lse2, part2 = cross_call(
        lens, x, part, other, gains[1:2], c_q, c_o, kv2, keep
    )
    if small:
        part2, *cot_rows = meet(part2, *cot_rows)
    cot_rows = with_other(cot_rows)
    other = swapped(part2, "mp", 1)
    h2, n3 = norm_call(core.reshape(1), h1, part2, other, gains[2:3], turn)

    n_rows = with_other(over_plane(n3))
    act, du, y_own, y_other, dn_own, dn_other = feed_call(n_rows, cot_rows, w_feed)
    dn3 = plane_sum(back_to_owner(dn_own, dn_other))
    dn3_other = swapped(dn3, "mp", 1)
    g2, low2, dgain3, dq2, dk2, dv2, dn2 = cross_back_call(
        lens, core.reshape(1), cot_turned, h2, dn3, dn3_other, turn, gains[2:3], c_q, c_o,
        q2, kv2, lse2, keep,
    )
    other = swapped(dn2, "mp", 1)
    def in_model_order(rows):
        high = to_low(lax.reduce_precision(rows, 8, 7))
        rest = to_low(rows - high.astype(f32))
        both = dot_t(jnp.concatenate([high, rest], axis=0), turn)
        return both[:span] + both[span:]

    cross_sent, cross_kept = halves(
        [(n2, dq2), (low2, cross)], [(flat_ext, dk2), (flat_ext, dv2)]
    )
    if small:
        *cross_sent, other, du, act = meet(*cross_sent, other, du, act)
        cross_got = reduce_first(cross_sent)
    g1, low1, dgain2, dq, dk, dv = self_back_call(
        g2, h1, dn2, other, gains[1:2], s_o, q, k, v, lse, seg_here, seg_keys, cos, sin
    )
    if small:
        *cross_got, low1, dq, dk, dv = meet(*cross_got, low1, dq, dk, dv)
        cross_kept, cross_got = reduce_second(cross_kept, cross_got)
    own, dn_mine, dn_given, dgain1 = inner_call(
        core.reshape(1), x_ext, dq, dk, dv, s_q, s_k, s_v
    )
    if small:
        dn_mine, dn_given, dgain1, dq, dk, dv, low1, *cross_got = meet(
            dn_mine, dn_given, dgain1, dq, dk, dv, low1, *cross_got
        )
    dgains = jnp.concatenate([dgain1, 0.5 * dgain2, 0.5 * dgain3], axis=0)
    if small:
        terms, rest = [], jnp.pad(dgains, ((0, 5), (0, 0)))
        for _ in range(3):
            terms.append(to_low(lax.reduce_precision(rest, 8, 7)))
            rest = rest - terms[-1].astype(f32)
        turned = dot_t(jnp.concatenate(terms, axis=0), turn)
        dgains = (turned[:8] + (turned[8:16] + turned[16:]))[:3]
        slots = jnp.pad(
            dgains.reshape(3, -1, shard_rows).transpose(1, 0, 2),
            ((0, 0), (0, 5), (0, PAIR - shard_rows)),
        )
        slots = jnp.repeat(slots, lax.axis_size("mp"), axis=0)
    self_sent, self_kept = halves(
        [(n1[halo * span :], dq), (low1, attn)],
        [(n1, dk), (n1, dv)],
    )
    if small:
        sent_a, sent_b, slots, du, act = meet(*self_sent, slots, du, act)
        self_got = reduce_first((sent_a, sent_b))
        slots = lax.all_to_all(slots, ("dp", "seq", "mp"), 0, 0, tiled=True)
        gains_part = jnp.sum(slots, axis=0)[:3, :shard_rows]
        cross_part = lax.psum_scatter(
            last_sum_call(cross_kept, cross_got)[0], "dp", scatter_dimension=0, tiled=True
        ).astype(f32)
        feed_grads = jnp.concatenate(
            [to_low(t_dot(n_rows, du)), to_low(t_dot(cot_rows, act))], axis=1
        )
        feed_low = lax.psum_scatter(feed_grads, "dp", scatter_dimension=0, tiled=True)
        *self_got, gains_part = meet(*self_got, gains_part)
        self_kept, self_got = reduce_second(self_kept, self_got)
        *self_got, h2_model = meet(*self_got, in_model_order(h2))
        self_col, mark = last_sum_call(self_kept, self_got)
        dn_mine, dn_given, y_own, y_other, mark = meet(dn_mine, dn_given, y_own, y_other, mark)
        self_got = exchanged(self_col, "dp")
    y_sums = back_to_owner(y_own, y_other)
    summed = to_low(dn_mine + swapped(dn_given, "mp", 1))
    if small:
        summed = to_low(dot_t(summed, turn))
    summed = summed.reshape(halo, half, model)
    back_parts = [shifted(summed[halo - k], "seq", -k) for k in range(1, halo + 1)]
    if small:
        squares = jnp.sum(cross_part * cross_part) + jnp.sum(jnp.square(feed_low.astype(f32)))
        self_got, squares = meet(self_got, squares)
        self_part, self_squares = total_call(self_got, mark)
    else:
        feed_grads = jnp.concatenate(
            [to_low(t_dot(n_rows, du)), to_low(t_dot(cot_rows, act))], axis=1
        )
        feed_low = lax.psum_scatter(feed_grads, "dp", scatter_dimension=0, tiled=True)
        feed_part = f_assembled(exchanged(feed_low, "seq"))
        cross_part, self_part = reduce_plain(cross_kept), reduce_plain(self_kept)
        squares = jnp.sum(feed_part * feed_part) + jnp.sum(cross_part * cross_part)
        self_squares = jnp.sum(jnp.square(self_part)).reshape(1, 1)
    if not small:
        gain_sums = butterfly(dgains, ("mp", "seq", "dp"))
        shard = lax.axis_index("dp") * lax.axis_size("seq") + s_index
        gains_part = lax.dynamic_slice_in_dim(gain_sums, shard * shard_rows, shard_rows, axis=1)
    first_model = (core == 0).astype(f32)
    local_squares = (
        self_squares
        + squares
        + first_model * jnp.sum(gains_part * gains_part)
    )
    if small:
        shares = [take(feed_low.reshape(plane, shard_rows, 2 * wide), spot, 0) for spot in spots]
        local_squares, *rest = meet(local_squares, *y_sums, *back_parts, *shares)
        y_sums, back_parts, shares = rest[:plane], rest[plane:-plane], rest[-plane:]
        shares = shares[:1] + [swapped(shares[k], "seq", k) for k in range(1, plane)]
        feed_got = jnp.zeros((plane, shard_rows, 2 * wide), bf16)
        for spot, piece in zip(spots, shares):
            feed_got = put(feed_got, piece[None], (spot, 0, 0))
        feed_part = f_assembled(feed_got)
    grad_norm = jnp.sqrt(sum_everywhere(local_squares).reshape(()))
    factor = jnp.minimum(1.0, clip_limit / (grad_norm + 1e-06))
    scalar = factor.reshape(1)
    mixed_order, plain = (0, 2, 3, 1), (0, 1)
    y_half = plane_sum(y_sums)
    y_other = swapped(y_half, "mp", 1)
    y_all = jnp.concatenate(
        [jnp.where(core == 0, y_half, y_other), jnp.where(core == 0, y_other, y_half)], axis=0
    )
    if halo:
        back = sum(p.astype(f32) for p in back_parts)
        if small:
            back = dot(to_low(back), turn)
        own = own + put(jnp.zeros_like(own), back, (core * half, 0))
    back, _ = rms_back(x.astype(f32), gains[:1], core_sum(own))
    in_grad = g1 + back

    if small:
        in_grad = in_model_order(in_grad)
        result = to_low(h2_model + y_all)
    else:
        result = to_low(h2 + y_all)
    in_grad = in_grad.reshape(row_count, span, model)
    out = result.reshape(row_count, span, model)
    (
        self_new, self_first_new, self_second_new,
        cross_new, cross_first_new, cross_second_new,
        feed_new, feed_first_new, feed_second_new,
    ) = adam_call(
        scalar,
        [
            (self_weights, self_part, self_first, self_second, mixed_order),
            (cross_weights, cross_part, cross_first, cross_second, mixed_order),
            (feed_weights, feed_part, feed_first, feed_second, plain),
        ],
    )
    gains_new, gains_first_new, gains_second_new = adam_step(
        norm_gains, gains_part, gains_first, gains_second, factor, gain_rate, 0.0
    )
    return (
        out,
        in_grad,
        grad_norm,
        self_new,
        cross_new,
        feed_new,
        gains_new,
        self_first_new,
        cross_first_new,
        feed_first_new,
        gains_first_new,
        self_second_new,
        cross_second_new,
        feed_second_new,
        gains_second_new,
    )


def solution(mesh):
    tok = P("dp", "seq", None)
    mat = P(None, ("dp", "seq"), "mp")
    vec = P(None, ("dp", "seq"))
    in_specs = (
        tok,
        P("dp", "seq", None, None, None),
        tok,
        P("dp", "seq"),
        tok,
    ) + (mat, mat, mat, vec) * 3
    out_specs = (tok, tok, P()) + (mat, mat, mat, vec) * 3
    return jax.shard_map(
        per_device, mesh=mesh, in_specs=in_specs, out_specs=out_specs, check_vma=False
    )
```

```python
import jax
import jax.numpy as jnp
from jax import lax
from jax.experimental import pallas as pl
from jax.experimental.pallas import tpu as pltpu
from jax.sharding import PartitionSpec as P

HEAD_DIM = 64
PAIR = 128
BLOCK = 64
NEIGHBOURS = 2
NEIGH_LEN = 128
KEYS = NEIGHBOURS * NEIGH_LEN
STEP = 10
DOC_MAX = 512
CHUNK = 256
TOKENS = 512

norm_eps = 1e-05
rope_base = 10000.0
beta_one = 0.9
beta_two = 0.95
adam_eps = 1e-08
weight_decay = 0.1
learn_rate = 0.1
gain_rate = 0.5
clip_limit = 1.0
masked_fill = -1e30
score_scale = HEAD_DIM ** (-0.5)
gelu_c = 0.7978845608028654
gelu_k = 0.044715

f32 = jnp.float32
bf16 = jnp.bfloat16


def to_low(array_in):
    return array_in.astype(bf16)


def shifted(value, axis, by):
    count = lax.axis_size(axis)
    return lax.ppermute(value, axis, [(i, i + by) for i in range(count) if 0 <= i + by < count])


def rotated(value, axis, by):
    count = lax.axis_size(axis)
    return lax.ppermute(value, axis, [(i, (i + by) % count) for i in range(count)])


def swapped(value, axis, by):
    count = lax.axis_size(axis)
    return lax.ppermute(value, axis, [(i, i ^ by) for i in range(count)])


def butterfly(value, axes):
    for axis in axes:
        step = 1
        while step < lax.axis_size(axis):
            value = value + swapped(value, axis, step)
            step *= 2
    return value


def sum_everywhere(value):
    axes = ("dp", "seq", "mp")
    if not small_mesh():
        return butterfly(value, axes)
    count = lax.axis_size("dp") * lax.axis_size("seq") * lax.axis_size("mp")
    spread = jnp.broadcast_to(value, (count, 8, PAIR))
    return jnp.sum(lax.all_to_all(spread, axes, 0, 0, tiled=True)[:, :1, :1], axis=0)


def core_sum(partial_out):
    return partial_out + swapped(partial_out, "mp", 1)


def small_mesh():
    return lax.axis_size("dp") == 4 and lax.axis_size("seq") == 4


def put(buffer, piece, starts):
    return lax.dynamic_update_slice(buffer, piece, starts)


def meet(*values):
    return lax.optimization_barrier(values)


ORDER = (0, 2, 1, 3)


def own_order(model, s):
    rows = model // 16
    spot = jnp.arange(model)
    near, z, inner = spot // (4 * rows), spot // rows % 4, spot % rows
    flip = (near % 2) * 2 + near // 2
    source = (z * 4 + (s ^ flip)) * rows + inner
    return (spot[:, None] == source[None, :]).astype(bf16)


def plane_sum(pieces):
    return (pieces[0] + pieces[1].astype(f32)) + (pieces[2].astype(f32) + pieces[3].astype(f32))


def take(array_in, index, axis):
    return lax.dynamic_index_in_dim(array_in, index, axis, keepdims=False)


def wide_for_dp(block):
    rows, cols = block.shape
    return jnp.broadcast_to(block[None], (4, rows, cols)).reshape(4 * rows, cols)


def exchanged(array_in, axis):
    return lax.all_to_all(array_in, axis, 0, 0, tiled=True)


def from_seq(column):
    return [swapped(column, "seq", k) for k in ORDER[1:]]


def weight(pieces, start):
    return [(p, start) for p in pieces]


def reduce_first(sent):
    return swapped(sent[0], "seq", 1), swapped(sent[1], "seq", 2)


def reduce_second(kept, got):
    sent_a, sent_b = half_sum_call(kept, got)
    return (*kept, *got), (swapped(sent_a, "seq", 2), swapped(sent_b, "seq", 1))


def reduce_last(got):
    rows, cols = got.shape
    return jnp.sum(got.reshape(4, rows // 4, cols).astype(f32), axis=0)


def reduce_plain(grads):
    return lax.psum_scatter(
        jnp.concatenate(grads, axis=1), ("dp", "seq"), scatter_dimension=0, tiled=True
    ).astype(f32)


def halves(left, right):
    if not small_mesh():
        return None, [jnp.concatenate([to_low(t_dot(a, b)) for a, b in left + right], axis=1)]

    def products(pairs, pick):
        parts = [to_low(t_dot(pick(a), b)) for a, b in pairs]
        return parts[0] if len(parts) == 1 else jnp.concatenate(parts, axis=1)

    def second(a, first):
        quarter = a.shape[1] // 4
        return jnp.concatenate(
            [
                a[:, first * quarter : (first + 1) * quarter],
                a[:, (first + 2) * quarter : (first + 3) * quarter],
            ],
            axis=1,
        )

    mid = left[0][0].shape[1] // 2
    sent = (products(left, lambda a: a[:, mid:]), products(right, lambda a: second(a, 1)))
    kept = (products(left, lambda a: a[:, :mid]), products(right, lambda a: second(a, 0)))
    return sent, kept


def adam_step(weight, gradient, first_old, second_old, factor, step_rate, decay_coef):
    clipped = gradient * factor
    first_new = beta_one * first_old + (1.0 - beta_one) * clipped
    second_new = beta_two * second_old + (1.0 - beta_two) * clipped * clipped
    first_hat = first_new / (1.0 - beta_one**STEP)
    second_hat = second_new / (1.0 - beta_two**STEP)
    weight_new = weight - step_rate * (
        first_hat / (jnp.sqrt(second_hat) + adam_eps) + decay_coef * weight
    )
    return (weight_new, first_new, second_new)


def call(kernel, grid, ins, outs, args, scratch=(), prefetch=0):
    specs, flat, counts = [], list(args[:prefetch]), [1] * prefetch
    for (shape, index), arg in zip(ins, args[prefetch:]):
        if not isinstance(arg, list):
            specs.append(pl.BlockSpec(shape, index))
            flat.append(arg)
            counts.append(1)
            continue
        for array_in, start in arg:
            place = lambda *ids, at=start // shape, f=index: (0, f(ids[0]) + at)
            specs.append(pl.BlockSpec((array_in.shape[0], shape), place))
            flat.append(array_in)
        counts.append(-len(arg))

    def body(*refs):
        refs, grouped = list(refs), []
        for count in counts:
            grouped.append(refs.pop(0) if count > 0 else [refs.pop(0) for _ in range(-count)])
        kernel(*grouped, *refs)

    return pl.pallas_call(
        body,
        out_shape=[jax.ShapeDtypeStruct(o[2], o[3]) for o in outs],
        grid_spec=pltpu.PrefetchScalarGridSpec(
            num_scalar_prefetch=prefetch,
            grid=grid,
            in_specs=specs,
            out_specs=[pl.BlockSpec(o[0], o[1]) for o in outs],
            scratch_shapes=list(scratch),
        ),
        compiler_params=pltpu.CompilerParams(
            dimension_semantics=("arbitrary",) * len(grid), vmem_limit_bytes=56 << 20
        ),
        name=kernel.__name__,
    )(*flat)


def whole_weight(refs):
    pieces = [r[...] for r in refs]
    return pieces[0] if len(pieces) == 1 else jnp.concatenate(pieces, axis=0)


first_block = lambda i: 0
each_block = lambda i: i


def dot(a, b):
    return jnp.dot(a, b, preferred_element_type=f32)


def dot_t(a, b):
    return lax.dot_general(a, b, (((1,), (1,)), ((), ())), preferred_element_type=f32)


def t_dot(a, b):
    return lax.dot_general(a, b, (((0,), (0,)), ((), ())), preferred_element_type=f32)


def rms_factor(z):
    return lax.rsqrt(jnp.mean(z * z, axis=-1, keepdims=True) + norm_eps)


def rms_back(z, gain, grad):
    factor = rms_factor(z)
    scaled = grad * gain
    inner = jnp.mean(scaled * z, axis=-1, keepdims=True)
    return factor * scaled - z * (factor * factor * factor * inner), grad * z * factor


def lane_in_head(shape):
    return lax.broadcasted_iota(jnp.int32, shape, 1)


def rope(z, cos, sin, sign):
    lane = lane_in_head(z.shape)
    lead = lane % HEAD_DIM < HEAD_DIM // 2
    partner = jnp.where(lead, -pltpu.roll(z, PAIR - 32, 1), pltpu.roll(z, 32, 1))
    return z * cos + partner * (sin * sign)


def split_heads(z):
    first = lane_in_head(z.shape) < HEAD_DIM
    zero = jnp.zeros_like(z)
    return jnp.where(first, z, zero), jnp.where(first, zero, z)


def join_heads(a, b):
    return jnp.where(lane_in_head(a.shape) < HEAD_DIM, a, b)


def qkv_kernel(x_ref, g_ref, wq, wk, wv, cos_ref, sin_ref, n_ref, q_ref, k_ref, v_ref):
    rows, span = n_ref.shape[0], q_ref.shape[0]

    @pl.when(pl.program_id(0) == 0)
    def _():
        x = x_ref[...].astype(f32)
        n_ref[...] = to_low(x * rms_factor(x) * g_ref[...])

    normed, cos, sin = n_ref[...], cos_ref[...], sin_ref[...]

    def turned(raw, cos, sin):
        return jnp.concatenate(
            [
                to_low(rope(raw[:, c : c + PAIR], cos, sin, 1.0))
                for c in range(0, raw.shape[1], PAIR)
            ],
            axis=1,
        )

    k_ref[...] = turned(dot(normed, whole_weight(wk)), cos, sin)
    v_ref[...] = to_low(dot(normed, whole_weight(wv)))
    own = rows - span
    q_ref[...] = turned(dot(normed[own:], whole_weight(wq)), cos[own:], sin[own:])


def qkv_call(x_ext, gain, wq, wk, wv, cos, sin, span, width):
    rows, model = x_ext.shape
    fix = lambda i: (0, 0)
    col = lambda i: (0, i)
    return call(
        qkv_kernel,
        (width // CHUNK,),
        [
            ((rows, model), fix),
            ((1, model), fix),
            (CHUNK, each_block),
            (CHUNK, each_block),
            (CHUNK, each_block),
            ((rows, PAIR), fix),
            ((rows, PAIR), fix),
        ],
        [
            ((rows, model), fix, (rows, model), bf16),
            ((span, CHUNK), col, (span, width), bf16),
            ((rows, CHUNK), col, (rows, width), bf16),
            ((rows, CHUNK), col, (rows, width), bf16),
        ],
        (x_ext, gain, wq, wk, wv, cos, sin),
    )


def self_bias(segq_ref, segk_ref, bias_ref):
    keys, span = bias_ref.shape
    key_pos = lax.broadcasted_iota(jnp.int32, (keys, span), 0) - (keys - span)
    query_pos = lax.broadcasted_iota(jnp.int32, (keys, span), 1)
    ok = jnp.logical_and(key_pos <= query_pos, segk_ref[...] == segq_ref[...])
    bias_ref[...] = jnp.where(ok, 0.0, masked_fill)


def self_kernel(q_ref, k_ref, v_ref, segq_ref, segk_ref, wo, o_ref, lse_ref, part_ref, bias_ref):
    @pl.when(pl.program_id(0) == 0)
    def _():
        self_bias(segq_ref, segk_ref, bias_ref)
        part_ref[...] = jnp.zeros_like(part_ref)

    k, v, bias = k_ref[...], v_ref[...], bias_ref[...]
    outs, lses = [], []
    for qh in split_heads(q_ref[...] * score_scale):
        s = dot_t(k, qh) + bias
        top = jnp.max(s, axis=0, keepdims=True)
        e = jnp.exp(s - top)
        total = jnp.sum(e, axis=0, keepdims=True)
        lses.append(top + jnp.log(total))
        outs.append(t_dot(to_low(e * (1.0 / total)), v))
    o = to_low(join_heads(outs[0], outs[1]))
    o_ref[...] = o
    lse_ref[0] = jnp.concatenate(lses, axis=0)
    part_ref[...] += dot_t(o, whole_weight(wo))


def self_call(q, k, v, segq, segk, wo, model):
    span, width = q.shape
    keys = k.shape[0]
    pair = lambda p: (0, p)
    fix = lambda p: (0, 0)
    return call(
        self_kernel,
        (width // PAIR,),
        [
            ((span, PAIR), pair),
            ((keys, PAIR), pair),
            ((keys, PAIR), pair),
            ((1, span), fix),
            ((keys, 1), fix),
            (PAIR, each_block),
        ],
        [
            ((span, PAIR), pair, (span, width), bf16),
            ((1, 2, span), lambda p: (p, 0, 0), (width // PAIR, 2, span), f32),
            ((span, model), fix, (span, model), f32),
        ],
        (q, k, v, segq, segk, wo),
        scratch=[pltpu.VMEM((keys, span), f32)],
    )


def block_bias(len_ref, block):
    key = lax.broadcasted_iota(jnp.int32, (KEYS, PAIR), 0)
    limit = jnp.where(key < NEIGH_LEN, len_ref[block, 0], len_ref[block, 1])
    return jnp.where(key % NEIGH_LEN < limit, 0.0, masked_fill)


def tile_bias(len_ref, tile, tiles):
    if tile:
        return block_bias(len_ref, tile)
    first = lax.broadcasted_iota(jnp.int32, (KEYS, PAIR), 1) % BLOCK == 0
    lead = jnp.where(first, masked_fill, block_bias(len_ref, 0))
    last = jnp.where(first, block_bias(len_ref, tiles), masked_fill)
    return jnp.concatenate([lead, last], axis=0)


def stack_heads(z):
    return jnp.concatenate(split_heads(z), axis=0)


def merge_heads(z):
    return join_heads(z[:BLOCK], z[BLOCK:])


def tile_keys(ref, tile, tiles):
    own = ref[tile * KEYS : (tile + 1) * KEYS, :]
    if tile:
        return own
    return jnp.concatenate([own, ref[tiles * KEYS : (tiles + 1) * KEYS, :]], axis=0)


def cross_kernel(
    len_ref, x_ref, pa_ref, pb_ref, g_ref, wq, k_ref, v_ref, keep_ref, wo,
    h_ref, n_ref, q_ref, o_ref, lse_ref, part_ref, acc_ref,
):
    span = x_ref.shape[0]
    tiles = span // BLOCK

    @pl.when(pl.program_id(0) == 0)
    def _():
        h = x_ref[...].astype(f32) + (pa_ref[...] + pb_ref[...])
        h_ref[...] = h
        n_ref[...] = to_low(h * rms_factor(h) * g_ref[...])
        part_ref[...] = jnp.zeros_like(part_ref)

    turned = pltpu.roll(to_low(dot(n_ref[...], whole_weight(wq))).astype(f32), 1, 0)
    q = to_low(turned * score_scale)
    q_ref[...] = q
    for tile in range(tiles):
        rows = slice(tile * BLOCK, (tile + 1) * BLOCK)
        k, v = tile_keys(k_ref, tile, tiles), tile_keys(v_ref, tile, tiles)
        sc = dot_t(k, stack_heads(q[rows])) + tile_bias(len_ref, tile, tiles)
        top = jnp.max(sc, axis=0, keepdims=True)
        e = jnp.exp(sc - top)
        total = jnp.sum(e, axis=0, keepdims=True)
        lse_ref[0, tile : tile + 1, :] = top + jnp.log(total)
        acc_ref[rows, :] = merge_heads(t_dot(to_low(e * (1.0 / total)), v))
    o = to_low(pltpu.roll(acc_ref[...] * keep_ref[...], span - 1, 0))
    o_ref[...] = o
    part_ref[...] += dot_t(o, whole_weight(wo))


def cross_call(lens, x, pa, pb, gain, wq, wo, kv2, keep):
    span, model = x.shape
    keys, width = kv2.shape[0], kv2.shape[1] // 2
    pairs = width // PAIR
    pair = lambda p, *_: (0, p)
    fix = lambda p, *_: (0, 0)
    return call(
        cross_kernel,
        (pairs,),
        [
            ((span, model), fix),
            ((span, model), fix),
            ((span, model), fix),
            ((1, model), fix),
            (PAIR, each_block),
            ((keys, PAIR), pair),
            ((keys, PAIR), lambda p, *_: (0, pairs + p)),
            ((span, 1), fix),
            (PAIR, each_block),
        ],
        [
            ((span, model), fix, (span, model), f32),
            ((span, model), fix, (span, model), bf16),
            ((span, PAIR), pair, (span, width), bf16),
            ((span, PAIR), pair, (span, width), bf16),
            ((1, span // BLOCK, PAIR), lambda p, *_: (p, 0, 0), (pairs, span // BLOCK, PAIR), f32),
            ((span, model), fix, (span, model), f32),
        ],
        (lens, x, pa, pb, gain, wq, kv2, kv2, keep, wo),
        scratch=[pltpu.VMEM((span, PAIR), f32)],
        prefetch=1,
    )


def gelu_and_slope(u):
    t = jnp.tanh(gelu_c * (u + gelu_k * (u * u * u)))
    slope = 0.5 * (1.0 + t) + 0.5 * u * (1.0 - t * t) * (gelu_c * (1.0 + 3.0 * gelu_k * (u * u)))
    return to_low(0.5 * u * (1.0 + t)), slope


def norm_kernel(core_ref, h1_ref, pa_ref, pb_ref, g_ref, turn_ref, h_ref, n_ref):
    h = h1_ref[...] + (pa_ref[...] + pb_ref[...])
    h_ref[...] = h
    normed = to_low(h * rms_factor(h) * g_ref[...])
    rows = n_ref.shape[0]
    mine = jnp.where(core_ref[0] == 0, normed[:rows], normed[rows:])
    n_ref[...] = to_low(dot_t(mine, turn_ref[...]))


def norm_call(core, h1, pa, pb, gain, turn):
    span, model = h1.shape
    fix = lambda i, *_: (0, 0)
    whole = ((span, model), fix)
    return call(
        norm_kernel,
        (1,),
        [whole, whole, whole, ((1, model), fix), ((model, model), fix)],
        [
            ((span, model), fix, (span, model), f32),
            ((span // 2, model), fix, (span // 2, model), bf16),
        ],
        (core, h1, pa, pb, gain, turn),
        prefetch=1,
    )


def feed_kernel(n_ref, cot_ref, up_ref, down_ref, act_ref, du_ref, ya_ref, yb_ref, da_ref, db_ref):
    up, down = up_ref[...], down_ref[...]
    act, slope = gelu_and_slope(dot(n_ref[...], up))
    du = to_low(dot(cot_ref[...], down) * slope)
    act_ref[...] = act
    du_ref[...] = du
    y, dn = dot_t(act, down), dot_t(du, up)
    step = pl.program_id(0)
    half = pl.num_programs(0) // 2

    @pl.when(step < half)
    def _():
        ya_ref[...] = to_low(y)
        da_ref[...] = dn

    @pl.when(step >= half)
    def _():
        yb_ref[...] = to_low(y)
        db_ref[...] = dn


def feed_call(n, cot, w_feed):
    rows, model = n.shape
    hidden = w_feed.shape[1] // 2
    half = rows // TOKENS // 2
    row = lambda i: (i, 0)
    lead = lambda i: (jnp.minimum(i, half - 1), 0)
    tail = lambda i: (jnp.maximum(i - half, 0), 0)
    block = (TOKENS, model)
    part = (rows // 2, model)
    return call(
        feed_kernel,
        (rows // TOKENS,),
        [
            (block, row),
            (block, row),
            ((model, hidden), lambda i: (0, 0)),
            ((model, hidden), lambda i: (0, 1)),
        ],
        [
            ((TOKENS, hidden), row, (rows, hidden), bf16),
            ((TOKENS, hidden), row, (rows, hidden), bf16),
            (block, lead, part, bf16),
            (block, tail, part, bf16),
            (block, lead, part, f32),
            (block, tail, part, f32),
        ],
        (n, cot, w_feed, w_feed),
    )


def cross_back_kernel(
    len_ref, core_ref, base_ref, h_ref, da_ref, db_ref, turn_ref, g_ref, wo, q_ref, k_ref, v_ref, lse_ref,
    keep_ref, wq,
    grad_ref, low_ref, gain_ref, dq_ref, dk_ref, dv_ref, dn_ref, acc_ref,
):
    span = h_ref.shape[0]
    tiles = span // BLOCK

    @pl.when(pl.program_id(0) == 0)
    def _():
        first, other = da_ref[...], db_ref[...]
        given = jnp.where(
            core_ref[0] == 0,
            jnp.concatenate([first, other], axis=0),
            jnp.concatenate([other, first], axis=0),
        )
        high = to_low(given)
        low = to_low(given - high.astype(f32))
        turn = turn_ref[...]
        back, gains = rms_back(h_ref[...], g_ref[...], dot(high, turn) + dot(low, turn))
        grad = base_ref[...].astype(f32) + back
        grad_ref[...] = grad
        low_ref[...] = to_low(grad)
        gain_ref[...] = jnp.sum(gains, axis=0, keepdims=True)
        dn_ref[...] = jnp.zeros_like(dn_ref)

    do = to_low(dot(low_ref[...], whole_weight(wo))).astype(f32)
    do = to_low(pltpu.roll(do, 1, 0) * keep_ref[...])
    q = q_ref[...]
    for tile in range(tiles):
        rows = slice(tile * BLOCK, (tile + 1) * BLOCK)
        k, v = tile_keys(k_ref, tile, tiles), tile_keys(v_ref, tile, tiles)
        qs, dos = stack_heads(q[rows]), stack_heads(do[rows])
        p = jnp.exp(dot_t(k, qs) + tile_bias(len_ref, tile, tiles) - lse_ref[0, tile : tile + 1, :])
        dp = dot_t(v, dos)
        ds = to_low(p * (dp - jnp.sum(p * dp, axis=0, keepdims=True)))
        acc_ref[rows, :] = merge_heads(t_dot(ds, k))
        dk = to_low(dot(ds, qs))
        dv = to_low(dot(to_low(p), dos))
        own = slice(tile * KEYS, (tile + 1) * KEYS)
        dk_ref[own, :] = dk[:KEYS]
        dv_ref[own, :] = dv[:KEYS]
        if not tile:
            last = slice(tiles * KEYS, (tiles + 1) * KEYS)
            dk_ref[last, :] = dk[KEYS:]
            dv_ref[last, :] = dv[KEYS:]
    dq = to_low(pltpu.roll(acc_ref[...] * score_scale, span - 1, 0))
    dq_ref[...] = dq
    dn_ref[...] += dot_t(dq, whole_weight(wq))


def cross_back_call(lens, core, base, h, da, db, turn, gain, wq, wo, q, kv2, lse, keep):
    span, model = h.shape
    keys, width = kv2.shape[0], kv2.shape[1] // 2
    pairs = width // PAIR
    pair = lambda p, *_: (0, p)
    fix = lambda p, *_: (0, 0)
    return call(
        cross_back_kernel,
        (pairs,),
        [
            ((span, model), fix),
            ((span, model), fix),
            ((span // 2, model), fix),
            ((span // 2, model), fix),
            ((model, model), fix),
            ((1, model), fix),
            (PAIR, each_block),
            ((span, PAIR), pair),
            ((keys, PAIR), pair),
            ((keys, PAIR), lambda p, *_: (0, pairs + p)),
            ((1, span // BLOCK, PAIR), lambda p, *_: (p, 0, 0)),
            ((span, 1), fix),
            (PAIR, each_block),
        ],
        [
            ((span, model), fix, (span, model), f32),
            ((span, model), fix, (span, model), bf16),
            ((1, model), fix, (1, model), f32),
            ((span, PAIR), pair, (span, width), bf16),
            ((keys, PAIR), pair, (keys, width), bf16),
            ((keys, PAIR), pair, (keys, width), bf16),
            ((span, model), fix, (span, model), f32),
        ],
        (lens, core, base, h, da, db, turn, gain, wo, q, kv2, kv2, lse, keep, wq),
        scratch=[pltpu.VMEM((span, PAIR), f32)],
        prefetch=2,
    )


def self_back_kernel(
    base_ref, h_ref, da_ref, db_ref, g_ref, wo, q_ref, k_ref, v_ref, lse_ref, segq_ref,
    segk_ref, cos_ref, sin_ref,
    grad_ref, low_ref, gain_ref, dq_ref, dk_ref, dv_ref, bias_ref,
):
    span = h_ref.shape[0]
    keys = k_ref.shape[0]

    @pl.when(pl.program_id(0) == 0)
    def _():
        back, gains = rms_back(h_ref[...], g_ref[...], da_ref[...] + db_ref[...])
        grad = base_ref[...] + back
        grad_ref[...] = grad
        low_ref[...] = to_low(grad)
        gain_ref[...] = jnp.sum(gains, axis=0, keepdims=True)
        self_bias(segq_ref, segk_ref, bias_ref)

    do = to_low(dot(low_ref[...], whole_weight(wo)))
    k, v, bias = k_ref[...], v_ref[...], bias_ref[...]
    qs, dos = split_heads(q_ref[...] * score_scale), split_heads(do)
    dqs, dk, dv = [], 0.0, 0.0
    for h in range(2):
        p = jnp.exp(dot_t(k, qs[h]) + bias - lse_ref[0, h : h + 1, :])
        dp = dot_t(v, dos[h])
        ds = to_low(p * (dp - jnp.sum(p * dp, axis=0, keepdims=True)))
        dqs.append(t_dot(ds, k))
        dk = dk + dot(ds, qs[h])
        dv = dv + dot(to_low(p), dos[h])
    cos, sin = cos_ref[...], sin_ref[...]
    dq = join_heads(dqs[0], dqs[1]) * score_scale
    dq_ref[...] = to_low(rope(dq, cos[keys - span :], sin[keys - span :], -1.0))
    dk_ref[...] = to_low(rope(dk, cos, sin, -1.0))
    dv_ref[...] = to_low(dv)


def self_back_call(base, h, da, db, gain, wo, q, k, v, lse, segq, segk, cos, sin):
    span, model = h.shape
    keys, width = k.shape
    pair = lambda p: (0, p)
    fix = lambda p: (0, 0)
    return call(
        self_back_kernel,
        (width // PAIR,),
        [
            ((span, model), fix),
            ((span, model), fix),
            ((span, model), fix),
            ((span, model), fix),
            ((1, model), fix),
            (PAIR, each_block),
            ((span, PAIR), pair),
            ((keys, PAIR), pair),
            ((keys, PAIR), pair),
            ((1, 2, span), lambda p: (p, 0, 0)),
            ((1, span), fix),
            ((keys, 1), fix),
            ((keys, PAIR), fix),
            ((keys, PAIR), fix),
        ],
        [
            ((span, model), fix, (span, model), f32),
            ((span, model), fix, (span, model), bf16),
            ((1, model), fix, (1, model), f32),
            ((span, PAIR), pair, (span, width), bf16),
            ((keys, PAIR), pair, (keys, width), bf16),
            ((keys, PAIR), pair, (keys, width), bf16),
        ],
        (base, h, da, db, gain, wo, q, k, v, lse, segq, segk, cos, sin),
        scratch=[pltpu.VMEM((keys, span), f32)],
    )


def inner_kernel(
    core_ref, x_ref, dq_ref, dk_ref, dv_ref, wq, wk, wv,
    own_ref, mine_ref, other_ref, gain_ref, dn_ref,
):
    step = pl.program_id(0)
    rows, span = x_ref.shape[0], dq_ref.shape[0]
    own, half = rows - span, span // 2
    dn = dot_t(dk_ref[...], whole_weight(wk)) + dot_t(dv_ref[...], whole_weight(wv))
    dn_own = dot_t(dq_ref[...], whole_weight(wq))

    @pl.when(step == 0)
    def _():
        dn_ref[...] = dn
        dn_ref[own:, :] += dn_own

    @pl.when(step > 0)
    def _():
        dn_ref[...] += dn
        dn_ref[own:, :] += dn_own

    @pl.when(step == pl.num_programs(0) - 1)
    def _():
        x = x_ref[...].astype(f32)
        gain_ref[...] = jnp.sum(dn_ref[...] * x * rms_factor(x), axis=0, keepdims=True)
        own_ref[...] = dn_ref[own:, :]
        core = core_ref[0]
        for k in range(own // span):
            spot = slice(k * half, (k + 1) * half)
            mine = pl.multiple_of(k * span + core * half, half)
            other = pl.multiple_of(k * span + (1 - core) * half, half)
            mine_ref[spot, :] = dn_ref[pl.ds(mine, half), :]
            other_ref[spot, :] = dn_ref[pl.ds(other, half), :]


def inner_call(core, x_ext, dq, dk, dv, wq, wk, wv):
    rows, model = x_ext.shape
    span, width = dq.shape
    fix = lambda i, *_: (0, 0)
    col = lambda i, *_: (0, i)
    part = ((rows - span) // 2, model)
    return call(
        inner_kernel,
        (width // CHUNK,),
        [
            ((rows, model), fix),
            ((span, CHUNK), col),
            ((rows, CHUNK), col),
            ((rows, CHUNK), col),
            (CHUNK, each_block),
            (CHUNK, each_block),
            (CHUNK, each_block),
        ],
        [
            ((span, model), fix, (span, model), f32),
            (part, fix, part, f32),
            (part, fix, part, f32),
            ((1, model), fix, (1, model), f32),
        ],
        (core, x_ext, dq, dk, dv, wq, wk, wv),
        scratch=[pltpu.VMEM((rows, model), f32)],
        prefetch=1,
    )


def adam_call(factor, groups):
    orders = [g[4] for g in groups]
    counts = len(groups)

    def adam_kernel(factor_ref, *refs):
        ins, outs = refs[: 4 * counts], refs[4 * counts :]
        for n, order in enumerate(orders):
            w_ref, g_ref, m_ref, v_ref = ins[4 * n : 4 * n + 4]
            wo_ref, mo_ref, vo_ref = outs[3 * n : 3 * n + 3]
            width = w_ref.shape[2]
            for j, at in enumerate(order):
                wo_ref[j], mo_ref[j], vo_ref[j] = adam_step(
                    w_ref[j],
                    g_ref[:, at * width : (at + 1) * width],
                    m_ref[j],
                    v_ref[j],
                    factor_ref[0],
                    learn_rate,
                    weight_decay,
                )

    def whole(a):
        return (a.shape, lambda i, *_, n=a.ndim: (0,) * n)

    arrays = [a for g in groups for a in g[:4]]
    results = [whole(g[0]) + (g[0].shape, f32) for g in groups for _ in range(3)]
    return call(
        adam_kernel, (1,), [whole(a) for a in arrays], results, (factor, *arrays), prefetch=1
    )


def last_sum_kernel(ka, kb, ga, gb, ra, rb, o_ref, mark_ref):
    mark_ref[...] = jnp.zeros_like(mark_ref)
    wide = ka.shape[1]
    o_ref[:, :wide] = to_low((ka[...].astype(f32) + ga[...].astype(f32)) + ra[...].astype(f32))
    o_ref[:, wide:] = to_low((kb[...].astype(f32) + gb[...].astype(f32)) + rb[...].astype(f32))


def last_sum_call(held, got):
    (rows, wide_a), wide_b = got[0].shape, got[1].shape[1]
    fix = lambda i: (0, 0)
    a, b, o = (rows, wide_a), (rows, wide_b), (rows, wide_a + wide_b)
    return call(
        last_sum_kernel,
        (1,),
        [(a, fix), (b, fix)] * 3,
        [(o, fix, o, bf16), ((8, PAIR), fix, (8, PAIR), f32)],
        (*held, *got),
    )


def total_kernel(got_ref, mark_ref, o_ref, squares_ref):
    rows = o_ref.shape[0]
    total = got_ref[:rows].astype(f32)
    for k in range(1, 4):
        total = total + got_ref[k * rows : (k + 1) * rows].astype(f32)
    o_ref[...] = total
    squares_ref[...] = jnp.sum(jnp.sum(total * total, axis=0, keepdims=True), axis=1, keepdims=True)


def total_call(got, mark):
    rows, cols = got.shape
    fix = lambda i: (0, 0)
    out = (rows // 4, cols)
    return call(
        total_kernel, (1,), [((rows, cols), fix), ((8, PAIR), fix)],
        [(out, fix, out, f32), ((1, 1), fix, (1, 1), f32)], (got, mark),
    )


def half_sum_kernel(ka, ga, kb, gb, out_a, out_b):
    out_a[...] = to_low(ka[...].astype(f32) + ga[...].astype(f32))
    out_b[...] = to_low(kb[...].astype(f32) + gb[...].astype(f32))


def half_sum_call(kept, got):
    rows, (wide_a, wide_b) = kept[0].shape[0] // 2, (k.shape[1] for k in kept)
    half = lambda i: (1, 0)
    fix = lambda i: (0, 0)
    a, b = (rows, wide_a), (rows, wide_b)
    return call(
        half_sum_kernel,
        (1,),
        [(a, half), (a, half), (b, half), (b, half)],
        [(a, fix, a, bf16), (b, fix, b, bf16)],
        (kept[0], got[0], kept[1], got[1]),
    )


def pack_call(place, own, cross, feed, gain_cols, firsts, spans, wide):
    _, rows, width = own.shape
    plane = len(spans)

    def pack_kernel(place_ref, own_ref, cross_ref, feed_ref, gain_ref, q_ref, c_ref, f_ref):
        for j in range(3):
            q_ref[:, j * width : (j + 1) * width] = to_low(own_ref[j])
        q_ref[:, 3 * width :] = to_low(gain_ref[...])
        for j, part in enumerate((cross_ref[1], cross_ref[2], own_ref[3], cross_ref[0], cross_ref[3])):
            c_ref[:, j * width : (j + 1) * width] = to_low(part)
        for k in range(plane):
            pieces = []
            for m in range(2):
                pieces.append(to_low(feed_ref[m, :, firsts[k] : firsts[k] + spans[k]]))
                if spans[k] < wide:
                    pieces.append(jnp.zeros((rows, wide - spans[k]), bf16))
            f_ref[place_ref[k]] = jnp.concatenate(pieces, axis=1)

    whole = lambda a: (a.shape, lambda i, *_: (0,) * a.ndim)
    outs = [(rows, 3 * width + PAIR), (rows, 5 * width), (plane, rows, 2 * wide)]
    return call(
        pack_kernel,
        (1,),
        [whole(own), whole(cross), whole(feed), whole(gain_cols)],
        [(o, lambda i, *_, n=len(o): (0,) * n, o, bf16) for o in outs],
        (place, own, cross, feed, gain_cols),
        prefetch=1,
    )


def rows_kernel(a_ref, w, o_ref):
    o_ref[...] = to_low(dot(a_ref[...], whole_weight(w)))


def rows_call(a, w, width):
    rows, model = a.shape
    block = CHUNK if width % CHUNK == 0 else width // 7 if width % 7 == 0 else width
    return call(
        rows_kernel,
        (width // block,),
        [((rows, model), lambda i: (0, 0)), (block, each_block)],
        [((rows, block), lambda i: (0, i), (rows, width), bf16)],
        (a, w),
    )[0]


def turn_call(a, turn):
    rows, model = a.shape
    return call(
        turn_kernel,
        (rows // KEYS,),
        [((KEYS, model), lambda i: (i, 0)), ((model, model), lambda i: (0, 0))],
        [((KEYS, model), lambda i: (i, 0), (rows, model), bf16)],
        (a, turn),
    )[0]


def turn_kernel(a_ref, t_ref, o_ref):
    o_ref[...] = to_low(dot(a_ref[...], t_ref[...]))


def per_device(
    tokens,
    neighbours,
    neighbour_lengths,
    segment_ids,
    out_grad,
    self_weights,
    cross_weights,
    feed_weights,
    norm_gains,
    self_first,
    cross_first,
    feed_first,
    gains_first,
    self_second,
    cross_second,
    feed_second,
    gains_second,
):
    row_count, span, model = tokens.shape
    width = self_weights.shape[2]
    hidden = feed_weights.shape[2]
    shard_rows = self_weights.shape[1]
    pairs = width // PAIR
    blocks = span // BLOCK
    halo = min(-(-(DOC_MAX - 1) // span), lax.axis_size("seq") - 1)
    s_index = lax.axis_index("seq")
    core = lax.axis_index("mp")

    def columns(*parts):
        return jnp.concatenate([to_low(p) for p in parts], axis=1)

    gain_cols = jnp.zeros((shard_rows, PAIR), f32).at[:, :3].set(norm_gains.T)
    small = small_mesh()
    x_own, cot = tokens.reshape(span, model), out_grad.reshape(span, model)
    flat_own = neighbours.reshape(-1, model)
    half, pad = span // 2, KEYS // 2
    seg_here = segment_ids.reshape(1, span) + 1
    lengths = neighbour_lengths.reshape(blocks, NEIGHBOURS)
    ints = jnp.concatenate([seg_here[0], lengths[-1]]).astype(bf16)
    ints = jnp.zeros((8, model), bf16).at[0, : span + NEIGHBOURS].set(ints)
    mine = lax.dynamic_slice_in_dim(x_own, core * half, half, 0)
    edge = lax.dynamic_slice_in_dim(flat_own, flat_own.shape[0] - KEYS + core * pad, pad, 0)
    frequency = rope_base ** (-(jnp.arange(PAIR) % (HEAD_DIM // 2)).astype(f32) / (HEAD_DIM // 2))
    places = (s_index - halo) * span + jnp.arange((halo + 1) * span)
    angles = places.astype(f32)[:, None] * frequency[None, :]

    plane = lax.axis_size("seq")
    groups = hidden // PAIR
    wide = -(-groups // plane) * PAIR
    spans = [(groups + plane - 1 - k) // plane * PAIR for k in range(plane)]
    firsts = [sum(spans[:k]) for k in range(plane)]

    small = small_mesh()
    places_of = [s_index ^ k if small else k for k in range(plane)]
    block_q, block_c, block_f = pack_call(
        jnp.stack([jnp.asarray(p, jnp.int32) for p in places_of]),
        self_weights, cross_weights, feed_weights, gain_cols, firsts, spans, wide,
    )
    near = shifted(jnp.concatenate([mine, edge, ints], axis=0), "seq", 1)
    far = [shifted(jnp.concatenate([mine, ints], axis=0), "seq", k) for k in range(2, halo + 1)]
    if small:
        col_q = exchanged(wide_for_dp(block_q), "dp")
        spots = [s_index ^ k for k in range(plane)]
        cos, sin, turn = jnp.cos(angles), jnp.sin(angles), own_order(model, s_index)
        shares = [block_f[k] for k in range(plane)]
        shares = shares[:1] + [swapped(shares[k], "seq", k) for k in range(1, plane)]
        col_q, near, block_c, cos, sin, turn, *rest = meet(
            col_q, near, block_c, cos, sin, turn, *shares, *far
        )
        shares, far = rest[:plane], rest[plane:]
        xy_q = from_seq(col_q)
    if small:
        col_c = lax.all_gather(block_c, "dp", axis=0, tiled=True)
        cot_turned = turn_call(cot, turn)
    else:
        cos, sin = jnp.cos(angles), jnp.sin(angles)
        turn = jnp.eye(model, dtype=bf16)
        cot_turned = cot
    got = jnp.concatenate([near[: half + pad]] + [f[:half] for f in far], axis=0)
    other = swapped(got, "mp", 1)
    low_half = jnp.where(core == 0, got, other)
    high_half = jnp.where(core == 0, other, got)

    def whole(start, size):
        return [low_half[start : start + size], high_half[start : start + size]]

    pieces = []
    for k in range(halo, 1, -1):
        pieces += whole(half + pad + (k - 2) * half, half)
    x_ext = jnp.concatenate(pieces + whole(0, half) + [x_own], axis=0)
    flat_ext = jnp.concatenate(whole(half, pad) + [flat_own], axis=0)
    ints_prev = [near[half + pad]] + [f[half] for f in far]
    ints_prev = [p[None, : span + NEIGHBOURS].astype(jnp.int32) for p in ints_prev]
    seg_keys = jnp.concatenate([p[:, :span] for p in ints_prev[::-1]] + [seg_here], axis=1)
    seg_keys = seg_keys.reshape(-1, 1)
    lens = jnp.concatenate([ints_prev[0][:, span:], lengths], axis=0)
    before = jnp.concatenate([ints_prev[0][0, span - 1 : span], seg_here[0, : span - 1]])
    heads_of = jnp.repeat(before[::BLOCK], BLOCK)
    spot = jnp.arange(span)
    starts = jnp.where(s_index == 0, BLOCK, 0)
    keep = jnp.logical_or(spot == 0, jnp.logical_and(before == heads_of, spot >= starts))
    keep = keep.astype(f32).reshape(span, 1)

    if small:
        x_ext = turn_call(x_ext, turn)
        col_c, turn, cot_turned, cos, sin, x_ext, flat_ext, cot, *rest = meet(
            col_c, turn, cot_turned, cos, sin, x_ext, flat_ext, cot, *xy_q, *shares
        )
        xy_q, shares = rest[:3], rest[3:]
        w_feed = jnp.broadcast_to(shares[0], (plane, shard_rows, 2 * wide))
        for spot, piece in zip(spots[1:], shares[1:]):
            w_feed = put(w_feed, piece[None], (spot, 0, 0))
        w_feed = w_feed.reshape(plane * shard_rows, 2 * wide)
        lead = 3 * width
        lead_c = from_seq(col_c[:, :lead])
        flat_ext = turn_call(flat_ext, turn)
        q_pieces = [col_q] + xy_q
        s_q, s_k, s_v = (weight(q_pieces, j * width) for j in range(3))
        gain_rows = jnp.concatenate(
            [p[:, 3 * width : 3 * width + PAIR] for p in q_pieces], axis=0
        )
    else:
        full_q, full_c = (
            lax.all_gather(b, ("dp", "seq"), axis=0, tiled=True) for b in (block_q, block_c)
        )
        w_feed = exchanged(block_f.reshape(plane * shard_rows, 2 * wide), "seq")
        w_feed = lax.all_gather(w_feed, "dp", axis=0, tiled=True)
        s_q, s_k, s_v = ([(full_q, j * width)] for j in range(3))
        gain_rows = full_q[:, 3 * width :]
        c_kv, s_o, c_q, c_o = ([(full_c, j * width)] for j in (0, 2, 3, 4))
    gains = gain_rows[:, :3].T.astype(f32)
    x = x_ext[halo * span :]
    n1, q, k, v = qkv_call(x_ext, gains[:1], s_q, s_k, s_v, cos, sin, span, width)
    if small:
        rest_c = col_c[:, lead:]
        q, flat_ext, seg_keys, lens, keep, cot, rest_c, w_feed, *lead_c = meet(
            q, flat_ext, seg_keys, lens, keep, cot, rest_c, w_feed, *lead_c
        )
        w_feed = lax.all_gather(w_feed, "dp", axis=0, tiled=True)
        tail_c = from_seq(rest_c)
        c_kv, s_o = (weight([col_c] + lead_c, j * width) for j in (0, 2))
    def over_plane(own):
        return [own] + [swapped(own, "seq", k) for k in range(1, plane)]

    def with_other(pieces):
        got = jnp.concatenate(pieces, axis=0)
        return jnp.concatenate([got, swapped(got, "mp", 1)], axis=0)

    def back_to_owner(own, other):
        total = own.astype(f32) + swapped(other, "mp", 1).astype(f32)
        sent = to_low(total)
        return [total[:half]] + [
            swapped(sent[k * half : (k + 1) * half], "seq", k) for k in range(1, plane)
        ]

    def f_assembled(got):
        got = got.reshape(plane, shard_rows, 2 * wide)
        return jnp.concatenate(
            [got[k, :, at : at + spans[k]] for at in (0, wide) for k in range(plane)], axis=1
        ).astype(f32)

    attn, lse, part = self_call(q, k, v, seg_here, seg_keys, s_o, model)
    kv2 = rows_call(flat_ext, c_kv, 2 * width)
    if small:
        part, kv2, cot, *tail_c = meet(part, kv2, cot, *tail_c)
        c_q, c_o = (weight([rest_c] + tail_c, j * width) for j in (0, 1))
    cot_rows = over_plane(lax.dynamic_slice_in_dim(cot, core * half, half, 0))
    other = swapped(part, "mp", 1)
    h1, n2, q2, cross, lse2, part2 = cross_call(
        lens, x, part, other, gains[1:2], c_q, c_o, kv2, keep
    )
    if small:
        part2, *cot_rows = meet(part2, *cot_rows)
    cot_rows = with_other(cot_rows)
    other = swapped(part2, "mp", 1)
    h2, n3 = norm_call(core.reshape(1), h1, part2, other, gains[2:3], turn)

    n_rows = with_other(over_plane(n3))
    act, du, y_own, y_other, dn_own, dn_other = feed_call(n_rows, cot_rows, w_feed)
    dn3 = plane_sum(back_to_owner(dn_own, dn_other))
    dn3_other = swapped(dn3, "mp", 1)
    g2, low2, dgain3, dq2, dk2, dv2, dn2 = cross_back_call(
        lens, core.reshape(1), cot_turned, h2, dn3, dn3_other, turn, gains[2:3], c_q, c_o,
        q2, kv2, lse2, keep,
    )
    other = swapped(dn2, "mp", 1)
    def in_model_order(rows):
        high = to_low(lax.reduce_precision(rows, 8, 7))
        rest = to_low(rows - high.astype(f32))
        both = dot_t(jnp.concatenate([high, rest], axis=0), turn)
        return both[:span] + both[span:]

    cross_sent, cross_kept = halves(
        [(n2, dq2), (low2, cross)], [(flat_ext, dk2), (flat_ext, dv2)]
    )
    if small:
        *cross_sent, other, du, act = meet(*cross_sent, other, du, act)
        cross_got = reduce_first(cross_sent)
    g1, low1, dgain2, dq, dk, dv = self_back_call(
        g2, h1, dn2, other, gains[1:2], s_o, q, k, v, lse, seg_here, seg_keys, cos, sin
    )
    if small:
        *cross_got, low1, dq, dk, dv = meet(*cross_got, low1, dq, dk, dv)
        cross_kept, cross_got = reduce_second(cross_kept, cross_got)
    own, dn_mine, dn_given, dgain1 = inner_call(
        core.reshape(1), x_ext, dq, dk, dv, s_q, s_k, s_v
    )
    if small:
        dn_mine, dn_given, dgain1, dq, dk, dv, low1, *cross_got = meet(
            dn_mine, dn_given, dgain1, dq, dk, dv, low1, *cross_got
        )
    dgains = jnp.concatenate([dgain1, 0.5 * dgain2, 0.5 * dgain3], axis=0)
    if small:
        terms, rest = [], jnp.pad(dgains, ((0, 5), (0, 0)))
        for _ in range(3):
            terms.append(to_low(lax.reduce_precision(rest, 8, 7)))
            rest = rest - terms[-1].astype(f32)
        turned = dot_t(jnp.concatenate(terms, axis=0), turn)
        dgains = (turned[:8] + (turned[8:16] + turned[16:]))[:3]
        slots = jnp.pad(
            dgains.reshape(3, -1, shard_rows).transpose(1, 0, 2),
            ((0, 0), (0, 5), (0, PAIR - shard_rows)),
        )
        slots = jnp.repeat(slots, lax.axis_size("mp"), axis=0)
    self_sent, self_kept = halves(
        [(n1[halo * span :], dq), (low1, attn)],
        [(n1, dk), (n1, dv)],
    )
    if small:
        sent_a, sent_b, du, act, *cross_got = meet(*self_sent, du, act, *cross_got)
        self_got = reduce_first((sent_a, sent_b))
        slots = lax.all_to_all(slots, ("dp", "seq", "mp"), 0, 0, tiled=True)
        gains_part = jnp.sum(slots, axis=0)[:3, :shard_rows]
        cross_part = lax.psum_scatter(
            last_sum_call(cross_kept, cross_got)[0], "dp", scatter_dimension=0, tiled=True
        ).astype(f32)
        feed_grads = jnp.concatenate(
            [to_low(t_dot(n_rows, du)), to_low(t_dot(cot_rows, act))], axis=1
        )
        feed_low = lax.psum_scatter(feed_grads, "dp", scatter_dimension=0, tiled=True)
        *self_got, gains_part = meet(*self_got, gains_part)
        self_kept, self_got = reduce_second(self_kept, self_got)
        *self_got, h2_model = meet(*self_got, in_model_order(h2))
        self_col, mark = last_sum_call(self_kept, self_got)
        dn_mine, dn_given, y_own, y_other, mark = meet(dn_mine, dn_given, y_own, y_other, mark)
        self_got = exchanged(self_col, "dp")
    y_sums = back_to_owner(y_own, y_other)
    summed = to_low(dn_mine + swapped(dn_given, "mp", 1))
    if small:
        summed = to_low(dot_t(summed, turn))
    summed = summed.reshape(halo, half, model)
    back_parts = [shifted(summed[halo - k], "seq", -k) for k in range(1, halo + 1)]
    if small:
        squares = jnp.sum(cross_part * cross_part) + jnp.sum(jnp.square(feed_low.astype(f32)))
        self_got, squares = meet(self_got, squares)
        self_part, self_squares = total_call(self_got, mark)
    else:
        feed_grads = jnp.concatenate(
            [to_low(t_dot(n_rows, du)), to_low(t_dot(cot_rows, act))], axis=1
        )
        feed_low = lax.psum_scatter(feed_grads, "dp", scatter_dimension=0, tiled=True)
        feed_part = f_assembled(exchanged(feed_low, "seq"))
        cross_part, self_part = reduce_plain(cross_kept), reduce_plain(self_kept)
        squares = jnp.sum(feed_part * feed_part) + jnp.sum(cross_part * cross_part)
        self_squares = jnp.sum(jnp.square(self_part)).reshape(1, 1)
    if not small:
        gain_sums = butterfly(dgains, ("mp", "seq", "dp"))
        shard = lax.axis_index("dp") * lax.axis_size("seq") + s_index
        gains_part = lax.dynamic_slice_in_dim(gain_sums, shard * shard_rows, shard_rows, axis=1)
    first_model = (core == 0).astype(f32)
    local_squares = (
        self_squares
        + squares
        + first_model * jnp.sum(gains_part * gains_part)
    )
    if small:
        shares = [take(feed_low.reshape(plane, shard_rows, 2 * wide), spot, 0) for spot in spots]
        local_squares, *rest = meet(local_squares, *y_sums, *back_parts, *shares)
        y_sums, back_parts, shares = rest[:plane], rest[plane:-plane], rest[-plane:]
        shares = shares[:1] + [swapped(shares[k], "seq", k) for k in range(1, plane)]
        feed_got = jnp.zeros((plane, shard_rows, 2 * wide), bf16)
        for spot, piece in zip(spots, shares):
            feed_got = put(feed_got, piece[None], (spot, 0, 0))
        feed_part = f_assembled(feed_got)
    grad_norm = jnp.sqrt(sum_everywhere(local_squares).reshape(()))
    factor = jnp.minimum(1.0, clip_limit / (grad_norm + 1e-06))
    scalar = factor.reshape(1)
    mixed_order, plain = (0, 2, 3, 1), (0, 1)
    y_half = plane_sum(y_sums)
    y_other = swapped(y_half, "mp", 1)
    y_all = jnp.concatenate(
        [jnp.where(core == 0, y_half, y_other), jnp.where(core == 0, y_other, y_half)], axis=0
    )
    if halo:
        back = sum(p.astype(f32) for p in back_parts)
        if small:
            back = dot(to_low(back), turn)
        own = own + put(jnp.zeros_like(own), back, (core * half, 0))
    back, _ = rms_back(x.astype(f32), gains[:1], core_sum(own))
    in_grad = g1 + back

    if small:
        in_grad = in_model_order(in_grad)
        result = to_low(h2_model + y_all)
    else:
        result = to_low(h2 + y_all)
    in_grad = in_grad.reshape(row_count, span, model)
    out = result.reshape(row_count, span, model)
    (
        self_new, self_first_new, self_second_new,
        cross_new, cross_first_new, cross_second_new,
        feed_new, feed_first_new, feed_second_new,
    ) = adam_call(
        scalar,
        [
            (self_weights, self_part, self_first, self_second, mixed_order),
            (cross_weights, cross_part, cross_first, cross_second, mixed_order),
            (feed_weights, feed_part, feed_first, feed_second, plain),
        ],
    )
    gains_new, gains_first_new, gains_second_new = adam_step(
        norm_gains, gains_part, gains_first, gains_second, factor, gain_rate, 0.0
    )
    return (
        out,
        in_grad,
        grad_norm,
        self_new,
        cross_new,
        feed_new,
        gains_new,
        self_first_new,
        cross_first_new,
        feed_first_new,
        gains_first_new,
        self_second_new,
        cross_second_new,
        feed_second_new,
        gains_second_new,
    )


def solution(mesh):
    tok = P("dp", "seq", None)
    mat = P(None, ("dp", "seq"), "mp")
    vec = P(None, ("dp", "seq"))
    in_specs = (
        tok,
        P("dp", "seq", None, None, None),
        tok,
        P("dp", "seq"),
        tok,
    ) + (mat, mat, mat, vec) * 3
    out_specs = (tok, tok, P()) + (mat, mat, mat, vec) * 3
    return jax.shard_map(
        per_device, mesh=mesh, in_specs=in_specs, out_specs=out_specs, check_vma=False
    )
```
